256 devices in a mesh: span: 4 (over y), ty: 8 (over z_hi, core), tx: 8 (over z_lo, x).
Axes of the slice: x: 4, y: 4, z: 8 (z_hi: 4, z_lo: 2; z = z_hi * 2 + z_lo), core: 2. Of those that a mesh axis runs over, the one named last changes fastest.
Arguments:
- queries: bfloat16 [4, 8, 8, 128, 1536], P('span', 'ty', 'tx'), may hold values from -125 to 125
- key_value: bfloat16 [4, 8, 8, 128, 1024], P('span', 'ty', 'tx'), may hold values from -5 to 5
- pattern: int32 [4, 8, 8, 5], P('span', 'ty', 'tx'), may hold values from 0 to 1
- counts: int32 [4, 8, 8], replicated, may hold values from 64 to 128, as said below
- span_mask: int32 [4, 4], replicated, may hold values from 0 to 1, as said below
Outputs:
- attended: bfloat16 [4, 8, 8, 128, 1536], P('span', 'ty', 'tx')
The draws below stay inside these ranges and needn't reach their ends.
Inputs may be any that keep to these rules, and one draw needn't show every extreme that they name: `counts`: in every span some tile has all 128 slots valid. span_mask[c, c] is 1 and span_mask[c, c'] is 0 for c' > c.
All inputs are finite; a program needn't handle non-finite values.
Results may differ from the reference program's by a relative error of at most 0.006.
Values may be sent and summed in bfloat16 or wider, within the bound.
A program may use at most 64 MiB of HBM per device.

```python
import math
import jax
import jax.numpy as jnp
from jax import lax

HEAD_SIZE = 128
KEY_VALUE_HEADS = 4
QUERY_PER_KV = 3
NEIGH = 5
TOKEN_SLOTS = 128
SPAN_COUNT = 4
TILE_ROWS = 8
TILE_COLUMNS = 8


def base_keys(key):
    key_sampler = jax.random.normal(jax.random.fold_in(key, 101), (SPAN_COUNT, TILE_ROWS, TILE_COLUMNS, TOKEN_SLOTS, KEY_VALUE_HEADS, HEAD_SIZE), jnp.float32)
    return jnp.clip(key_sampler, -5.0, 5.0)


def draw_key_value(key, part):
    key_sampler = base_keys(key)
    complete_shape = (SPAN_COUNT, TILE_ROWS, TILE_COLUMNS, TOKEN_SLOTS, KEY_VALUE_HEADS, HEAD_SIZE)
    value_matrix = jnp.clip(jax.random.normal(jax.random.fold_in(key, 102), complete_shape, jnp.float32), -5.0, 5.0)
    packed_rows = jnp.concatenate([key_sampler.reshape(SPAN_COUNT, TILE_ROWS, TILE_COLUMNS, TOKEN_SLOTS, KEY_VALUE_HEADS * HEAD_SIZE), value_matrix.reshape(SPAN_COUNT, TILE_ROWS, TILE_COLUMNS, TOKEN_SLOTS, KEY_VALUE_HEADS * HEAD_SIZE)], axis=-1)
    return packed_rows.astype(jnp.bfloat16)


def draw_queries(key, part):
    complete_shape = (SPAN_COUNT, TILE_ROWS, TILE_COLUMNS, TOKEN_SLOTS, KEY_VALUE_HEADS, QUERY_PER_KV, HEAD_SIZE)
    sampled_blocks = jnp.clip(jax.random.normal(jax.random.fold_in(key, 103), complete_shape, jnp.float32), -5.0, 5.0)
    return sampled_blocks.reshape(SPAN_COUNT, TILE_ROWS, TILE_COLUMNS, TOKEN_SLOTS, KEY_VALUE_HEADS * QUERY_PER_KV * HEAD_SIZE).astype(jnp.bfloat16)


def draw_pattern(key, part):
    opened = (jax.random.randint(jax.random.fold_in(key, 104), (SPAN_COUNT, TILE_ROWS, TILE_COLUMNS, NEIGH), 0, 4) > 0).astype(jnp.int32)
    return opened.at[..., 0].set(1)


def draw_counts(key, part):
    filled = jax.random.randint(jax.random.fold_in(key, 105), (SPAN_COUNT, TILE_ROWS * TILE_COLUMNS), TOKEN_SLOTS // 2, TOKEN_SLOTS + 1)
    fullest = jax.random.randint(jax.random.fold_in(key, 106), (SPAN_COUNT,), 0, TILE_ROWS * TILE_COLUMNS)
    filled = filled.at[jnp.arange(SPAN_COUNT), fullest].set(TOKEN_SLOTS)
    return filled.reshape(SPAN_COUNT, TILE_ROWS, TILE_COLUMNS).astype(jnp.int32)


def draw_span_mask(key, part):
    bits_drawn = (jax.random.randint(jax.random.fold_in(key, 107), (SPAN_COUNT, SPAN_COUNT), 0, 4) > 0).astype(jnp.int32)
    row_ids = jnp.arange(SPAN_COUNT)[:, None]
    col_ids = jnp.arange(SPAN_COUNT)[None, :]
    return jnp.where(row_ids > col_ids, bits_drawn, jnp.where(row_ids == col_ids, 1, 0)).astype(jnp.int32)


def setup_inputs(seed: int = 0) -> dict:
    keys = jax.random.split(jax.random.key(seed), 6)
    return {
        "queries": draw_queries(jax.random.fold_in(keys[5], 71), 0),
        "key_value": draw_key_value(jax.random.fold_in(keys[5], 71), 0),
        "pattern": draw_pattern(jax.random.fold_in(keys[5], 71), 0),
        "counts": draw_counts(jax.random.fold_in(keys[5], 71), 0),
        "span_mask": draw_span_mask(jax.random.fold_in(keys[5], 71), 0),
    }


OFFSETS = ((0, 0), (-1, 0), (1, 0), (0, -1), (0, 1))

def as_index(value):
    return jnp.asarray(value).astype(jnp.int32)

def reference(queries, key_value, pattern, counts, span_mask):
    window_radius = KEY_VALUE_HEADS * HEAD_SIZE
    scale = 1.0 / math.sqrt(HEAD_SIZE)
    ext_kv = jnp.pad(key_value, ((0, 0), (1, 1), (1, 1), (0, 0), (0, 0)))
    ext_counts = jnp.pad(counts, ((0, 0), (1, 1), (1, 1)))
    flat_query = queries.reshape(SPAN_COUNT * TILE_ROWS * TILE_COLUMNS, TOKEN_SLOTS, KEY_VALUE_HEADS, QUERY_PER_KV, HEAD_SIZE)
    flat_pattern = pattern.reshape(SPAN_COUNT * TILE_ROWS * TILE_COLUMNS, NEIGH)
    row_ids = jnp.arange(TOKEN_SLOTS, dtype=jnp.int32)
    zero_index = as_index(0)

    def one_tile(tile_index):
        span_id = as_index(tile_index // (TILE_ROWS * TILE_COLUMNS))
        tile_y = as_index(tile_index // TILE_COLUMNS % TILE_ROWS)
        tile_x = as_index(tile_index % TILE_COLUMNS)
        kv_pieces = []
        alive_list = []
        for shift_y, shift_x in OFFSETS:
            start_y = as_index(tile_y + (1 + shift_y))
            start_x = as_index(tile_x + (1 + shift_x))
            piece_kv = lax.dynamic_slice(ext_kv, (zero_index, start_y, start_x, zero_index, zero_index), (SPAN_COUNT, 1, 1, TOKEN_SLOTS, 2 * window_radius))
            kv_pieces.append(piece_kv.reshape(SPAN_COUNT, TOKEN_SLOTS, 2 * window_radius))
            piece_count = lax.dynamic_slice(ext_counts, (zero_index, start_y, start_x), (SPAN_COUNT, 1, 1)).reshape(SPAN_COUNT)
            alive_list.append(row_ids[None, :] < piece_count[:, None])
        key_value_block = jnp.stack(kv_pieces, axis=1)
        alive_keys = jnp.stack(alive_list, axis=1)
        opened = lax.dynamic_index_in_dim(flat_pattern, tile_index, 0, keepdims=False) > 0
        causal = lax.dynamic_index_in_dim(span_mask, span_id, 0, keepdims=False) > 0
        alive_keys = (alive_keys & opened[None, :, None] & causal[:, None, None]).reshape(-1)
        key_matrix = key_value_block[..., :window_radius].reshape(-1, KEY_VALUE_HEADS, HEAD_SIZE).astype(jnp.float32)
        value_matrix = key_value_block[..., window_radius:].reshape(-1, KEY_VALUE_HEADS, HEAD_SIZE).astype(jnp.float32)
        query_rows = lax.dynamic_index_in_dim(flat_query, tile_index, 0, keepdims=False).astype(jnp.float32)
        scores = jnp.einsum('tkgd,lkd->tkgl', query_rows, key_matrix) * scale
        scores = jnp.where(alive_keys, scores, -1e+30)
        row_max = lax.optimization_barrier(jnp.max(scores, axis=-1, keepdims=True))
        weights = jnp.where(alive_keys, jnp.exp(scores - row_max), 0.0)
        denom_sum = lax.optimization_barrier(jnp.sum(weights, axis=-1))
        rounded = lax.optimization_barrier(weights.astype(jnp.bfloat16)).astype(jnp.float32)
        attended = jnp.einsum('tkgl,lkd->tkgd', rounded, value_matrix) / denom_sum[..., None]
        own_count = ext_counts[span_id, tile_y + 1, tile_x + 1]
        attended = jnp.where(row_ids[:, None, None, None] < own_count, attended, 0.0)
        return attended.reshape(TOKEN_SLOTS, KEY_VALUE_HEADS * QUERY_PER_KV * HEAD_SIZE).astype(jnp.bfloat16)
    final_output = lax.map(one_tile, jnp.arange(SPAN_COUNT * TILE_ROWS * TILE_COLUMNS, dtype=jnp.int32))
    return final_output.reshape(SPAN_COUNT, TILE_ROWS, TILE_COLUMNS, TOKEN_SLOTS, KEY_VALUE_HEADS * QUERY_PER_KV * HEAD_SIZE)
```

```python
import jax
import jax.numpy as jnp
from jax import lax
from jax.experimental import pallas as pl
from jax.experimental.pallas import tpu as pltpu
from jax.sharding import PartitionSpec as P

HEAD_SIZE = 128
NEIGH = 5


def padded(block, sides, width):
    for axis, dim in sides:
        count = lax.axis_size(axis)
        forward = [(i, i + 1) for i in range(count - 1)]
        backward = [(target, source) for source, target in forward]
        low = lax.ppermute(
            lax.slice_in_dim(block, block.shape[dim] - width, None, axis=dim), axis, forward
        )
        high = lax.ppermute(lax.slice_in_dim(block, 0, width, axis=dim), axis, backward)
        block = jnp.concatenate([low, block, high], axis=dim)
    return block


def cross_tiles(extended):
    return jnp.stack(
        [
            extended[:, 1, 1],
            extended[:, 0, 1],
            extended[:, 2, 1],
            extended[:, 1, 0],
            extended[:, 1, 2],
        ],
        axis=1,
    )


def attend_kernel(q_ref, kv_ref, live_ref, rowok_ref, o_ref):
    kv_heads = kv_ref.shape[1] // (2 * HEAD_SIZE)
    groups = q_ref.shape[1] // (kv_heads * HEAD_SIZE)
    tok = q_ref.shape[0]
    width = kv_heads * HEAD_SIZE
    scale = HEAD_SIZE ** (-0.5)
    live = live_ref[...] > 0
    rowok = jnp.concatenate([rowok_ref[...]] * groups, axis=0) > 0
    for h in range(kv_heads):
        qh = jnp.concatenate(
            [q_ref[:, (h * groups + g) * HEAD_SIZE:(h * groups + g + 1) * HEAD_SIZE] for g in range(groups)],
            axis=0,
        )
        kh = kv_ref[:, h * HEAD_SIZE:(h + 1) * HEAD_SIZE]
        s = lax.dot_general(qh, kh, (((1,), (1,)), ((), ())), preferred_element_type=jnp.float32)
        s = s * scale
        s = jnp.where(live, s, -1e30)
        m = jnp.max(s, axis=1, keepdims=True)
        p = jnp.where(live, jnp.exp(s - m), 0.0)
        tot = jnp.sum(p, axis=1, keepdims=True)
        vh = kv_ref[:, width + h * HEAD_SIZE:width + (h + 1) * HEAD_SIZE]
        acc = jnp.dot(p.astype(jnp.bfloat16), vh, preferred_element_type=jnp.float32)
        res = jnp.where(rowok, acc / tot, 0.0).astype(o_ref.dtype)
        for g in range(groups):
            col = (h * groups + g) * HEAD_SIZE
            o_ref[:, col:col + HEAD_SIZE] = res[g * tok:(g + 1) * tok]


def attend(q, kv, live, rowok):
    tok, qw = q.shape
    keys, kw = kv.shape
    flops = 2 * 2 * tok * qw * keys
    return pl.pallas_call(
        attend_kernel,
        out_shape=jax.ShapeDtypeStruct((tok, qw), q.dtype),
        in_specs=[pl.BlockSpec(memory_space=pltpu.VMEM)] * 4,
        out_specs=pl.BlockSpec(memory_space=pltpu.VMEM),
        compiler_params=pltpu.CompilerParams(vmem_limit_bytes=48 * 1024 * 1024),
        cost_estimate=pl.CostEstimate(
            flops=flops, transcendentals=tok * qw // HEAD_SIZE * keys,
            bytes_accessed=2 * (2 * tok * qw + keys * kw)),
    )(q, kv, live, rowok)


def shards(queries, key_value, pattern, counts, span_mask):
    tok_rows = queries.shape[3]
    spans = counts.shape[0]
    my_span = lax.axis_index("span")
    my_row = lax.axis_index("ty")
    my_col = lax.axis_index("tx")
    zero_index = jnp.asarray(0).astype(jnp.int32)
    padded_counts = jnp.pad(counts, ((0, 0), (1, 1), (1, 1)))
    window = lax.dynamic_slice(padded_counts, (zero_index, my_row, my_col), (spans, 3, 3))
    near_counts = cross_tiles(window)
    own_count = lax.dynamic_index_in_dim(window[:, 1, 1], my_span, 0, keepdims=False)
    allowed = pattern.reshape(NEIGH) > 0
    span_row = lax.dynamic_index_in_dim(span_mask, my_span, 0, keepdims=False) > 0
    row_ids = jnp.arange(tok_rows, dtype=jnp.int32)
    cached = lax.all_gather(key_value, "span", axis=0, tiled=True)
    extended = padded(cached, (("ty", 1), ("tx", 2)), 1)
    kv_piece = cross_tiles(extended)
    kv_flat = kv_piece.reshape(spans * NEIGH * tok_rows, -1)
    live = (
        (row_ids[None, None, :] < near_counts[:, :, None])
        & allowed[None, :, None]
        & span_row[:, None, None]
    ).reshape(1, -1).astype(jnp.float32)
    rowok = (row_ids < own_count).astype(jnp.float32).reshape(tok_rows, 1)
    out = attend(queries.reshape(tok_rows, -1), kv_flat, live, rowok)
    return out.reshape(1, 1, 1, tok_rows, -1)


def solution(mesh):
    return jax.shard_map(
        shards,
        mesh=mesh,
        in_specs=(
            P("span", "ty", "tx", None, None),
            P("span", "ty", "tx", None, None),
            P("span", "ty", "tx", None),
            P(),
            P(),
        ),
        out_specs=P("span", "ty", "tx", None, None),
        check_vma=False,
    )
```

```python
import jax
import jax.numpy as jnp
from jax import lax
from jax.experimental import pallas as pl
from jax.experimental.pallas import tpu as pltpu
from jax.sharding import PartitionSpec as P

HEAD_SIZE = 128
NEIGH = 5
OFFSETS = ((0, 0), (-1, 0), (1, 0), (0, -1), (0, 1))
INVERSE = (0, 2, 1, 4, 3)


def cross_tiles(extended):
    return jnp.stack(
        [
            extended[:, 1, 1],
            extended[:, 0, 1],
            extended[:, 2, 1],
            extended[:, 1, 0],
            extended[:, 1, 2],
        ],
        axis=1,
    )


def attend_body(q_ref, kv_ref, live_ref, rowok_ref, o_ref):
    kv_heads = kv_ref.shape[1] // (2 * HEAD_SIZE)
    groups = q_ref.shape[1] // (kv_heads * HEAD_SIZE)
    tok = q_ref.shape[0]
    width = kv_heads * HEAD_SIZE
    scale = HEAD_SIZE ** (-0.5)
    live = live_ref[...] > 0
    rowok = jnp.concatenate([rowok_ref[...]] * groups, axis=0) > 0
    for h in range(kv_heads):
        qh = jnp.concatenate(
            [q_ref[:, (h * groups + g) * HEAD_SIZE:(h * groups + g + 1) * HEAD_SIZE] for g in range(groups)],
            axis=0,
        )
        kh = kv_ref[:, h * HEAD_SIZE:(h + 1) * HEAD_SIZE]
        s = lax.dot_general(qh, kh, (((1,), (1,)), ((), ())), preferred_element_type=jnp.float32)
        s = s * scale
        s = jnp.where(live, s, -1e30)
        m = jnp.max(s, axis=1, keepdims=True)
        p = jnp.where(live, jnp.exp(s - m), 0.0)
        tot = jnp.sum(p, axis=1, keepdims=True)
        vh = kv_ref[:, width + h * HEAD_SIZE:width + (h + 1) * HEAD_SIZE]
        acc = jnp.dot(p.astype(jnp.bfloat16), vh, preferred_element_type=jnp.float32)
        res = jnp.where(rowok, acc / tot, 0.0).astype(o_ref.dtype)
        for g in range(groups):
            col = (h * groups + g) * HEAD_SIZE
            o_ref[:, col:col + HEAD_SIZE] = res[g * tok:(g + 1) * tok]


def window_kernel(spans, rows, cols, q_ref, kv_ref, live_ref, rowok_ref, o_ref,
                  kvbuf, send_sem, recv_sem, local_sem):
    tok = kv_ref.shape[0]
    c = lax.axis_index("span")
    i = lax.axis_index("ty")
    j = lax.axis_index("tx")

    def inside(d):
        dy, dx = OFFSETS[d]
        y, x = i + dy, j + dx
        return (y >= 0) & (y < rows) & (x >= 0) & (x < cols)

    def slot(s, o):
        return kvbuf.at[pl.ds((s * NEIGH + o) * tok, tok), :]

    n_nb = sum(inside(d).astype(jnp.int32) for d in range(1, NEIGH))

    barrier = pltpu.get_barrier_semaphore()
    for s in range(spans):
        @pl.when(s != c)
        def _():
            pl.semaphore_signal(barrier, 1, device_id=(s, i, j), device_id_type=pl.DeviceIdType.MESH)
    for d in range(1, NEIGH):
        dy, dx = OFFSETS[d]
        @pl.when(inside(d))
        def _():
            pl.semaphore_signal(barrier, 1, device_id=(c, i + dy, j + dx), device_id_type=pl.DeviceIdType.MESH)
    pl.semaphore_wait(barrier, spans - 1 + n_nb)

    def up_copy(s):
        return pltpu.make_async_remote_copy(
            src_ref=kv_ref, dst_ref=slot(c, 0), send_sem=send_sem.at[s], recv_sem=recv_sem.at[c * NEIGH],
            device_id=(s, i, j), device_id_type=pl.DeviceIdType.MESH)

    def side_copy(s, d, src):
        dy, dx = OFFSETS[d]
        return pltpu.make_async_remote_copy(
            src_ref=src, dst_ref=slot(s, INVERSE[d]),
            send_sem=send_sem.at[spans + s * (NEIGH - 1) + d - 1],
            recv_sem=recv_sem.at[s * NEIGH + INVERSE[d]],
            device_id=(c, i + dy, j + dx), device_id_type=pl.DeviceIdType.MESH)

    for s in range(spans):
        @pl.when(s > c)
        def _():
            up_copy(s).start()

    for s in range(spans):
        @pl.when(s == c)
        def _():
            for d in range(1, NEIGH):
                @pl.when(inside(d))
                def _():
                    side_copy(s, d, kv_ref).start()

    own = pltpu.make_async_copy(kv_ref, slot(0, 0), local_sem.at[0])
    for s in range(spans):
        @pl.when(s == c)
        def _():
            pltpu.make_async_copy(kv_ref, slot(s, 0), local_sem.at[0]).start()

    zeros = jnp.zeros((tok, kv_ref.shape[1]), kv_ref.dtype)
    for s in range(spans):
        @pl.when(s > c)
        def _():
            for o in range(NEIGH):
                slot(s, o)[...] = zeros
        @pl.when(s <= c)
        def _():
            for d in range(1, NEIGH):
                @pl.when(jnp.logical_not(inside(INVERSE[d])))
                def _():
                    slot(s, INVERSE[d])[...] = zeros

    for s in range(spans):
        @pl.when(s < c)
        def _():
            pltpu.make_async_remote_copy(
                src_ref=kv_ref, dst_ref=slot(s, 0), send_sem=send_sem.at[s], recv_sem=recv_sem.at[s * NEIGH],
                device_id=(s, i, j), device_id_type=pl.DeviceIdType.MESH).wait_recv()
            for d in range(1, NEIGH):
                @pl.when(inside(d))
                def _():
                    side_copy(s, d, slot(s, 0)).start()

    for s in range(spans):
        @pl.when(s <= c)
        def _():
            for o in range(1, NEIGH):
                dy, dx = OFFSETS[o]
                @pl.when(inside(o))
                def _():
                    pltpu.make_async_remote_copy(
                        src_ref=kv_ref, dst_ref=slot(s, o), send_sem=send_sem.at[0],
                        recv_sem=recv_sem.at[s * NEIGH + o],
                        device_id=(c, i + dy, j + dx), device_id_type=pl.DeviceIdType.MESH).wait_recv()

    for s in range(spans):
        @pl.when(s > c)
        def _():
            up_copy(s).wait_send()
        @pl.when(s <= c)
        def _():
            for d in range(1, NEIGH):
                @pl.when(inside(d))
                def _():
                    side_copy(s, d, kv_ref).wait_send()
    own.wait()

    attend_body(q_ref, kvbuf, live_ref, rowok_ref, o_ref)


def window_attend(q, kv, live, rowok, spans, rows, cols):
    tok, qw = q.shape
    kw = kv.shape[1]
    keys = spans * NEIGH * tok
    flops = 2 * 2 * tok * qw * keys
    kernel = lambda *refs: window_kernel(spans, rows, cols, *refs)
    return pl.pallas_call(
        kernel,
        out_shape=jax.ShapeDtypeStruct((tok, qw), q.dtype),
        in_specs=[pl.BlockSpec(memory_space=pltpu.VMEM)] * 4,
        out_specs=pl.BlockSpec(memory_space=pltpu.VMEM),
        scratch_shapes=[
            pltpu.VMEM((keys, kw), kv.dtype),
            pltpu.SemaphoreType.DMA((spans + spans * (NEIGH - 1),)),
            pltpu.SemaphoreType.DMA((spans * NEIGH,)),
            pltpu.SemaphoreType.DMA((1,)),
        ],
        compiler_params=pltpu.CompilerParams(
            vmem_limit_bytes=48 * 1024 * 1024, collective_id=0, has_side_effects=True),
        cost_estimate=pl.CostEstimate(
            flops=flops, transcendentals=tok * qw // HEAD_SIZE * keys,
            bytes_accessed=2 * (2 * tok * qw + keys * kw)),
    )(q, kv, live, rowok)


def shards(queries, key_value, pattern, counts, span_mask):
    tok_rows = queries.shape[3]
    spans, rows, cols = counts.shape
    my_span = lax.axis_index("span")
    my_row = lax.axis_index("ty")
    my_col = lax.axis_index("tx")
    zero_index = jnp.asarray(0).astype(jnp.int32)
    padded_counts = jnp.pad(counts, ((0, 0), (1, 1), (1, 1)))
    window = lax.dynamic_slice(padded_counts, (zero_index, my_row, my_col), (spans, 3, 3))
    near_counts = cross_tiles(window)
    own_count = lax.dynamic_index_in_dim(window[:, 1, 1], my_span, 0, keepdims=False)
    allowed = pattern.reshape(NEIGH) > 0
    span_row = lax.dynamic_index_in_dim(span_mask, my_span, 0, keepdims=False) > 0
    row_ids = jnp.arange(tok_rows, dtype=jnp.int32)
    live = (
        (row_ids[None, None, :] < near_counts[:, :, None])
        & allowed[None, :, None]
        & span_row[:, None, None]
    ).reshape(1, -1).astype(jnp.float32)
    rowok = (row_ids < own_count).astype(jnp.float32).reshape(tok_rows, 1)
    out = window_attend(
        queries.reshape(tok_rows, -1), key_value.reshape(tok_rows, -1), live, rowok, spans, rows, cols)
    return out.reshape(1, 1, 1, tok_rows, -1)


def solution(mesh):
    return jax.shard_map(
        shards,
        mesh=mesh,
        in_specs=(
            P("span", "ty", "tx", None, None),
            P("span", "ty", "tx", None, None),
            P("span", "ty", "tx", None),
            P(),
            P(),
        ),
        out_specs=P("span", "ty", "tx", None, None),
        check_vma=False,
    )
```

```python
import jax
import jax.numpy as jnp
from jax import lax
from jax.experimental import pallas as pl
from jax.experimental.pallas import tpu as pltpu
from jax.sharding import PartitionSpec as P

HEAD_SIZE = 128
NEIGH = 5
OFFSETS = ((0, 0), (-1, 0), (1, 0), (0, -1), (0, 1))
INVERSE = (0, 2, 1, 4, 3)


def cross_tiles(extended):
    return jnp.stack(
        [
            extended[:, 1, 1],
            extended[:, 0, 1],
            extended[:, 2, 1],
            extended[:, 1, 0],
            extended[:, 1, 2],
        ],
        axis=1,
    )


def attend_body(q_ref, kv_ref, live_ref, rowok_ref, o_ref):
    kv_heads = kv_ref.shape[1] // (2 * HEAD_SIZE)
    groups = q_ref.shape[1] // (kv_heads * HEAD_SIZE)
    tok = q_ref.shape[0]
    width = kv_heads * HEAD_SIZE
    scale = HEAD_SIZE ** (-0.5)
    live = live_ref[...] > 0
    rowok = jnp.concatenate([rowok_ref[...]] * groups, axis=0) > 0
    for h in range(kv_heads):
        qh = jnp.concatenate(
            [q_ref[:, (h * groups + g) * HEAD_SIZE:(h * groups + g + 1) * HEAD_SIZE] for g in range(groups)],
            axis=0,
        )
        kh = kv_ref[:, h * HEAD_SIZE:(h + 1) * HEAD_SIZE]
        s = lax.dot_general(qh, kh, (((1,), (1,)), ((), ())), preferred_element_type=jnp.float32)
        s = s * scale
        s = jnp.where(live, s, -1e30)
        m = jnp.max(s, axis=1, keepdims=True)
        p = jnp.where(live, jnp.exp(s - m), 0.0)
        tot = jnp.sum(p, axis=1, keepdims=True)
        vh = kv_ref[:, width + h * HEAD_SIZE:width + (h + 1) * HEAD_SIZE]
        acc = jnp.dot(p.astype(jnp.bfloat16), vh, preferred_element_type=jnp.float32)
        res = jnp.where(rowok, acc / tot, 0.0).astype(o_ref.dtype)
        for g in range(groups):
            col = (h * groups + g) * HEAD_SIZE
            o_ref[:, col:col + HEAD_SIZE] = res[g * tok:(g + 1) * tok]


def window_kernel(spans, rows, cols, q_ref, kv_ref, live_ref, rowok_ref, o_ref,
                  kvbuf, trans, send_sem, recv_sem, fwd_sem, trans_sem, local_sem):
    tok = kv_ref.shape[0]
    c = lax.axis_index("span")
    i = lax.axis_index("ty")
    j = lax.axis_index("tx")
    mesh_id = pl.DeviceIdType.MESH
    relayed = cols >= 4
    half = cols // 2
    is_a = j == half - 1
    is_b = j == half

    def relay_col(s):
        return 0 if s % 2 == 0 else cols - 1

    def inside(d):
        dy, dx = OFFSETS[d]
        y, x = i + dy, j + dx
        return (y >= 0) & (y < rows) & (x >= 0) & (x < cols)

    def slot(s, o):
        return kvbuf.at[pl.ds((s * NEIGH + o) * tok, tok), :]

    def boundary(d):
        if not relayed or d not in (3, 4):
            return None
        return is_a if d == 4 else is_b

    n_nb = sum(inside(d).astype(jnp.int32) for d in range(1, NEIGH))
    ends = (is_a | is_b | (j == 0) | (j == cols - 1)) if relayed else (j < 0)
    n_extra = jnp.where(ends, 2, 0)

    barrier = pltpu.get_barrier_semaphore()
    def greet(target):
        pl.semaphore_signal(barrier, 1, device_id=target, device_id_type=mesh_id)
    for s in range(spans):
        @pl.when(s != c)
        def _():
            greet((s, i, j))
    for d in range(1, NEIGH):
        dy, dx = OFFSETS[d]
        @pl.when(inside(d))
        def _():
            greet((c, i + dy, j + dx))
    if relayed:
        @pl.when(is_a | is_b)
        def _():
            greet((c, i, 0))
            greet((c, i, cols - 1))
        @pl.when((j == 0) | (j == cols - 1))
        def _():
            greet((c, i, half - 1))
            greet((c, i, half))
    pl.semaphore_wait(barrier, spans - 1 + n_nb + n_extra)

    def up_copy(s):
        return pltpu.make_async_remote_copy(
            src_ref=kv_ref, dst_ref=slot(c, 0), send_sem=send_sem.at[s], recv_sem=recv_sem.at[c * NEIGH],
            device_id=(s, i, j), device_id_type=mesh_id)

    def side_copy(s, d, src):
        dy, dx = OFFSETS[d]
        return pltpu.make_async_remote_copy(
            src_ref=src, dst_ref=slot(s, INVERSE[d]),
            send_sem=send_sem.at[spans + s * (NEIGH - 1) + d - 1],
            recv_sem=recv_sem.at[s * NEIGH + INVERSE[d]],
            device_id=(c, i + dy, j + dx), device_id_type=mesh_id)

    def to_relay(s, d, src):
        way = 0 if d == 4 else 1
        return pltpu.make_async_remote_copy(
            src_ref=src, dst_ref=trans.at[way, s],
            send_sem=send_sem.at[spans + s * (NEIGH - 1) + d - 1],
            recv_sem=trans_sem.at[way, s],
            device_id=(c, i, relay_col(s)), device_id_type=mesh_id)

    def from_relay(s, way):
        target = half if way == 0 else half - 1
        o = 3 if way == 0 else 4
        return pltpu.make_async_remote_copy(
            src_ref=trans.at[way, s], dst_ref=slot(s, o),
            send_sem=fwd_sem.at[way, s], recv_sem=recv_sem.at[s * NEIGH + o],
            device_id=(c, i, target), device_id_type=mesh_id)

    def send_side(s, d, src, wait=False):
        bnd = boundary(d)
        direct = inside(d) if bnd is None else inside(d) & jnp.logical_not(bnd)
        @pl.when(direct)
        def _():
            cp = side_copy(s, d, src)
            cp.wait_send() if wait else cp.start()
        if bnd is not None:
            @pl.when(bnd)
            def _():
                cp = to_relay(s, d, src)
                cp.wait_send() if wait else cp.start()

    def relay(s, wait=False):
        if not relayed:
            return
        @pl.when(j == relay_col(s))
        def _():
            for way in (0, 1):
                if wait:
                    from_relay(s, way).wait_send()
                else:
                    to_relay(s, 4 if way == 0 else 3, kv_ref).wait_recv()
                    from_relay(s, way).start()

    for s in range(spans):
        @pl.when(s > c)
        def _():
            up_copy(s).start()

    for s in range(spans):
        @pl.when(s == c)
        def _():
            for d in range(1, NEIGH):
                send_side(s, d, kv_ref)

    own = pltpu.make_async_copy(kv_ref, slot(0, 0), local_sem.at[0])
    for s in range(spans):
        @pl.when(s == c)
        def _():
            pltpu.make_async_copy(kv_ref, slot(s, 0), local_sem.at[0]).start()

    zeros = jnp.zeros((tok, kv_ref.shape[1]), kv_ref.dtype)
    for s in range(spans):
        @pl.when(s > c)
        def _():
            for o in range(NEIGH):
                slot(s, o)[...] = zeros
        @pl.when(s <= c)
        def _():
            for d in range(1, NEIGH):
                @pl.when(jnp.logical_not(inside(INVERSE[d])))
                def _():
                    slot(s, INVERSE[d])[...] = zeros

    for s in range(spans):
        @pl.when(s == c)
        def _():
            relay(s)

    for s in range(spans):
        @pl.when(s < c)
        def _():
            pltpu.make_async_remote_copy(
                src_ref=kv_ref, dst_ref=slot(s, 0), send_sem=send_sem.at[s], recv_sem=recv_sem.at[s * NEIGH],
                device_id=(s, i, j), device_id_type=mesh_id).wait_recv()
            for d in range(1, NEIGH):
                send_side(s, d, slot(s, 0))
            relay(s)

    for s in range(spans):
        @pl.when(s <= c)
        def _():
            for o in range(1, NEIGH):
                dy, dx = OFFSETS[o]
                @pl.when(inside(o))
                def _():
                    pltpu.make_async_remote_copy(
                        src_ref=kv_ref, dst_ref=slot(s, o), send_sem=send_sem.at[0],
                        recv_sem=recv_sem.at[s * NEIGH + o],
                        device_id=(c, i + dy, j + dx), device_id_type=mesh_id).wait_recv()

    for s in range(spans):
        @pl.when(s > c)
        def _():
            up_copy(s).wait_send()
        @pl.when(s <= c)
        def _():
            for d in range(1, NEIGH):
                send_side(s, d, kv_ref, wait=True)
            relay(s, wait=True)
    own.wait()

    attend_body(q_ref, kvbuf, live_ref, rowok_ref, o_ref)


def window_attend(q, kv, live, rowok, spans, rows, cols):
    tok, qw = q.shape
    kw = kv.shape[1]
    keys = spans * NEIGH * tok
    flops = 2 * 2 * tok * qw * keys
    kernel = lambda *refs: window_kernel(spans, rows, cols, *refs)
    return pl.pallas_call(
        kernel,
        out_shape=jax.ShapeDtypeStruct((tok, qw), q.dtype),
        in_specs=[pl.BlockSpec(memory_space=pltpu.VMEM)] * 4,
        out_specs=pl.BlockSpec(memory_space=pltpu.VMEM),
        scratch_shapes=[
            pltpu.VMEM((keys, kw), kv.dtype),
            pltpu.VMEM((2, spans, tok, kw), kv.dtype),
            pltpu.SemaphoreType.DMA((spans + spans * (NEIGH - 1),)),
            pltpu.SemaphoreType.DMA((spans * NEIGH,)),
            pltpu.SemaphoreType.DMA((2, spans)),
            pltpu.SemaphoreType.DMA((2, spans)),
            pltpu.SemaphoreType.DMA((1,)),
        ],
        compiler_params=pltpu.CompilerParams(
            vmem_limit_bytes=48 * 1024 * 1024, collective_id=0, has_side_effects=True),
        cost_estimate=pl.CostEstimate(
            flops=flops, transcendentals=tok * qw // HEAD_SIZE * keys,
            bytes_accessed=2 * (2 * tok * qw + keys * kw)),
    )(q, kv, live, rowok)


def shards(queries, key_value, pattern, counts, span_mask):
    tok_rows = queries.shape[3]
    spans, rows, cols = counts.shape
    my_span = lax.axis_index("span")
    my_row = lax.axis_index("ty")
    my_col = lax.axis_index("tx")
    zero_index = jnp.asarray(0).astype(jnp.int32)
    padded_counts = jnp.pad(counts, ((0, 0), (1, 1), (1, 1)))
    window = lax.dynamic_slice(padded_counts, (zero_index, my_row, my_col), (spans, 3, 3))
    near_counts = cross_tiles(window)
    own_count = lax.dynamic_index_in_dim(window[:, 1, 1], my_span, 0, keepdims=False)
    allowed = pattern.reshape(NEIGH) > 0
    span_row = lax.dynamic_index_in_dim(span_mask, my_span, 0, keepdims=False) > 0
    row_ids = jnp.arange(tok_rows, dtype=jnp.int32)
    live = (
        (row_ids[None, None, :] < near_counts[:, :, None])
        & allowed[None, :, None]
        & span_row[:, None, None]
    ).reshape(1, -1).astype(jnp.float32)
    rowok = (row_ids < own_count).astype(jnp.float32).reshape(tok_rows, 1)
    out = window_attend(
        queries.reshape(tok_rows, -1), key_value.reshape(tok_rows, -1), live, rowok, spans, rows, cols)
    return out.reshape(1, 1, 1, tok_rows, -1)


def solution(mesh):
    return jax.shard_map(
        shards,
        mesh=mesh,
        in_specs=(
            P("span", "ty", "tx", None, None),
            P("span", "ty", "tx", None, None),
            P("span", "ty", "tx", None),
            P(),
            P(),
        ),
        out_specs=P("span", "ty", "tx", None, None),
        check_vma=False,
    )
```

```python
import jax
import jax.numpy as jnp
from jax import lax
from jax.experimental import pallas as pl
from jax.experimental.pallas import tpu as pltpu
from jax.sharding import PartitionSpec as P

HEAD_SIZE = 128
NEIGH = 5
OFFSETS = ((0, 0), (-1, 0), (1, 0), (0, -1), (0, 1))
INVERSE = (0, 2, 1, 4, 3)


def cross_tiles(extended):
    return jnp.stack(
        [
            extended[:, 1, 1],
            extended[:, 0, 1],
            extended[:, 2, 1],
            extended[:, 1, 0],
            extended[:, 1, 2],
        ],
        axis=1,
    )


def attend_body(q_ref, kv_ref, live_ref, rowok_ref, o_ref):
    kv_heads = kv_ref.shape[1] // (2 * HEAD_SIZE)
    groups = q_ref.shape[1] // (kv_heads * HEAD_SIZE)
    tok = q_ref.shape[0]
    width = kv_heads * HEAD_SIZE
    scale = HEAD_SIZE ** (-0.5)
    live = live_ref[...] > 0
    rowok = jnp.concatenate([rowok_ref[...]] * groups, axis=0) > 0
    for h in range(kv_heads):
        qh = jnp.concatenate(
            [q_ref[:, (h * groups + g) * HEAD_SIZE:(h * groups + g + 1) * HEAD_SIZE] for g in range(groups)],
            axis=0,
        )
        kh = kv_ref[:, h * HEAD_SIZE:(h + 1) * HEAD_SIZE]
        s = lax.dot_general(qh, kh, (((1,), (1,)), ((), ())), preferred_element_type=jnp.float32)
        s = s * scale
        s = jnp.where(live, s, -1e30)
        m = jnp.max(s, axis=1, keepdims=True)
        p = jnp.where(live, jnp.exp(s - m), 0.0)
        tot = jnp.sum(p, axis=1, keepdims=True)
        vh = kv_ref[:, width + h * HEAD_SIZE:width + (h + 1) * HEAD_SIZE]
        acc = jnp.dot(p.astype(jnp.bfloat16), vh, preferred_element_type=jnp.float32)
        res = jnp.where(rowok, acc / tot, 0.0).astype(o_ref.dtype)
        for g in range(groups):
            col = (h * groups + g) * HEAD_SIZE
            o_ref[:, col:col + HEAD_SIZE] = res[g * tok:(g + 1) * tok]


def window_kernel(spans, rows, cols, q_hbm, kv_ref, live_ref, rowok_ref, o_ref,
                  q_ref, kvbuf, trans, send_sem, recv_sem, fwd_sem, trans_sem, local_sem):
    tok = kv_ref.shape[0]
    c = lax.axis_index("span")
    i = lax.axis_index("ty")
    j = lax.axis_index("tx")
    mesh_id = pl.DeviceIdType.MESH
    relayed = cols >= 4
    half = cols // 2
    is_a = j == half - 1
    is_b = j == half

    def relay_col(s):
        return 0 if s % 2 == 0 else cols - 1

    def inside(d):
        dy, dx = OFFSETS[d]
        y, x = i + dy, j + dx
        return (y >= 0) & (y < rows) & (x >= 0) & (x < cols)

    def slot(s, o):
        return kvbuf.at[pl.ds((s * NEIGH + o) * tok, tok), :]

    def boundary(d):
        if not relayed or d not in (3, 4):
            return None
        return is_a if d == 4 else is_b

    n_nb = sum(inside(d).astype(jnp.int32) for d in range(1, NEIGH))
    ends = (is_a | is_b | (j == 0) | (j == cols - 1)) if relayed else (j < 0)
    n_extra = jnp.where(ends, 2, 0)

    barrier = pltpu.get_barrier_semaphore()
    def greet(target):
        pl.semaphore_signal(barrier, 1, device_id=target, device_id_type=mesh_id)
    for s in range(spans):
        @pl.when(s != c)
        def _():
            greet((s, i, j))
    for d in range(1, NEIGH):
        dy, dx = OFFSETS[d]
        @pl.when(inside(d))
        def _():
            greet((c, i + dy, j + dx))
    if relayed:
        @pl.when(is_a | is_b)
        def _():
            greet((c, i, 0))
            greet((c, i, cols - 1))
        @pl.when((j == 0) | (j == cols - 1))
        def _():
            greet((c, i, half - 1))
            greet((c, i, half))
    pl.semaphore_wait(barrier, spans - 1 + n_nb + n_extra)

    def up_copy(s):
        return pltpu.make_async_remote_copy(
            src_ref=kv_ref, dst_ref=slot(c, 0), send_sem=send_sem.at[s], recv_sem=recv_sem.at[c * NEIGH],
            device_id=(s, i, j), device_id_type=mesh_id)

    def side_copy(s, d, src):
        dy, dx = OFFSETS[d]
        return pltpu.make_async_remote_copy(
            src_ref=src, dst_ref=slot(s, INVERSE[d]),
            send_sem=send_sem.at[spans + s * (NEIGH - 1) + d - 1],
            recv_sem=recv_sem.at[s * NEIGH + INVERSE[d]],
            device_id=(c, i + dy, j + dx), device_id_type=mesh_id)

    def to_relay(s, d, src):
        way = 0 if d == 4 else 1
        return pltpu.make_async_remote_copy(
            src_ref=src, dst_ref=trans.at[way, s],
            send_sem=send_sem.at[spans + s * (NEIGH - 1) + d - 1],
            recv_sem=trans_sem.at[way, s],
            device_id=(c, i, relay_col(s)), device_id_type=mesh_id)

    def from_relay(s, way):
        target = half if way == 0 else half - 1
        o = 3 if way == 0 else 4
        return pltpu.make_async_remote_copy(
            src_ref=trans.at[way, s], dst_ref=slot(s, o),
            send_sem=fwd_sem.at[way, s], recv_sem=recv_sem.at[s * NEIGH + o],
            device_id=(c, i, target), device_id_type=mesh_id)

    def send_side(s, d, src, wait=False):
        bnd = boundary(d)
        direct = inside(d) if bnd is None else inside(d) & jnp.logical_not(bnd)
        @pl.when(direct)
        def _():
            cp = side_copy(s, d, src)
            cp.wait_send() if wait else cp.start()
        if bnd is not None:
            @pl.when(bnd)
            def _():
                cp = to_relay(s, d, src)
                cp.wait_send() if wait else cp.start()

    def relay(s, wait=False):
        if not relayed:
            return
        @pl.when(j == relay_col(s))
        def _():
            for way in (0, 1):
                if wait:
                    from_relay(s, way).wait_send()
                else:
                    to_relay(s, 4 if way == 0 else 3, kv_ref).wait_recv()
                    from_relay(s, way).start()

    q_load = pltpu.make_async_copy(q_hbm, q_ref, local_sem.at[1])
    q_load.start()

    for s in range(spans):
        @pl.when(s > c)
        def _():
            up_copy(s).start()

    for s in range(spans):
        @pl.when(s == c)
        def _():
            for d in range(1, NEIGH):
                send_side(s, d, kv_ref)

    own = pltpu.make_async_copy(kv_ref, slot(0, 0), local_sem.at[0])
    for s in range(spans):
        @pl.when(s == c)
        def _():
            pltpu.make_async_copy(kv_ref, slot(s, 0), local_sem.at[0]).start()

    zeros = jnp.zeros((tok, kv_ref.shape[1]), kv_ref.dtype)
    for s in range(spans):
        @pl.when(s > c)
        def _():
            for o in range(NEIGH):
                slot(s, o)[...] = zeros
        @pl.when(s <= c)
        def _():
            for d in range(1, NEIGH):
                @pl.when(jnp.logical_not(inside(INVERSE[d])))
                def _():
                    slot(s, INVERSE[d])[...] = zeros

    for s in range(spans):
        @pl.when(s == c)
        def _():
            relay(s)

    def ring_gap(a, b):
        return min((a - b) % spans, (b - a) % spans)

    for cc in range(spans):
        @pl.when(c == cc)
        def _():
            for s in sorted(range(cc), key=lambda s: (ring_gap(s, cc), -s)):
                pltpu.make_async_remote_copy(
                    src_ref=kv_ref, dst_ref=slot(s, 0), send_sem=send_sem.at[s], recv_sem=recv_sem.at[s * NEIGH],
                    device_id=(s, i, j), device_id_type=mesh_id).wait_recv()
                for d in range(1, NEIGH):
                    send_side(s, d, slot(s, 0))
                relay(s)

    for s in range(spans):
        @pl.when(s <= c)
        def _():
            for o in range(1, NEIGH):
                dy, dx = OFFSETS[o]
                @pl.when(inside(o))
                def _():
                    pltpu.make_async_remote_copy(
                        src_ref=kv_ref, dst_ref=slot(s, o), send_sem=send_sem.at[0],
                        recv_sem=recv_sem.at[s * NEIGH + o],
                        device_id=(c, i + dy, j + dx), device_id_type=mesh_id).wait_recv()

    for s in range(spans):
        @pl.when(s > c)
        def _():
            up_copy(s).wait_send()
        @pl.when(s <= c)
        def _():
            for d in range(1, NEIGH):
                send_side(s, d, kv_ref, wait=True)
            relay(s, wait=True)
    own.wait()
    q_load.wait()

    attend_body(q_ref, kvbuf, live_ref, rowok_ref, o_ref)


def window_attend(q, kv, live, rowok, spans, rows, cols):
    tok, qw = q.shape
    kw = kv.shape[1]
    keys = spans * NEIGH * tok
    flops = 2 * 2 * tok * qw * keys
    kernel = lambda *refs: window_kernel(spans, rows, cols, *refs)
    return pl.pallas_call(
        kernel,
        out_shape=jax.ShapeDtypeStruct((tok, qw), q.dtype),
        in_specs=[pl.BlockSpec(memory_space=pl.ANY)] * 2 + [pl.BlockSpec(memory_space=pltpu.VMEM)] * 2,
        out_specs=pl.BlockSpec(memory_space=pltpu.VMEM),
        scratch_shapes=[
            pltpu.VMEM((tok, qw), q.dtype),
            pltpu.VMEM((keys, kw), kv.dtype),
            pltpu.VMEM((2, spans, tok, kw), kv.dtype),
            pltpu.SemaphoreType.DMA((spans + spans * (NEIGH - 1),)),
            pltpu.SemaphoreType.DMA((spans * NEIGH,)),
            pltpu.SemaphoreType.DMA((2, spans)),
            pltpu.SemaphoreType.DMA((2, spans)),
            pltpu.SemaphoreType.DMA((2,)),
        ],
        compiler_params=pltpu.CompilerParams(
            vmem_limit_bytes=67043328, collective_id=0, has_side_effects=True),
        cost_estimate=pl.CostEstimate(
            flops=flops, transcendentals=tok * qw // HEAD_SIZE * keys,
            bytes_accessed=2 * (2 * tok * qw + keys * kw)),
    )(q, kv, live, rowok)


def shards(queries, key_value, pattern, counts, span_mask):
    tok_rows = queries.shape[3]
    spans, rows, cols = counts.shape
    my_span = lax.axis_index("span")
    my_row = lax.axis_index("ty")
    my_col = lax.axis_index("tx")
    zero_index = jnp.asarray(0).astype(jnp.int32)
    padded_counts = jnp.pad(counts, ((0, 0), (1, 1), (1, 1)))
    window = lax.dynamic_slice(padded_counts, (zero_index, my_row, my_col), (spans, 3, 3))
    near_counts = cross_tiles(window)
    own_count = lax.dynamic_index_in_dim(window[:, 1, 1], my_span, 0, keepdims=False)
    allowed = pattern.reshape(NEIGH) > 0
    span_row = lax.dynamic_index_in_dim(span_mask, my_span, 0, keepdims=False) > 0
    row_ids = jnp.arange(tok_rows, dtype=jnp.int32)
    live = (
        (row_ids[None, None, :] < near_counts[:, :, None])
        & allowed[None, :, None]
        & span_row[:, None, None]
    ).reshape(1, -1).astype(jnp.float32)
    rowok = (row_ids < own_count).astype(jnp.float32).reshape(tok_rows, 1)
    out = window_attend(
        queries.reshape(tok_rows, -1), key_value.reshape(tok_rows, -1), live, rowok, spans, rows, cols)
    return out.reshape(1, 1, 1, tok_rows, -1)


def solution(mesh):
    return jax.shard_map(
        shards,
        mesh=mesh,
        in_specs=(
            P("span", "ty", "tx", None, None),
            P("span", "ty", "tx", None, None),
            P("span", "ty", "tx", None),
            P(),
            P(),
        ),
        out_specs=P("span", "ty", "tx", None, None),
        check_vma=False,
    )
```

```python
import jax
import jax.numpy as jnp
from jax import lax
from jax.experimental import pallas as pl
from jax.experimental.pallas import tpu as pltpu
from jax.sharding import PartitionSpec as P

HEAD_SIZE = 128
NEIGH = 5
OFFSETS = ((0, 0), (-1, 0), (1, 0), (0, -1), (0, 1))
INVERSE = (0, 2, 1, 4, 3)


def cross_tiles(extended):
    return jnp.stack(
        [
            extended[:, 1, 1],
            extended[:, 0, 1],
            extended[:, 2, 1],
            extended[:, 1, 0],
            extended[:, 1, 2],
        ],
        axis=1,
    )


def load_queries(q_ref, q3, kv_heads, groups):
    for h in range(kv_heads):
        q3[h] = jnp.concatenate(
            [q_ref[:, (h * groups + g) * HEAD_SIZE:(h * groups + g + 1) * HEAD_SIZE] for g in range(groups)],
            axis=0,
        )


def attend_chunk(q3, kvbuf, live_ref, m_sc, l_sc, acc_sc, s, tok):
    kv_heads = q3.shape[0]
    width = kv_heads * HEAD_SIZE
    scale = HEAD_SIZE ** (-0.5)
    lo, n = s * NEIGH * tok, NEIGH * tok
    live = live_ref[:, lo:lo + n] > 0
    for h in range(kv_heads):
        kh = kvbuf[lo:lo + n, h * HEAD_SIZE:(h + 1) * HEAD_SIZE]
        sc = lax.dot_general(q3[h], kh, (((1,), (1,)), ((), ())), preferred_element_type=jnp.float32)
        sc = jnp.where(live, sc * scale, -1e30)
        m_old = m_sc[h]
        m_new = jnp.maximum(m_old, jnp.max(sc, axis=1, keepdims=True))
        p = jnp.where(live, jnp.exp(sc - m_new), 0.0)
        fade = jnp.exp(m_old - m_new)
        l_sc[h] = l_sc[h] * fade + jnp.sum(p, axis=1, keepdims=True)
        vh = kvbuf[lo:lo + n, width + h * HEAD_SIZE:width + (h + 1) * HEAD_SIZE]
        acc_sc[h] = acc_sc[h] * fade + jnp.dot(p.astype(jnp.bfloat16), vh, preferred_element_type=jnp.float32)
        m_sc[h] = m_new


def attend_finish(rowok_ref, l_sc, acc_sc, o_ref, groups, tok):
    kv_heads = acc_sc.shape[0]
    rowok = jnp.concatenate([rowok_ref[...]] * groups, axis=0) > 0
    for h in range(kv_heads):
        res = jnp.where(rowok, acc_sc[h] / l_sc[h], 0.0).astype(o_ref.dtype)
        for g in range(groups):
            col = (h * groups + g) * HEAD_SIZE
            o_ref[:, col:col + HEAD_SIZE] = res[g * tok:(g + 1) * tok]


def window_kernel(spans, rows, cols, q_hbm, kv_ref, live_ref, rowok_ref, o_ref,
                  q_ref, kvbuf, trans, q3, m_sc, l_sc, acc_sc,
                  send_sem, recv_sem, fwd_sem, trans_sem, local_sem):
    tok = kv_ref.shape[0]
    c = lax.axis_index("span")
    i = lax.axis_index("ty")
    j = lax.axis_index("tx")
    mesh_id = pl.DeviceIdType.MESH
    relayed = cols >= 4
    half = cols // 2
    is_a = j == half - 1
    is_b = j == half

    def relay_col(s):
        return 0 if s % 2 == 0 else cols - 1

    def inside(d):
        dy, dx = OFFSETS[d]
        y, x = i + dy, j + dx
        return (y >= 0) & (y < rows) & (x >= 0) & (x < cols)

    def slot(s, o):
        return kvbuf.at[pl.ds((s * NEIGH + o) * tok, tok), :]

    def boundary(d):
        if not relayed or d not in (3, 4):
            return None
        return is_a if d == 4 else is_b

    n_nb = sum(inside(d).astype(jnp.int32) for d in range(1, NEIGH))
    ends = (is_a | is_b | (j == 0) | (j == cols - 1)) if relayed else (j < 0)
    n_extra = jnp.where(ends, 2, 0)

    barrier = pltpu.get_barrier_semaphore()
    def greet(target):
        pl.semaphore_signal(barrier, 1, device_id=target, device_id_type=mesh_id)
    for s in range(spans):
        @pl.when(s != c)
        def _():
            greet((s, i, j))
    for d in range(1, NEIGH):
        dy, dx = OFFSETS[d]
        @pl.when(inside(d))
        def _():
            greet((c, i + dy, j + dx))
    if relayed:
        @pl.when(is_a | is_b)
        def _():
            greet((c, i, 0))
            greet((c, i, cols - 1))
        @pl.when((j == 0) | (j == cols - 1))
        def _():
            greet((c, i, half - 1))
            greet((c, i, half))
    pl.semaphore_wait(barrier, spans - 1 + n_nb + n_extra)

    def up_copy(s):
        return pltpu.make_async_remote_copy(
            src_ref=kv_ref, dst_ref=slot(c, 0), send_sem=send_sem.at[s], recv_sem=recv_sem.at[c * NEIGH],
            device_id=(s, i, j), device_id_type=mesh_id)

    def side_copy(s, d, src):
        dy, dx = OFFSETS[d]
        return pltpu.make_async_remote_copy(
            src_ref=src, dst_ref=slot(s, INVERSE[d]),
            send_sem=send_sem.at[spans + s * (NEIGH - 1) + d - 1],
            recv_sem=recv_sem.at[s * NEIGH + INVERSE[d]],
            device_id=(c, i + dy, j + dx), device_id_type=mesh_id)

    def to_relay(s, d, src):
        way = 0 if d == 4 else 1
        return pltpu.make_async_remote_copy(
            src_ref=src, dst_ref=trans.at[way, s],
            send_sem=send_sem.at[spans + s * (NEIGH - 1) + d - 1],
            recv_sem=trans_sem.at[way, s],
            device_id=(c, i, relay_col(s)), device_id_type=mesh_id)

    def from_relay(s, way):
        target = half if way == 0 else half - 1
        o = 3 if way == 0 else 4
        return pltpu.make_async_remote_copy(
            src_ref=trans.at[way, s], dst_ref=slot(s, o),
            send_sem=fwd_sem.at[way, s], recv_sem=recv_sem.at[s * NEIGH + o],
            device_id=(c, i, target), device_id_type=mesh_id)

    def send_side(s, d, src, wait=False):
        bnd = boundary(d)
        direct = inside(d) if bnd is None else inside(d) & jnp.logical_not(bnd)
        @pl.when(direct)
        def _():
            cp = side_copy(s, d, src)
            cp.wait_send() if wait else cp.start()
        if bnd is not None:
            @pl.when(bnd)
            def _():
                cp = to_relay(s, d, src)
                cp.wait_send() if wait else cp.start()

    def relay(s, wait=False):
        if not relayed:
            return
        @pl.when(j == relay_col(s))
        def _():
            for way in (0, 1):
                if wait:
                    from_relay(s, way).wait_send()
                else:
                    to_relay(s, 4 if way == 0 else 3, kv_ref).wait_recv()
                    from_relay(s, way).start()

    q_load = pltpu.make_async_copy(q_hbm, q_ref, local_sem.at[1])
    q_load.start()

    for s in range(spans):
        @pl.when(s > c)
        def _():
            up_copy(s).start()

    for s in range(spans):
        @pl.when(s == c)
        def _():
            for d in range(1, NEIGH):
                send_side(s, d, kv_ref)

    own = pltpu.make_async_copy(kv_ref, slot(0, 0), local_sem.at[0])
    for s in range(spans):
        @pl.when(s == c)
        def _():
            pltpu.make_async_copy(kv_ref, slot(s, 0), local_sem.at[0]).start()

    zeros = jnp.zeros((tok, kv_ref.shape[1]), kv_ref.dtype)
    for s in range(spans):
        @pl.when(s <= c)
        def _():
            for d in range(1, NEIGH):
                @pl.when(jnp.logical_not(inside(INVERSE[d])))
                def _():
                    slot(s, INVERSE[d])[...] = zeros

    for s in range(spans):
        @pl.when(s == c)
        def _():
            relay(s)

    def ring_gap(a, b):
        return min((a - b) % spans, (b - a) % spans)

    for cc in range(spans):
        @pl.when(c == cc)
        def _():
            for s in sorted(range(cc), key=lambda s: (ring_gap(s, cc), -s)):
                pltpu.make_async_remote_copy(
                    src_ref=kv_ref, dst_ref=slot(s, 0), send_sem=send_sem.at[s], recv_sem=recv_sem.at[s * NEIGH],
                    device_id=(s, i, j), device_id_type=mesh_id).wait_recv()
                for d in range(1, NEIGH):
                    send_side(s, d, slot(s, 0))
                relay(s)

    for s in range(spans):
        @pl.when(s > c)
        def _():
            up_copy(s).wait_send()
    own.wait()
    q_load.wait()

    kv_heads = q3.shape[0]
    groups = q_ref.shape[1] // (kv_heads * HEAD_SIZE)
    load_queries(q_ref, q3, kv_heads, groups)
    m_sc[...] = jnp.full(m_sc.shape, -1e30, jnp.float32)
    l_sc[...] = jnp.zeros(l_sc.shape, jnp.float32)
    acc_sc[...] = jnp.zeros(acc_sc.shape, jnp.float32)

    for cc in range(spans):
        @pl.when(c == cc)
        def _():
            order = [cc] + sorted(range(cc), key=lambda s: (ring_gap(s, cc), -s))
            for s in order:
                for o in range(1, NEIGH):
                    dy, dx = OFFSETS[o]
                    @pl.when(inside(o))
                    def _():
                        pltpu.make_async_remote_copy(
                            src_ref=kv_ref, dst_ref=slot(s, o), send_sem=send_sem.at[0],
                            recv_sem=recv_sem.at[s * NEIGH + o],
                            device_id=(c, i + dy, j + dx), device_id_type=mesh_id).wait_recv()
                attend_chunk(q3, kvbuf, live_ref, m_sc, l_sc, acc_sc, s, tok)

    for s in range(spans):
        @pl.when(s <= c)
        def _():
            for d in range(1, NEIGH):
                send_side(s, d, kv_ref, wait=True)
            relay(s, wait=True)

    attend_finish(rowok_ref, l_sc, acc_sc, o_ref, groups, tok)


def window_attend(q, kv, live, rowok, spans, rows, cols):
    tok, qw = q.shape
    kw = kv.shape[1]
    keys = spans * NEIGH * tok
    flops = 2 * 2 * tok * qw * keys
    kernel = lambda *refs: window_kernel(spans, rows, cols, *refs)
    return pl.pallas_call(
        kernel,
        out_shape=jax.ShapeDtypeStruct((tok, qw), q.dtype),
        in_specs=[pl.BlockSpec(memory_space=pl.ANY)] * 2 + [pl.BlockSpec(memory_space=pltpu.VMEM)] * 2,
        out_specs=pl.BlockSpec(memory_space=pltpu.VMEM),
        scratch_shapes=[
            pltpu.VMEM((tok, qw), q.dtype),
            pltpu.VMEM((keys, kw), kv.dtype),
            pltpu.VMEM((2, spans, tok, kw), kv.dtype),
            pltpu.VMEM((kw // (2 * HEAD_SIZE), qw // (kw // 2) * tok, HEAD_SIZE), q.dtype),
            pltpu.VMEM((kw // (2 * HEAD_SIZE), qw // (kw // 2) * tok, 1), jnp.float32),
            pltpu.VMEM((kw // (2 * HEAD_SIZE), qw // (kw // 2) * tok, 1), jnp.float32),
            pltpu.VMEM((kw // (2 * HEAD_SIZE), qw // (kw // 2) * tok, HEAD_SIZE), jnp.float32),
            pltpu.SemaphoreType.DMA((spans + spans * (NEIGH - 1),)),
            pltpu.SemaphoreType.DMA((spans * NEIGH,)),
            pltpu.SemaphoreType.DMA((2, spans)),
            pltpu.SemaphoreType.DMA((2, spans)),
            pltpu.SemaphoreType.DMA((2,)),
        ],
        compiler_params=pltpu.CompilerParams(
            vmem_limit_bytes=67043328, collective_id=0, has_side_effects=True),
        cost_estimate=pl.CostEstimate(
            flops=flops, transcendentals=tok * qw // HEAD_SIZE * keys,
            bytes_accessed=2 * (2 * tok * qw + keys * kw)),
    )(q, kv, live, rowok)


def shards(queries, key_value, pattern, counts, span_mask):
    tok_rows = queries.shape[3]
    spans, rows, cols = counts.shape
    my_span = lax.axis_index("span")
    my_row = lax.axis_index("ty")
    my_col = lax.axis_index("tx")
    zero_index = jnp.asarray(0).astype(jnp.int32)
    padded_counts = jnp.pad(counts, ((0, 0), (1, 1), (1, 1)))
    window = lax.dynamic_slice(padded_counts, (zero_index, my_row, my_col), (spans, 3, 3))
    near_counts = cross_tiles(window)
    own_count = lax.dynamic_index_in_dim(window[:, 1, 1], my_span, 0, keepdims=False)
    allowed = pattern.reshape(NEIGH) > 0
    span_row = lax.dynamic_index_in_dim(span_mask, my_span, 0, keepdims=False) > 0
    row_ids = jnp.arange(tok_rows, dtype=jnp.int32)
    live = (
        (row_ids[None, None, :] < near_counts[:, :, None])
        & allowed[None, :, None]
        & span_row[:, None, None]
    ).reshape(1, -1).astype(jnp.float32)
    rowok = (row_ids < own_count).astype(jnp.float32).reshape(tok_rows, 1)
    out = window_attend(
        queries.reshape(tok_rows, -1), key_value.reshape(tok_rows, -1), live, rowok, spans, rows, cols)
    return out.reshape(1, 1, 1, tok_rows, -1)


def solution(mesh):
    return jax.shard_map(
        shards,
        mesh=mesh,
        in_specs=(
            P("span", "ty", "tx", None, None),
            P("span", "ty", "tx", None, None),
            P("span", "ty", "tx", None),
            P(),
            P(),
        ),
        out_specs=P("span", "ty", "tx", None, None),
        check_vma=False,
    )
```

```python
import jax
import jax.numpy as jnp
from jax import lax
from jax.experimental import pallas as pl
from jax.experimental.pallas import tpu as pltpu
from jax.sharding import PartitionSpec as P

HEAD_SIZE = 128
NEIGH = 5
OFFSETS = ((0, 0), (-1, 0), (1, 0), (0, -1), (0, 1))
INVERSE = (0, 2, 1, 4, 3)


def cross_tiles(extended):
    return jnp.stack(
        [
            extended[:, 1, 1],
            extended[:, 0, 1],
            extended[:, 2, 1],
            extended[:, 1, 0],
            extended[:, 1, 2],
        ],
        axis=1,
    )


def load_queries(q_ref, q3, kv_heads, groups):
    for h in range(kv_heads):
        q3[h] = jnp.concatenate(
            [q_ref[:, (h * groups + g) * HEAD_SIZE:(h * groups + g + 1) * HEAD_SIZE] for g in range(groups)],
            axis=0,
        )


def attend_chunk(q3, kvbuf, live_ref, m_sc, l_sc, acc_sc, s, tok):
    kv_heads = q3.shape[0]
    width = kv_heads * HEAD_SIZE
    scale = HEAD_SIZE ** (-0.5)
    lo, n = s * NEIGH * tok, NEIGH * tok
    live = live_ref[:, lo:lo + n] > 0
    for h in range(kv_heads):
        kh = kvbuf[lo:lo + n, h * HEAD_SIZE:(h + 1) * HEAD_SIZE]
        sc = lax.dot_general(q3[h], kh, (((1,), (1,)), ((), ())), preferred_element_type=jnp.float32)
        sc = jnp.where(live, sc * scale, -1e30)
        m_old = m_sc[h]
        m_new = jnp.maximum(m_old, jnp.max(sc, axis=1, keepdims=True))
        p = jnp.where(live, jnp.exp(sc - m_new), 0.0)
        fade = jnp.exp(m_old - m_new)
        l_sc[h] = l_sc[h] * fade + jnp.sum(p, axis=1, keepdims=True)
        vh = kvbuf[lo:lo + n, width + h * HEAD_SIZE:width + (h + 1) * HEAD_SIZE]
        acc_sc[h] = acc_sc[h] * fade + jnp.dot(p.astype(jnp.bfloat16), vh, preferred_element_type=jnp.float32)
        m_sc[h] = m_new


def attend_finish(rowok_ref, l_sc, acc_sc, o_ref, groups, tok):
    kv_heads = acc_sc.shape[0]
    rowok = jnp.concatenate([rowok_ref[...]] * groups, axis=0) > 0
    for h in range(kv_heads):
        res = jnp.where(rowok, acc_sc[h] / l_sc[h], 0.0).astype(o_ref.dtype)
        for g in range(groups):
            col = (h * groups + g) * HEAD_SIZE
            o_ref[:, col:col + HEAD_SIZE] = res[g * tok:(g + 1) * tok]


def window_kernel(spans, rows, cols, q_hbm, kv_ref, live_ref, rowok_ref, o_ref,
                  q_ref, kvbuf, trans, q3, m_sc, l_sc, acc_sc,
                  send_sem, recv_sem, fwd_sem, trans_sem, local_sem):
    tok = kv_ref.shape[0]
    c = lax.axis_index("span")
    i = lax.axis_index("ty")
    j = lax.axis_index("tx")
    mesh_id = pl.DeviceIdType.MESH
    relayed = cols >= 4
    half = cols // 2
    is_a = j == half - 1
    is_b = j == half

    def relay_col(s):
        return 0 if s % 2 == 0 else cols - 1

    def inside(d):
        dy, dx = OFFSETS[d]
        y, x = i + dy, j + dx
        return (y >= 0) & (y < rows) & (x >= 0) & (x < cols)

    def slot(s, o):
        return kvbuf.at[pl.ds((s * NEIGH + o) * tok, tok), :]

    def boundary(d):
        if not relayed or d not in (3, 4):
            return None
        return is_a if d == 4 else is_b

    n_nb = sum(inside(d).astype(jnp.int32) for d in range(1, NEIGH))
    ends = (is_a | is_b | (j == 0) | (j == cols - 1)) if relayed else (j < 0)
    n_extra = jnp.where(ends, 2, 0)

    barrier = pltpu.get_barrier_semaphore()
    def greet(target):
        pl.semaphore_signal(barrier, 1, device_id=target, device_id_type=mesh_id)
    for s in range(spans):
        @pl.when(s != c)
        def _():
            greet((s, i, j))
    for d in range(1, NEIGH):
        dy, dx = OFFSETS[d]
        @pl.when(inside(d))
        def _():
            greet((c, i + dy, j + dx))
    if relayed:
        @pl.when(is_a | is_b)
        def _():
            greet((c, i, 0))
            greet((c, i, cols - 1))
        @pl.when((j == 0) | (j == cols - 1))
        def _():
            greet((c, i, half - 1))
            greet((c, i, half))
    pl.semaphore_wait(barrier, spans - 1 + n_nb + n_extra)

    def up_copy(s):
        return pltpu.make_async_remote_copy(
            src_ref=kv_ref, dst_ref=slot(c, 0), send_sem=send_sem.at[s], recv_sem=recv_sem.at[c * NEIGH],
            device_id=(s, i, j), device_id_type=mesh_id)

    def side_copy(s, d, src):
        dy, dx = OFFSETS[d]
        return pltpu.make_async_remote_copy(
            src_ref=src, dst_ref=slot(s, INVERSE[d]),
            send_sem=send_sem.at[spans + s * (NEIGH - 1) + d - 1],
            recv_sem=recv_sem.at[s * NEIGH + INVERSE[d]],
            device_id=(c, i + dy, j + dx), device_id_type=mesh_id)

    def to_relay(s, d, src):
        way = 0 if d == 4 else 1
        return pltpu.make_async_remote_copy(
            src_ref=src, dst_ref=trans.at[way, s],
            send_sem=send_sem.at[spans + s * (NEIGH - 1) + d - 1],
            recv_sem=trans_sem.at[way, s],
            device_id=(c, i, relay_col(s)), device_id_type=mesh_id)

    def from_relay(s, way):
        target = half if way == 0 else half - 1
        o = 3 if way == 0 else 4
        return pltpu.make_async_remote_copy(
            src_ref=trans.at[way, s], dst_ref=slot(s, o),
            send_sem=fwd_sem.at[way, s], recv_sem=recv_sem.at[s * NEIGH + o],
            device_id=(c, i, target), device_id_type=mesh_id)

    def send_side(s, d, src, wait=False):
        bnd = boundary(d)
        direct = inside(d) if bnd is None else inside(d) & jnp.logical_not(bnd)
        @pl.when(direct)
        def _():
            cp = side_copy(s, d, src)
            cp.wait_send() if wait else cp.start()
        if bnd is not None:
            @pl.when(bnd)
            def _():
                cp = to_relay(s, d, src)
                cp.wait_send() if wait else cp.start()

    def relay(s, wait=False):
        if not relayed:
            return
        @pl.when(j == relay_col(s))
        def _():
            for way in (0, 1):
                if wait:
                    from_relay(s, way).wait_send()
                else:
                    to_relay(s, 4 if way == 0 else 3, kv_ref).wait_recv()
                    from_relay(s, way).start()

    q_load = pltpu.make_async_copy(q_hbm, q_ref, local_sem.at[1])
    q_load.start()

    for s in range(spans):
        @pl.when(s > c)
        def _():
            up_copy(s).start()

    for s in range(spans):
        @pl.when(s == c)
        def _():
            for d in range(1, NEIGH):
                send_side(s, d, kv_ref)

    own = pltpu.make_async_copy(kv_ref, slot(0, 0), local_sem.at[0])
    for s in range(spans):
        @pl.when(s == c)
        def _():
            pltpu.make_async_copy(kv_ref, slot(s, 0), local_sem.at[0]).start()

    zeros = jnp.zeros((tok, kv_ref.shape[1]), kv_ref.dtype)
    for s in range(spans):
        @pl.when(s <= c)
        def _():
            for d in range(1, NEIGH):
                @pl.when(jnp.logical_not(inside(INVERSE[d])))
                def _():
                    slot(s, INVERSE[d])[...] = zeros

    for s in range(spans):
        @pl.when(s == c)
        def _():
            relay(s)

    def ring_gap(a, b):
        return min((a - b) % spans, (b - a) % spans)

    for cc in range(spans):
        @pl.when(c == cc)
        def _():
            for s in sorted(range(cc), key=lambda s: (ring_gap(s, cc), -s)):
                pltpu.make_async_remote_copy(
                    src_ref=kv_ref, dst_ref=slot(s, 0), send_sem=send_sem.at[s], recv_sem=recv_sem.at[s * NEIGH],
                    device_id=(s, i, j), device_id_type=mesh_id).wait_recv()
                for d in range(1, NEIGH):
                    send_side(s, d, slot(s, 0))
            for s in sorted(range(cc), key=lambda s: (ring_gap(s, cc), -s)):
                relay(s)

    for s in range(spans):
        @pl.when(s > c)
        def _():
            up_copy(s).wait_send()
    own.wait()
    q_load.wait()

    kv_heads = q3.shape[0]
    groups = q_ref.shape[1] // (kv_heads * HEAD_SIZE)
    load_queries(q_ref, q3, kv_heads, groups)
    m_sc[...] = jnp.full(m_sc.shape, -1e30, jnp.float32)
    l_sc[...] = jnp.zeros(l_sc.shape, jnp.float32)
    acc_sc[...] = jnp.zeros(acc_sc.shape, jnp.float32)

    for cc in range(spans):
        @pl.when(c == cc)
        def _():
            order = [cc] + sorted(range(cc), key=lambda s: (ring_gap(s, cc), -s))
            for s in order:
                for o in range(1, NEIGH):
                    dy, dx = OFFSETS[o]
                    @pl.when(inside(o))
                    def _():
                        pltpu.make_async_remote_copy(
                            src_ref=kv_ref, dst_ref=slot(s, o), send_sem=send_sem.at[0],
                            recv_sem=recv_sem.at[s * NEIGH + o],
                            device_id=(c, i + dy, j + dx), device_id_type=mesh_id).wait_recv()
                attend_chunk(q3, kvbuf, live_ref, m_sc, l_sc, acc_sc, s, tok)

    for s in range(spans):
        @pl.when(s <= c)
        def _():
            for d in range(1, NEIGH):
                send_side(s, d, kv_ref, wait=True)
            relay(s, wait=True)

    attend_finish(rowok_ref, l_sc, acc_sc, o_ref, groups, tok)


def window_attend(q, kv, live, rowok, spans, rows, cols):
    tok, qw = q.shape
    kw = kv.shape[1]
    keys = spans * NEIGH * tok
    flops = 2 * 2 * tok * qw * keys
    kernel = lambda *refs: window_kernel(spans, rows, cols, *refs)
    return pl.pallas_call(
        kernel,
        out_shape=jax.ShapeDtypeStruct((tok, qw), q.dtype),
        in_specs=[pl.BlockSpec(memory_space=pl.ANY)] * 2 + [pl.BlockSpec(memory_space=pltpu.VMEM)] * 2,
        out_specs=pl.BlockSpec(memory_space=pltpu.VMEM),
        scratch_shapes=[
            pltpu.VMEM((tok, qw), q.dtype),
            pltpu.VMEM((keys, kw), kv.dtype),
            pltpu.VMEM((2, spans, tok, kw), kv.dtype),
            pltpu.VMEM((kw // (2 * HEAD_SIZE), qw // (kw // 2) * tok, HEAD_SIZE), q.dtype),
            pltpu.VMEM((kw // (2 * HEAD_SIZE), qw // (kw // 2) * tok, 1), jnp.float32),
            pltpu.VMEM((kw // (2 * HEAD_SIZE), qw // (kw // 2) * tok, 1), jnp.float32),
            pltpu.VMEM((kw // (2 * HEAD_SIZE), qw // (kw // 2) * tok, HEAD_SIZE), jnp.float32),
            pltpu.SemaphoreType.DMA((spans + spans * (NEIGH - 1),)),
            pltpu.SemaphoreType.DMA((spans * NEIGH,)),
            pltpu.SemaphoreType.DMA((2, spans)),
            pltpu.SemaphoreType.DMA((2, spans)),
            pltpu.SemaphoreType.DMA((2,)),
        ],
        compiler_params=pltpu.CompilerParams(
            vmem_limit_bytes=67043328, collective_id=0, has_side_effects=True),
        cost_estimate=pl.CostEstimate(
            flops=flops, transcendentals=tok * qw // HEAD_SIZE * keys,
            bytes_accessed=2 * (2 * tok * qw + keys * kw)),
    )(q, kv, live, rowok)


def shards(queries, key_value, pattern, counts, span_mask):
    tok_rows = queries.shape[3]
    spans, rows, cols = counts.shape
    my_span = lax.axis_index("span")
    my_row = lax.axis_index("ty")
    my_col = lax.axis_index("tx")
    zero_index = jnp.asarray(0).astype(jnp.int32)
    padded_counts = jnp.pad(counts, ((0, 0), (1, 1), (1, 1)))
    window = lax.dynamic_slice(padded_counts, (zero_index, my_row, my_col), (spans, 3, 3))
    near_counts = cross_tiles(window)
    own_count = lax.dynamic_index_in_dim(window[:, 1, 1], my_span, 0, keepdims=False)
    allowed = pattern.reshape(NEIGH) > 0
    span_row = lax.dynamic_index_in_dim(span_mask, my_span, 0, keepdims=False) > 0
    row_ids = jnp.arange(tok_rows, dtype=jnp.int32)
    live = (
        (row_ids[None, None, :] < near_counts[:, :, None])
        & allowed[None, :, None]
        & span_row[:, None, None]
    ).reshape(1, -1).astype(jnp.float32)
    rowok = (row_ids < own_count).astype(jnp.float32).reshape(tok_rows, 1)
    out = window_attend(
        queries.reshape(tok_rows, -1), key_value.reshape(tok_rows, -1), live, rowok, spans, rows, cols)
    return out.reshape(1, 1, 1, tok_rows, -1)


def solution(mesh):
    return jax.shard_map(
        shards,
        mesh=mesh,
        in_specs=(
            P("span", "ty", "tx", None, None),
            P("span", "ty", "tx", None, None),
            P("span", "ty", "tx", None),
            P(),
            P(),
        ),
        out_specs=P("span", "ty", "tx", None, None),
        check_vma=False,
    )
```

```python
import jax
import jax.numpy as jnp
from jax import lax
from jax.experimental import pallas as pl
from jax.experimental.pallas import tpu as pltpu
from jax.sharding import PartitionSpec as P

HEAD_SIZE = 128
NEIGH = 5
OFFSETS = ((0, 0), (-1, 0), (1, 0), (0, -1), (0, 1))
INVERSE = (0, 2, 1, 4, 3)


def cross_tiles(extended):
    return jnp.stack(
        [
            extended[:, 1, 1],
            extended[:, 0, 1],
            extended[:, 2, 1],
            extended[:, 1, 0],
            extended[:, 1, 2],
        ],
        axis=1,
    )


def load_queries(q_ref, q3, kv_heads, groups):
    for h in range(kv_heads):
        q3[h] = jnp.concatenate(
            [q_ref[:, (h * groups + g) * HEAD_SIZE:(h * groups + g + 1) * HEAD_SIZE] for g in range(groups)],
            axis=0,
        )


def attend_chunk(q3, kvbuf, live_ref, m_sc, l_sc, acc_sc, s, tok):
    kv_heads = q3.shape[0]
    width = kv_heads * HEAD_SIZE
    scale = HEAD_SIZE ** (-0.5)
    lo, n = s * NEIGH * tok, NEIGH * tok
    live = live_ref[:, lo:lo + n] > 0
    for h in range(kv_heads):
        kh = kvbuf[lo:lo + n, h * HEAD_SIZE:(h + 1) * HEAD_SIZE]
        sc = lax.dot_general(q3[h], kh, (((1,), (1,)), ((), ())), preferred_element_type=jnp.float32)
        sc = jnp.where(live, sc * scale, -1e30)
        m_old = m_sc[h]
        m_new = jnp.maximum(m_old, jnp.max(sc, axis=1, keepdims=True))
        p = jnp.where(live, jnp.exp(sc - m_new), 0.0)
        fade = jnp.exp(m_old - m_new)
        l_sc[h] = l_sc[h] * fade + jnp.sum(p, axis=1, keepdims=True)
        vh = kvbuf[lo:lo + n, width + h * HEAD_SIZE:width + (h + 1) * HEAD_SIZE]
        acc_sc[h] = acc_sc[h] * fade + jnp.dot(p.astype(jnp.bfloat16), vh, preferred_element_type=jnp.float32)
        m_sc[h] = m_new


def attend_finish(rowok_ref, l_sc, acc_sc, o_ref, groups, tok):
    kv_heads = acc_sc.shape[0]
    rowok = jnp.concatenate([rowok_ref[...]] * groups, axis=0) > 0
    for h in range(kv_heads):
        res = jnp.where(rowok, acc_sc[h] / l_sc[h], 0.0).astype(o_ref.dtype)
        for g in range(groups):
            col = (h * groups + g) * HEAD_SIZE
            o_ref[:, col:col + HEAD_SIZE] = res[g * tok:(g + 1) * tok]


def window_kernel(spans, rows, cols, q_hbm, kv_ref, live_ref, rowok_ref, o_ref,
                  q_ref, kvbuf, q3, m_sc, l_sc, acc_sc,
                  send_sem, recv_sem, lift_sem, local_sem):
    tok = kv_ref.shape[0]
    c = lax.axis_index("span")
    i = lax.axis_index("ty")
    j = lax.axis_index("tx")
    mesh_id = pl.DeviceIdType.MESH
    lifted = cols >= 4
    half = cols // 2
    is_a = j == half - 1
    is_b = j == half

    def inside(d):
        dy, dx = OFFSETS[d]
        y, x = i + dy, j + dx
        return (y >= 0) & (y < rows) & (x >= 0) & (x < cols)

    def slot(s, o):
        return kvbuf.at[pl.ds((s * NEIGH + o) * tok, tok), :]

    def crossing(d):
        if not lifted or d not in (3, 4):
            return None
        return is_a if d == 4 else is_b

    n_nb = sum(inside(d).astype(jnp.int32) for d in range(1, NEIGH))

    barrier = pltpu.get_barrier_semaphore()
    def greet(target):
        pl.semaphore_signal(barrier, 1, device_id=target, device_id_type=mesh_id)
    for s in range(spans):
        @pl.when(s != c)
        def _():
            greet((s, i, j))
    for d in range(1, NEIGH):
        dy, dx = OFFSETS[d]
        @pl.when(inside(d))
        def _():
            greet((c, i + dy, j + dx))
    pl.semaphore_wait(barrier, spans - 1 + n_nb)

    def up_copy(s):
        return pltpu.make_async_remote_copy(
            src_ref=kv_ref, dst_ref=slot(c, 0), send_sem=send_sem.at[s], recv_sem=recv_sem.at[c * NEIGH],
            device_id=(s, i, j), device_id_type=mesh_id)

    def side_copy(s, d, src):
        dy, dx = OFFSETS[d]
        return pltpu.make_async_remote_copy(
            src_ref=src, dst_ref=slot(s, INVERSE[d]),
            send_sem=send_sem.at[spans + s * (NEIGH - 1) + d - 1],
            recv_sem=recv_sem.at[s * NEIGH + INVERSE[d]],
            device_id=(c, i + dy, j + dx), device_id_type=mesh_id)

    def lift_copy(s, o):
        return pltpu.make_async_remote_copy(
            src_ref=slot(c, o), dst_ref=slot(c, o), send_sem=lift_sem.at[s],
            recv_sem=recv_sem.at[c * NEIGH + o],
            device_id=(s, i, j), device_id_type=mesh_id)

    def send_side(s, d, src, wait=False, own=False):
        cross = crossing(d)
        go = inside(d) if (cross is None or own) else inside(d) & jnp.logical_not(cross)
        @pl.when(go)
        def _():
            cp = side_copy(s, d, src)
            cp.wait_send() if wait else cp.start()

    q_load = pltpu.make_async_copy(q_hbm, q_ref, local_sem.at[1])
    q_load.start()

    for s in range(spans):
        @pl.when(s > c)
        def _():
            up_copy(s).start()

    for s in range(spans):
        @pl.when(s == c)
        def _():
            for d in range(1, NEIGH):
                send_side(s, d, kv_ref, own=True)

    own = pltpu.make_async_copy(kv_ref, slot(0, 0), local_sem.at[0])
    for s in range(spans):
        @pl.when(s == c)
        def _():
            pltpu.make_async_copy(kv_ref, slot(s, 0), local_sem.at[0]).start()

    if lifted:
        for o, end in ((4, is_a), (3, is_b)):
            dy, dx = OFFSETS[o]
            @pl.when(end)
            def _():
                for s in range(spans):
                    @pl.when(s == c)
                    def _():
                        pltpu.make_async_remote_copy(
                            src_ref=kv_ref, dst_ref=slot(s, o), send_sem=send_sem.at[0],
                            recv_sem=recv_sem.at[s * NEIGH + o],
                            device_id=(c, i + dy, j + dx), device_id_type=mesh_id).wait_recv()
                for s in range(spans):
                    @pl.when(s > c)
                    def _():
                        lift_copy(s, o).start()

    zeros = jnp.zeros((tok, kv_ref.shape[1]), kv_ref.dtype)
    for s in range(spans):
        @pl.when(s <= c)
        def _():
            for d in range(1, NEIGH):
                @pl.when(jnp.logical_not(inside(INVERSE[d])))
                def _():
                    slot(s, INVERSE[d])[...] = zeros

    def ring_gap(a, b):
        return min((a - b) % spans, (b - a) % spans)

    for cc in range(spans):
        @pl.when(c == cc)
        def _():
            for s in sorted(range(cc), key=lambda s: (ring_gap(s, cc), -s)):
                pltpu.make_async_remote_copy(
                    src_ref=kv_ref, dst_ref=slot(s, 0), send_sem=send_sem.at[s], recv_sem=recv_sem.at[s * NEIGH],
                    device_id=(s, i, j), device_id_type=mesh_id).wait_recv()
                for d in range(1, NEIGH):
                    send_side(s, d, slot(s, 0))

    for s in range(spans):
        @pl.when(s > c)
        def _():
            up_copy(s).wait_send()
    own.wait()
    q_load.wait()

    kv_heads = q3.shape[0]
    groups = q_ref.shape[1] // (kv_heads * HEAD_SIZE)
    load_queries(q_ref, q3, kv_heads, groups)
    m_sc[...] = jnp.full(m_sc.shape, -1e30, jnp.float32)
    l_sc[...] = jnp.zeros(l_sc.shape, jnp.float32)
    acc_sc[...] = jnp.zeros(acc_sc.shape, jnp.float32)

    for cc in range(spans):
        @pl.when(c == cc)
        def _():
            order = [cc] + sorted(range(cc), key=lambda s: (ring_gap(s, cc), -s))
            for s in order:
                for o in range(1, NEIGH):
                    dy, dx = OFFSETS[o]
                    done = inside(o)
                    if lifted and s == cc and o in (3, 4):
                        done = done & jnp.logical_not(is_a if o == 4 else is_b)
                    @pl.when(done)
                    def _():
                        pltpu.make_async_remote_copy(
                            src_ref=kv_ref, dst_ref=slot(s, o), send_sem=send_sem.at[0],
                            recv_sem=recv_sem.at[s * NEIGH + o],
                            device_id=(c, i + dy, j + dx), device_id_type=mesh_id).wait_recv()
                attend_chunk(q3, kvbuf, live_ref, m_sc, l_sc, acc_sc, s, tok)

    for cc in range(spans):
        @pl.when(c == cc)
        def _():
            for s in range(cc + 1):
                for d in range(1, NEIGH):
                    send_side(s, d, kv_ref, wait=True, own=(s == cc))
            if lifted:
                for o, end in ((4, is_a), (3, is_b)):
                    @pl.when(end)
                    def _():
                        for s in range(cc + 1, spans):
                            lift_copy(s, o).wait_send()

    attend_finish(rowok_ref, l_sc, acc_sc, o_ref, groups, tok)


def window_attend(q, kv, live, rowok, spans, rows, cols):
    tok, qw = q.shape
    kw = kv.shape[1]
    keys = spans * NEIGH * tok
    flops = 2 * 2 * tok * qw * keys
    kernel = lambda *refs: window_kernel(spans, rows, cols, *refs)
    return pl.pallas_call(
        kernel,
        out_shape=jax.ShapeDtypeStruct((tok, qw), q.dtype),
        in_specs=[pl.BlockSpec(memory_space=pl.ANY)] * 2 + [pl.BlockSpec(memory_space=pltpu.VMEM)] * 2,
        out_specs=pl.BlockSpec(memory_space=pltpu.VMEM),
        scratch_shapes=[
            pltpu.VMEM((tok, qw), q.dtype),
            pltpu.VMEM((keys, kw), kv.dtype),
            pltpu.VMEM((kw // (2 * HEAD_SIZE), qw // (kw // 2) * tok, HEAD_SIZE), q.dtype),
            pltpu.VMEM((kw // (2 * HEAD_SIZE), qw // (kw // 2) * tok, 1), jnp.float32),
            pltpu.VMEM((kw // (2 * HEAD_SIZE), qw // (kw // 2) * tok, 1), jnp.float32),
            pltpu.VMEM((kw // (2 * HEAD_SIZE), qw // (kw // 2) * tok, HEAD_SIZE), jnp.float32),
            pltpu.SemaphoreType.DMA((spans + spans * (NEIGH - 1),)),
            pltpu.SemaphoreType.DMA((spans * NEIGH,)),
            pltpu.SemaphoreType.DMA((spans,)),
            pltpu.SemaphoreType.DMA((2,)),
        ],
        compiler_params=pltpu.CompilerParams(
            vmem_limit_bytes=67043328, collective_id=0, has_side_effects=True),
        cost_estimate=pl.CostEstimate(
            flops=flops, transcendentals=tok * qw // HEAD_SIZE * keys,
            bytes_accessed=2 * (2 * tok * qw + keys * kw)),
    )(q, kv, live, rowok)


def shards(queries, key_value, pattern, counts, span_mask):
    tok_rows = queries.shape[3]
    spans, rows, cols = counts.shape
    my_span = lax.axis_index("span")
    my_row = lax.axis_index("ty")
    my_col = lax.axis_index("tx")
    zero_index = jnp.asarray(0).astype(jnp.int32)
    padded_counts = jnp.pad(counts, ((0, 0), (1, 1), (1, 1)))
    window = lax.dynamic_slice(padded_counts, (zero_index, my_row, my_col), (spans, 3, 3))
    near_counts = cross_tiles(window)
    own_count = lax.dynamic_index_in_dim(window[:, 1, 1], my_span, 0, keepdims=False)
    allowed = pattern.reshape(NEIGH) > 0
    span_row = lax.dynamic_index_in_dim(span_mask, my_span, 0, keepdims=False) > 0
    row_ids = jnp.arange(tok_rows, dtype=jnp.int32)
    live = (
        (row_ids[None, None, :] < near_counts[:, :, None])
        & allowed[None, :, None]
        & span_row[:, None, None]
    ).reshape(1, -1).astype(jnp.float32)
    rowok = (row_ids < own_count).astype(jnp.float32).reshape(tok_rows, 1)
    out = window_attend(
        queries.reshape(tok_rows, -1), key_value.reshape(tok_rows, -1), live, rowok, spans, rows, cols)
    return out.reshape(1, 1, 1, tok_rows, -1)


def solution(mesh):
    return jax.shard_map(
        shards,
        mesh=mesh,
        in_specs=(
            P("span", "ty", "tx", None, None),
            P("span", "ty", "tx", None, None),
            P("span", "ty", "tx", None),
            P(),
            P(),
        ),
        out_specs=P("span", "ty", "tx", None, None),
        check_vma=False,
    )
```

```python
import jax
import jax.numpy as jnp
from jax import lax
from jax.experimental import pallas as pl
from jax.experimental.pallas import tpu as pltpu
from jax.sharding import PartitionSpec as P

HEAD_SIZE = 128
NEIGH = 5
OFFSETS = ((0, 0), (-1, 0), (1, 0), (0, -1), (0, 1))
INVERSE = (0, 2, 1, 4, 3)


def cross_tiles(extended):
    return jnp.stack(
        [
            extended[:, 1, 1],
            extended[:, 0, 1],
            extended[:, 2, 1],
            extended[:, 1, 0],
            extended[:, 1, 2],
        ],
        axis=1,
    )


def load_queries(q_ref, q3, kv_heads, groups):
    for h in range(kv_heads):
        q3[h] = jnp.concatenate(
            [q_ref[:, (h * groups + g) * HEAD_SIZE:(h * groups + g + 1) * HEAD_SIZE] for g in range(groups)],
            axis=0,
        )


def attend_chunk(q3, kvbuf, limits, m_sc, l_sc, acc_sc, s, tok):
    kv_heads = q3.shape[0]
    width = kv_heads * HEAD_SIZE
    scale = HEAD_SIZE ** (-0.5)
    lo, n = s * NEIGH * tok, NEIGH * tok
    lane = lax.broadcasted_iota(jnp.int32, (1, n), 1)
    block = lane // tok
    limit = jnp.full((1, n), limits[NEIGH - 1], jnp.int32)
    for o in range(NEIGH - 2, -1, -1):
        limit = jnp.where(block == o, limits[o], limit)
    live = (lane % tok) < limit
    for h in range(kv_heads):
        kh = kvbuf[lo:lo + n, h * HEAD_SIZE:(h + 1) * HEAD_SIZE]
        sc = lax.dot_general(q3[h], kh, (((1,), (1,)), ((), ())), preferred_element_type=jnp.float32)
        sc = jnp.where(live, sc * scale, -1e30)
        m_old = m_sc[h]
        m_new = jnp.maximum(m_old, jnp.max(sc, axis=1, keepdims=True))
        p = jnp.where(live, jnp.exp(sc - m_new), 0.0)
        fade = jnp.exp(m_old - m_new)
        l_sc[h] = l_sc[h] * fade + jnp.sum(p, axis=1, keepdims=True)
        vh = kvbuf[lo:lo + n, width + h * HEAD_SIZE:width + (h + 1) * HEAD_SIZE]
        acc_sc[h] = acc_sc[h] * fade + jnp.dot(p.astype(jnp.bfloat16), vh, preferred_element_type=jnp.float32)
        m_sc[h] = m_new


def attend_finish(own_count, l_sc, acc_sc, o_ref, groups, tok):
    kv_heads = acc_sc.shape[0]
    rowok = (lax.broadcasted_iota(jnp.int32, (groups * tok, 1), 0) % tok) < own_count
    for h in range(kv_heads):
        res = jnp.where(rowok, acc_sc[h] / l_sc[h], 0.0).astype(o_ref.dtype)
        for g in range(groups):
            col = (h * groups + g) * HEAD_SIZE
            o_ref[:, col:col + HEAD_SIZE] = res[g * tok:(g + 1) * tok]


def window_kernel(spans, rows, cols, q_hbm, kv_ref, counts_ref, pattern_ref, mask_ref, o_ref,
                  q_ref, kvbuf, q3, m_sc, l_sc, acc_sc,
                  send_sem, recv_sem, lift_sem, local_sem):
    tok = kv_ref.shape[0]
    c = lax.axis_index("span")
    i = lax.axis_index("ty")
    j = lax.axis_index("tx")
    mesh_id = pl.DeviceIdType.MESH
    lifted = cols >= 4
    half = cols // 2
    is_a = j == half - 1
    is_b = j == half

    def inside(d):
        dy, dx = OFFSETS[d]
        y, x = i + dy, j + dx
        return (y >= 0) & (y < rows) & (x >= 0) & (x < cols)

    def slot(s, o):
        return kvbuf.at[pl.ds((s * NEIGH + o) * tok, tok), :]

    def crossing(d):
        if not lifted or d not in (3, 4):
            return None
        return is_a if d == 4 else is_b

    n_nb = sum(inside(d).astype(jnp.int32) for d in range(1, NEIGH))

    def window_limits(s):
        reads = mask_ref[c, s] > 0
        limits = []
        for o in range(NEIGH):
            dy, dx = OFFSETS[o]
            y = jnp.minimum(jnp.maximum(i + dy, 0), rows - 1)
            x = jnp.minimum(jnp.maximum(j + dx, 0), cols - 1)
            ok = inside(o) & reads & (pattern_ref[0, 0, 0, o] > 0)
            limits.append(jnp.where(ok, counts_ref[s, y, x], 0))
        return limits

    barrier = pltpu.get_barrier_semaphore()
    def greet(target):
        pl.semaphore_signal(barrier, 1, device_id=target, device_id_type=mesh_id)
    for s in range(spans):
        @pl.when(s != c)
        def _():
            greet((s, i, j))
    for d in range(1, NEIGH):
        dy, dx = OFFSETS[d]
        @pl.when(inside(d))
        def _():
            greet((c, i + dy, j + dx))
    pl.semaphore_wait(barrier, spans - 1 + n_nb)

    def up_copy(s):
        return pltpu.make_async_remote_copy(
            src_ref=kv_ref, dst_ref=slot(c, 0), send_sem=send_sem.at[s], recv_sem=recv_sem.at[c * NEIGH],
            device_id=(s, i, j), device_id_type=mesh_id)

    def side_copy(s, d, src):
        dy, dx = OFFSETS[d]
        return pltpu.make_async_remote_copy(
            src_ref=src, dst_ref=slot(s, INVERSE[d]),
            send_sem=send_sem.at[spans + s * (NEIGH - 1) + d - 1],
            recv_sem=recv_sem.at[s * NEIGH + INVERSE[d]],
            device_id=(c, i + dy, j + dx), device_id_type=mesh_id)

    def lift_copy(s, o):
        return pltpu.make_async_remote_copy(
            src_ref=slot(c, o), dst_ref=slot(c, o), send_sem=lift_sem.at[s],
            recv_sem=recv_sem.at[c * NEIGH + o],
            device_id=(s, i, j), device_id_type=mesh_id)

    def send_side(s, d, src, wait=False, own=False):
        cross = crossing(d)
        go = inside(d) if (cross is None or own) else inside(d) & jnp.logical_not(cross)
        @pl.when(go)
        def _():
            cp = side_copy(s, d, src)
            cp.wait_send() if wait else cp.start()

    q_load = pltpu.make_async_copy(q_hbm, q_ref, local_sem.at[1])
    q_load.start()

    for s in range(spans):
        @pl.when(s > c)
        def _():
            up_copy(s).start()

    for s in range(spans):
        @pl.when(s == c)
        def _():
            for d in range(1, NEIGH):
                send_side(s, d, kv_ref, own=True)

    own = pltpu.make_async_copy(kv_ref, slot(0, 0), local_sem.at[0])
    for s in range(spans):
        @pl.when(s == c)
        def _():
            pltpu.make_async_copy(kv_ref, slot(s, 0), local_sem.at[0]).start()

    if lifted:
        for o, end in ((4, is_a), (3, is_b)):
            dy, dx = OFFSETS[o]
            @pl.when(end)
            def _():
                for s in range(spans):
                    @pl.when(s == c)
                    def _():
                        pltpu.make_async_remote_copy(
                            src_ref=kv_ref, dst_ref=slot(s, o), send_sem=send_sem.at[0],
                            recv_sem=recv_sem.at[s * NEIGH + o],
                            device_id=(c, i + dy, j + dx), device_id_type=mesh_id).wait_recv()
                for s in range(spans):
                    @pl.when(s > c)
                    def _():
                        lift_copy(s, o).start()

    zeros = jnp.zeros((tok, kv_ref.shape[1]), kv_ref.dtype)
    for s in range(spans):
        @pl.when(s <= c)
        def _():
            for d in range(1, NEIGH):
                @pl.when(jnp.logical_not(inside(INVERSE[d])))
                def _():
                    slot(s, INVERSE[d])[...] = zeros

    def ring_gap(a, b):
        return min((a - b) % spans, (b - a) % spans)

    for cc in range(spans):
        @pl.when(c == cc)
        def _():
            for s in sorted(range(cc), key=lambda s: (ring_gap(s, cc), -s)):
                pltpu.make_async_remote_copy(
                    src_ref=kv_ref, dst_ref=slot(s, 0), send_sem=send_sem.at[s], recv_sem=recv_sem.at[s * NEIGH],
                    device_id=(s, i, j), device_id_type=mesh_id).wait_recv()
                for d in range(1, NEIGH):
                    send_side(s, d, slot(s, 0))

    for s in range(spans):
        @pl.when(s > c)
        def _():
            up_copy(s).wait_send()
    own.wait()
    q_load.wait()

    kv_heads = q3.shape[0]
    groups = q_ref.shape[1] // (kv_heads * HEAD_SIZE)
    load_queries(q_ref, q3, kv_heads, groups)
    m_sc[...] = jnp.full(m_sc.shape, -1e30, jnp.float32)
    l_sc[...] = jnp.zeros(l_sc.shape, jnp.float32)
    acc_sc[...] = jnp.zeros(acc_sc.shape, jnp.float32)

    for cc in range(spans):
        @pl.when(c == cc)
        def _():
            order = [cc] + sorted(range(cc), key=lambda s: (ring_gap(s, cc), -s))
            for s in order:
                for o in range(1, NEIGH):
                    dy, dx = OFFSETS[o]
                    done = inside(o)
                    if lifted and s == cc and o in (3, 4):
                        done = done & jnp.logical_not(is_a if o == 4 else is_b)
                    @pl.when(done)
                    def _():
                        pltpu.make_async_remote_copy(
                            src_ref=kv_ref, dst_ref=slot(s, o), send_sem=send_sem.at[0],
                            recv_sem=recv_sem.at[s * NEIGH + o],
                            device_id=(c, i + dy, j + dx), device_id_type=mesh_id).wait_recv()
                attend_chunk(q3, kvbuf, window_limits(s), m_sc, l_sc, acc_sc, s, tok)

    for cc in range(spans):
        @pl.when(c == cc)
        def _():
            for s in range(cc + 1):
                for d in range(1, NEIGH):
                    send_side(s, d, kv_ref, wait=True, own=(s == cc))
            if lifted:
                for o, end in ((4, is_a), (3, is_b)):
                    @pl.when(end)
                    def _():
                        for s in range(cc + 1, spans):
                            lift_copy(s, o).wait_send()

    attend_finish(counts_ref[c, i, j], l_sc, acc_sc, o_ref, groups, tok)


def window_attend(q, kv, pattern, counts, span_mask):
    tok, qw = q.shape
    kw = kv.shape[1]
    spans, rows, cols = counts.shape
    keys = spans * NEIGH * tok
    flops = 2 * 2 * tok * qw * keys
    kernel = lambda *refs: window_kernel(spans, rows, cols, *refs)
    return pl.pallas_call(
        kernel,
        out_shape=jax.ShapeDtypeStruct((tok, qw), q.dtype),
        in_specs=[pl.BlockSpec(memory_space=pl.ANY)] * 2 + [pl.BlockSpec(memory_space=pltpu.SMEM)] * 3,
        out_specs=pl.BlockSpec(memory_space=pltpu.VMEM),
        scratch_shapes=[
            pltpu.VMEM((tok, qw), q.dtype),
            pltpu.VMEM((keys, kw), kv.dtype),
            pltpu.VMEM((kw // (2 * HEAD_SIZE), qw // (kw // 2) * tok, HEAD_SIZE), q.dtype),
            pltpu.VMEM((kw // (2 * HEAD_SIZE), qw // (kw // 2) * tok, 1), jnp.float32),
            pltpu.VMEM((kw // (2 * HEAD_SIZE), qw // (kw // 2) * tok, 1), jnp.float32),
            pltpu.VMEM((kw // (2 * HEAD_SIZE), qw // (kw // 2) * tok, HEAD_SIZE), jnp.float32),
            pltpu.SemaphoreType.DMA((spans + spans * (NEIGH - 1),)),
            pltpu.SemaphoreType.DMA((spans * NEIGH,)),
            pltpu.SemaphoreType.DMA((spans,)),
            pltpu.SemaphoreType.DMA((2,)),
        ],
        compiler_params=pltpu.CompilerParams(
            vmem_limit_bytes=67043328, collective_id=0, has_side_effects=True),
        cost_estimate=pl.CostEstimate(
            flops=flops, transcendentals=tok * qw // HEAD_SIZE * keys,
            bytes_accessed=2 * (2 * tok * qw + keys * kw)),
    )(q, kv, counts, pattern, span_mask)


def shards(queries, key_value, pattern, counts, span_mask):
    tok_rows = queries.shape[3]
    out = window_attend(
        queries.reshape(tok_rows, -1), key_value.reshape(tok_rows, -1), pattern, counts, span_mask)
    return out.reshape(1, 1, 1, tok_rows, -1)


def solution(mesh):
    return jax.shard_map(
        shards,
        mesh=mesh,
        in_specs=(
            P("span", "ty", "tx", None, None),
            P("span", "ty", "tx", None, None),
            P("span", "ty", "tx", None),
            P(),
            P(),
        ),
        out_specs=P("span", "ty", "tx", None, None),
        check_vma=False,
    )
```

```python
import jax
import jax.numpy as jnp
from jax import lax
from jax.experimental import pallas as pl
from jax.experimental.pallas import tpu as pltpu
from jax.sharding import PartitionSpec as P

HEAD_SIZE = 128
NEIGH = 5
OFFSETS = ((0, 0), (-1, 0), (1, 0), (0, -1), (0, 1))
INVERSE = (0, 2, 1, 4, 3)


def cross_tiles(extended):
    return jnp.stack(
        [
            extended[:, 1, 1],
            extended[:, 0, 1],
            extended[:, 2, 1],
            extended[:, 1, 0],
            extended[:, 1, 2],
        ],
        axis=1,
    )


def load_queries(q_ref, q3, kv_heads, groups):
    for h in range(kv_heads):
        q3[h] = jnp.concatenate(
            [q_ref[:, (h * groups + g) * HEAD_SIZE:(h * groups + g + 1) * HEAD_SIZE] for g in range(groups)],
            axis=0,
        )


def attend_chunk(q3, kvbuf, limits, m_sc, l_sc, acc_sc, s, tok):
    kv_heads = q3.shape[0]
    width = kv_heads * HEAD_SIZE
    scale = HEAD_SIZE ** (-0.5)
    lo, n = s * NEIGH * tok, NEIGH * tok
    lane = lax.broadcasted_iota(jnp.int32, (1, n), 1)
    block = lane // tok
    limit = jnp.full((1, n), limits[NEIGH - 1], jnp.int32)
    for o in range(NEIGH - 2, -1, -1):
        limit = jnp.where(block == o, limits[o], limit)
    live = (lane % tok) < limit
    for h in range(kv_heads):
        kh = kvbuf[lo:lo + n, h * HEAD_SIZE:(h + 1) * HEAD_SIZE]
        sc = lax.dot_general(q3[h], kh, (((1,), (1,)), ((), ())), preferred_element_type=jnp.float32)
        sc = jnp.where(live, sc * scale, -1e30)
        m_old = m_sc[h]
        m_new = jnp.maximum(m_old, jnp.max(sc, axis=1, keepdims=True))
        p = jnp.where(live, jnp.exp(sc - m_new), 0.0)
        fade = jnp.exp(m_old - m_new)
        l_sc[h] = l_sc[h] * fade + jnp.sum(p, axis=1, keepdims=True)
        vh = kvbuf[lo:lo + n, width + h * HEAD_SIZE:width + (h + 1) * HEAD_SIZE]
        acc_sc[h] = acc_sc[h] * fade + jnp.dot(p.astype(jnp.bfloat16), vh, preferred_element_type=jnp.float32)
        m_sc[h] = m_new


def attend_finish(own_count, l_sc, acc_sc, o_ref, groups, tok):
    kv_heads = acc_sc.shape[0]
    rowok = (lax.broadcasted_iota(jnp.int32, (groups * tok, 1), 0) % tok) < own_count
    for h in range(kv_heads):
        res = jnp.where(rowok, acc_sc[h] / l_sc[h], 0.0).astype(o_ref.dtype)
        for g in range(groups):
            col = (h * groups + g) * HEAD_SIZE
            o_ref[:, col:col + HEAD_SIZE] = res[g * tok:(g + 1) * tok]


def window_kernel(spans, rows, cols, q_hbm, kv_ref, counts_ref, pattern_ref, mask_ref, o_hbm,
                  q_ref, o_ref, kvbuf, q3, m_sc, l_sc, acc_sc,
                  send_sem, recv_sem, lift_sem, local_sem):
    tok = kv_ref.shape[0]
    c = lax.axis_index("span")
    i = lax.axis_index("ty")
    j = lax.axis_index("tx")
    mesh_id = pl.DeviceIdType.MESH
    lifted = cols >= 4
    half = cols // 2
    is_a = j == half - 1
    is_b = j == half

    def inside(d):
        dy, dx = OFFSETS[d]
        y, x = i + dy, j + dx
        return (y >= 0) & (y < rows) & (x >= 0) & (x < cols)

    def slot(s, o):
        return kvbuf.at[pl.ds((s * NEIGH + o) * tok, tok), :]

    def crossing(d):
        if not lifted or d not in (3, 4):
            return None
        return is_a if d == 4 else is_b

    n_nb = sum(inside(d).astype(jnp.int32) for d in range(1, NEIGH))

    def window_limits(s):
        reads = mask_ref[c, s] > 0
        limits = []
        for o in range(NEIGH):
            dy, dx = OFFSETS[o]
            y = jnp.minimum(jnp.maximum(i + dy, 0), rows - 1)
            x = jnp.minimum(jnp.maximum(j + dx, 0), cols - 1)
            ok = inside(o) & reads & (pattern_ref[0, 0, 0, o] > 0)
            limits.append(jnp.where(ok, counts_ref[s, y, x], 0))
        return limits

    barrier = pltpu.get_barrier_semaphore()
    def greet(target):
        pl.semaphore_signal(barrier, 1, device_id=target, device_id_type=mesh_id)
    for s in range(spans):
        @pl.when(s != c)
        def _():
            greet((s, i, j))
    for d in range(1, NEIGH):
        dy, dx = OFFSETS[d]
        @pl.when(inside(d))
        def _():
            greet((c, i + dy, j + dx))
    pl.semaphore_wait(barrier, spans - 1 + n_nb)

    def up_copy(s):
        return pltpu.make_async_remote_copy(
            src_ref=kv_ref, dst_ref=slot(c, 0), send_sem=send_sem.at[s], recv_sem=recv_sem.at[c * NEIGH],
            device_id=(s, i, j), device_id_type=mesh_id)

    def side_copy(s, d, src):
        dy, dx = OFFSETS[d]
        return pltpu.make_async_remote_copy(
            src_ref=src, dst_ref=slot(s, INVERSE[d]),
            send_sem=send_sem.at[spans + s * (NEIGH - 1) + d - 1],
            recv_sem=recv_sem.at[s * NEIGH + INVERSE[d]],
            device_id=(c, i + dy, j + dx), device_id_type=mesh_id)

    def lift_copy(s, o):
        return pltpu.make_async_remote_copy(
            src_ref=slot(c, o), dst_ref=slot(c, o), send_sem=lift_sem.at[s],
            recv_sem=recv_sem.at[c * NEIGH + o],
            device_id=(s, i, j), device_id_type=mesh_id)

    def send_side(s, d, src, wait=False, own=False):
        cross = crossing(d)
        go = inside(d) if (cross is None or own) else inside(d) & jnp.logical_not(cross)
        @pl.when(go)
        def _():
            cp = side_copy(s, d, src)
            cp.wait_send() if wait else cp.start()

    q_load = pltpu.make_async_copy(q_hbm, q_ref, local_sem.at[1])
    q_load.start()

    for s in range(spans):
        @pl.when(s > c)
        def _():
            up_copy(s).start()

    for s in range(spans):
        @pl.when(s == c)
        def _():
            for d in range(1, NEIGH):
                send_side(s, d, kv_ref, own=True)

    own = pltpu.make_async_copy(kv_ref, slot(0, 0), local_sem.at[0])
    for s in range(spans):
        @pl.when(s == c)
        def _():
            pltpu.make_async_copy(kv_ref, slot(s, 0), local_sem.at[0]).start()

    if lifted:
        for o, end in ((4, is_a), (3, is_b)):
            dy, dx = OFFSETS[o]
            @pl.when(end)
            def _():
                for s in range(spans):
                    @pl.when(s == c)
                    def _():
                        pltpu.make_async_remote_copy(
                            src_ref=kv_ref, dst_ref=slot(s, o), send_sem=send_sem.at[0],
                            recv_sem=recv_sem.at[s * NEIGH + o],
                            device_id=(c, i + dy, j + dx), device_id_type=mesh_id).wait_recv()
                for s in range(spans):
                    @pl.when(s > c)
                    def _():
                        lift_copy(s, o).start()

    zeros = jnp.zeros((tok, kv_ref.shape[1]), kv_ref.dtype)
    for s in range(spans):
        @pl.when(s <= c)
        def _():
            for d in range(1, NEIGH):
                @pl.when(jnp.logical_not(inside(INVERSE[d])))
                def _():
                    slot(s, INVERSE[d])[...] = zeros

    def ring_gap(a, b):
        return min((a - b) % spans, (b - a) % spans)

    for cc in range(spans):
        @pl.when(c == cc)
        def _():
            for s in sorted(range(cc), key=lambda s: (ring_gap(s, cc), -s)):
                pltpu.make_async_remote_copy(
                    src_ref=kv_ref, dst_ref=slot(s, 0), send_sem=send_sem.at[s], recv_sem=recv_sem.at[s * NEIGH],
                    device_id=(s, i, j), device_id_type=mesh_id).wait_recv()
                for d in range(1, NEIGH):
                    send_side(s, d, slot(s, 0))

    for s in range(spans):
        @pl.when(s > c)
        def _():
            up_copy(s).wait_send()
    own.wait()
    q_load.wait()

    kv_heads = q3.shape[0]
    groups = q_ref.shape[1] // (kv_heads * HEAD_SIZE)
    load_queries(q_ref, q3, kv_heads, groups)
    m_sc[...] = jnp.full(m_sc.shape, -1e30, jnp.float32)
    l_sc[...] = jnp.zeros(l_sc.shape, jnp.float32)
    acc_sc[...] = jnp.zeros(acc_sc.shape, jnp.float32)

    for cc in range(spans):
        @pl.when(c == cc)
        def _():
            order = [cc] + sorted(range(cc), key=lambda s: (ring_gap(s, cc), -s))
            for s in order:
                for o in range(1, NEIGH):
                    dy, dx = OFFSETS[o]
                    done = inside(o)
                    if lifted and s == cc and o in (3, 4):
                        done = done & jnp.logical_not(is_a if o == 4 else is_b)
                    @pl.when(done)
                    def _():
                        pltpu.make_async_remote_copy(
                            src_ref=kv_ref, dst_ref=slot(s, o), send_sem=send_sem.at[0],
                            recv_sem=recv_sem.at[s * NEIGH + o],
                            device_id=(c, i + dy, j + dx), device_id_type=mesh_id).wait_recv()
                attend_chunk(q3, kvbuf, window_limits(s), m_sc, l_sc, acc_sc, s, tok)

    for cc in range(spans):
        @pl.when(c == cc)
        def _():
            for s in range(cc + 1):
                for d in range(1, NEIGH):
                    send_side(s, d, kv_ref, wait=True, own=(s == cc))
            if lifted:
                for o, end in ((4, is_a), (3, is_b)):
                    @pl.when(end)
                    def _():
                        for s in range(cc + 1, spans):
                            lift_copy(s, o).wait_send()

    attend_finish(counts_ref[c, i, j], l_sc, acc_sc, o_ref, groups, tok)
    store = pltpu.make_async_copy(o_ref, o_hbm, local_sem.at[1])
    store.start()
    store.wait()


def window_attend(q, kv, pattern, counts, span_mask):
    tok, qw = q.shape
    kw = kv.shape[1]
    spans, rows, cols = counts.shape
    keys = spans * NEIGH * tok
    flops = 2 * 2 * tok * qw * keys
    kernel = lambda *refs: window_kernel(spans, rows, cols, *refs)
    return pl.pallas_call(
        kernel,
        out_shape=jax.ShapeDtypeStruct((tok, qw), q.dtype),
        in_specs=[pl.BlockSpec(memory_space=pl.ANY)] * 2 + [pl.BlockSpec(memory_space=pltpu.SMEM)] * 3,
        out_specs=pl.BlockSpec(memory_space=pl.ANY),
        scratch_shapes=[
            pltpu.VMEM((tok, qw), q.dtype),
            pltpu.VMEM((tok, qw), q.dtype),
            pltpu.VMEM((keys, kw), kv.dtype),
            pltpu.VMEM((kw // (2 * HEAD_SIZE), qw // (kw // 2) * tok, HEAD_SIZE), q.dtype),
            pltpu.VMEM((kw // (2 * HEAD_SIZE), qw // (kw // 2) * tok, 1), jnp.float32),
            pltpu.VMEM((kw // (2 * HEAD_SIZE), qw // (kw // 2) * tok, 1), jnp.float32),
            pltpu.VMEM((kw // (2 * HEAD_SIZE), qw // (kw // 2) * tok, HEAD_SIZE), jnp.float32),
            pltpu.SemaphoreType.DMA((spans + spans * (NEIGH - 1),)),
            pltpu.SemaphoreType.DMA((spans * NEIGH,)),
            pltpu.SemaphoreType.DMA((spans,)),
            pltpu.SemaphoreType.DMA((2,)),
        ],
        compiler_params=pltpu.CompilerParams(
            vmem_limit_bytes=67043328, collective_id=0, has_side_effects=True),
        cost_estimate=pl.CostEstimate(
            flops=flops, transcendentals=tok * qw // HEAD_SIZE * keys,
            bytes_accessed=2 * (2 * tok * qw + keys * kw)),
    )(q, kv, counts, pattern, span_mask)


def shards(queries, key_value, pattern, counts, span_mask):
    tok_rows = queries.shape[3]
    out = window_attend(
        queries.reshape(tok_rows, -1), key_value.reshape(tok_rows, -1), pattern, counts, span_mask)
    return out.reshape(1, 1, 1, tok_rows, -1)


def solution(mesh):
    return jax.shard_map(
        shards,
        mesh=mesh,
        in_specs=(
            P("span", "ty", "tx", None, None),
            P("span", "ty", "tx", None, None),
            P("span", "ty", "tx", None),
            P(),
            P(),
        ),
        out_specs=P("span", "ty", "tx", None, None),
        check_vma=False,
    )
```

```python
import jax
import jax.numpy as jnp
from jax import lax
from jax.experimental import pallas as pl
from jax.experimental.pallas import tpu as pltpu
from jax.sharding import PartitionSpec as P

HEAD_SIZE = 128
NEIGH = 5
OFFSETS = ((0, 0), (-1, 0), (1, 0), (0, -1), (0, 1))
INVERSE = (0, 2, 1, 4, 3)


def cross_tiles(extended):
    return jnp.stack(
        [
            extended[:, 1, 1],
            extended[:, 0, 1],
            extended[:, 2, 1],
            extended[:, 1, 0],
            extended[:, 1, 2],
        ],
        axis=1,
    )


def load_queries(q_ref, q3, kv_heads, groups):
    for h in range(kv_heads):
        q3[h] = jnp.concatenate(
            [q_ref[:, (h * groups + g) * HEAD_SIZE:(h * groups + g + 1) * HEAD_SIZE] for g in range(groups)],
            axis=0,
        )


def attend_chunk(q3, kvbuf, limits, m_sc, l_sc, acc_sc, lo, tok):
    kv_heads = q3.shape[0]
    width = kv_heads * HEAD_SIZE
    scale = HEAD_SIZE ** (-0.5)
    n = len(limits) * tok
    lane = lax.broadcasted_iota(jnp.int32, (1, n), 1)
    block = lane // tok
    limit = jnp.full((1, n), limits[-1], jnp.int32)
    for o in range(len(limits) - 2, -1, -1):
        limit = jnp.where(block == o, limits[o], limit)
    live = (lane % tok) < limit

    def head(h, carry):
        kc = pl.multiple_of(h * HEAD_SIZE, HEAD_SIZE)
        vc = pl.multiple_of(width + h * HEAD_SIZE, HEAD_SIZE)
        kh = kvbuf[pl.ds(lo, n), pl.ds(kc, HEAD_SIZE)]
        sc = lax.dot_general(q3[h], kh, (((1,), (1,)), ((), ())), preferred_element_type=jnp.float32)
        sc = jnp.where(live, sc * scale, -1e30)
        m_old = m_sc[h]
        m_new = jnp.maximum(m_old, jnp.max(sc, axis=1, keepdims=True))
        p = jnp.where(live, jnp.exp(sc - m_new), 0.0)
        fade = jnp.exp(m_old - m_new)
        l_sc[h] = l_sc[h] * fade + jnp.sum(p, axis=1, keepdims=True)
        vh = kvbuf[pl.ds(lo, n), pl.ds(vc, HEAD_SIZE)]
        acc_sc[h] = acc_sc[h] * fade + jnp.dot(p.astype(jnp.bfloat16), vh, preferred_element_type=jnp.float32)
        m_sc[h] = m_new
        return carry

    lax.fori_loop(0, kv_heads, head, 0)


def attend_finish(own_count, l_sc, acc_sc, o_ref, groups, tok):
    kv_heads = acc_sc.shape[0]
    rowok = (lax.broadcasted_iota(jnp.int32, (groups * tok, 1), 0) % tok) < own_count
    for h in range(kv_heads):
        res = jnp.where(rowok, acc_sc[h] / l_sc[h], 0.0).astype(o_ref.dtype)
        for g in range(groups):
            col = (h * groups + g) * HEAD_SIZE
            o_ref[:, col:col + HEAD_SIZE] = res[g * tok:(g + 1) * tok]


def window_kernel(spans, rows, cols, q_hbm, kv_ref, counts_ref, pattern_ref, mask_ref, o_hbm,
                  q_ref, o_ref, kvbuf, q3, m_sc, l_sc, acc_sc,
                  send_sem, recv_sem, lift_sem, local_sem):
    tok = kv_ref.shape[0]
    c = lax.axis_index("span")
    i = lax.axis_index("ty")
    j = lax.axis_index("tx")
    mesh_id = pl.DeviceIdType.MESH
    lifted = cols >= 4
    half = cols // 2
    is_a = j == half - 1
    is_b = j == half

    def inside(d):
        dy, dx = OFFSETS[d]
        y, x = i + dy, j + dx
        return (y >= 0) & (y < rows) & (x >= 0) & (x < cols)

    def slot(s, o):
        return kvbuf.at[pl.ds((s * NEIGH + o) * tok, tok), :]

    def crossing(d):
        if not lifted or d not in (3, 4):
            return None
        return is_a if d == 4 else is_b

    n_nb = sum(inside(d).astype(jnp.int32) for d in range(1, NEIGH))

    def window_limits(s):
        reads = mask_ref[c, s] > 0
        limits = []
        for o in range(NEIGH):
            dy, dx = OFFSETS[o]
            y = jnp.minimum(jnp.maximum(i + dy, 0), rows - 1)
            x = jnp.minimum(jnp.maximum(j + dx, 0), cols - 1)
            ok = inside(o) & reads & (pattern_ref[0, 0, 0, o] > 0)
            limits.append(jnp.where(ok, counts_ref[s, y, x], 0))
        return limits

    barrier = pltpu.get_barrier_semaphore()
    def greet(target):
        pl.semaphore_signal(barrier, 1, device_id=target, device_id_type=mesh_id)
    for s in range(spans):
        @pl.when(s != c)
        def _():
            greet((s, i, j))
    for d in range(1, NEIGH):
        dy, dx = OFFSETS[d]
        @pl.when(inside(d))
        def _():
            greet((c, i + dy, j + dx))
    pl.semaphore_wait(barrier, spans - 1 + n_nb)

    def up_copy(s):
        return pltpu.make_async_remote_copy(
            src_ref=kv_ref, dst_ref=slot(c, 0), send_sem=send_sem.at[s], recv_sem=recv_sem.at[c * NEIGH],
            device_id=(s, i, j), device_id_type=mesh_id)

    def side_copy(s, d, src):
        dy, dx = OFFSETS[d]
        return pltpu.make_async_remote_copy(
            src_ref=src, dst_ref=slot(s, INVERSE[d]),
            send_sem=send_sem.at[spans + s * (NEIGH - 1) + d - 1],
            recv_sem=recv_sem.at[s * NEIGH + INVERSE[d]],
            device_id=(c, i + dy, j + dx), device_id_type=mesh_id)

    def lift_copy(s, o):
        return pltpu.make_async_remote_copy(
            src_ref=slot(c, o), dst_ref=slot(c, o), send_sem=lift_sem.at[s],
            recv_sem=recv_sem.at[c * NEIGH + o],
            device_id=(s, i, j), device_id_type=mesh_id)

    def send_side(s, d, src, wait=False, own=False):
        cross = crossing(d)
        go = inside(d) if (cross is None or own) else inside(d) & jnp.logical_not(cross)
        @pl.when(go)
        def _():
            cp = side_copy(s, d, src)
            cp.wait_send() if wait else cp.start()

    q_load = pltpu.make_async_copy(q_hbm, q_ref, local_sem.at[1])
    q_load.start()

    for s in range(spans):
        @pl.when(s > c)
        def _():
            up_copy(s).start()

    for s in range(spans):
        @pl.when(s == c)
        def _():
            for d in range(1, NEIGH):
                send_side(s, d, kv_ref, own=True)

    own = pltpu.make_async_copy(kv_ref, slot(0, 0), local_sem.at[0])
    for s in range(spans):
        @pl.when(s == c)
        def _():
            pltpu.make_async_copy(kv_ref, slot(s, 0), local_sem.at[0]).start()

    if lifted:
        for o, end in ((4, is_a), (3, is_b)):
            dy, dx = OFFSETS[o]
            @pl.when(end)
            def _():
                for s in range(spans):
                    @pl.when(s == c)
                    def _():
                        pltpu.make_async_remote_copy(
                            src_ref=kv_ref, dst_ref=slot(s, o), send_sem=send_sem.at[0],
                            recv_sem=recv_sem.at[s * NEIGH + o],
                            device_id=(c, i + dy, j + dx), device_id_type=mesh_id).wait_recv()
                for s in range(spans):
                    @pl.when(s > c)
                    def _():
                        lift_copy(s, o).start()

    zeros = jnp.zeros((tok, kv_ref.shape[1]), kv_ref.dtype)
    for s in range(spans):
        @pl.when(s <= c)
        def _():
            for d in range(1, NEIGH):
                @pl.when(jnp.logical_not(inside(INVERSE[d])))
                def _():
                    slot(s, INVERSE[d])[...] = zeros

    def ring_gap(a, b):
        return min((a - b) % spans, (b - a) % spans)

    for cc in range(spans):
        @pl.when(c == cc)
        def _():
            for s in sorted(range(cc), key=lambda s: (ring_gap(s, cc), -s)):
                pltpu.make_async_remote_copy(
                    src_ref=kv_ref, dst_ref=slot(s, 0), send_sem=send_sem.at[s], recv_sem=recv_sem.at[s * NEIGH],
                    device_id=(s, i, j), device_id_type=mesh_id).wait_recv()
                for d in range(1, NEIGH):
                    send_side(s, d, slot(s, 0))

    for s in range(spans):
        @pl.when(s > c)
        def _():
            up_copy(s).wait_send()
    own.wait()
    q_load.wait()

    kv_heads = q3.shape[0]
    groups = q_ref.shape[1] // (kv_heads * HEAD_SIZE)
    load_queries(q_ref, q3, kv_heads, groups)
    m_sc[...] = jnp.full(m_sc.shape, -1e30, jnp.float32)
    l_sc[...] = jnp.zeros(l_sc.shape, jnp.float32)
    acc_sc[...] = jnp.zeros(acc_sc.shape, jnp.float32)

    for cc in range(spans):
        @pl.when(c == cc)
        def _():
            order = [cc] + sorted(range(cc), key=lambda s: (ring_gap(s, cc), -s))
            for s in order[:-1] if cc > 0 else []:
                for o in range(1, NEIGH):
                    dy, dx = OFFSETS[o]
                    done = inside(o)
                    if lifted and s == cc and o in (3, 4):
                        done = done & jnp.logical_not(is_a if o == 4 else is_b)
                    @pl.when(done)
                    def _():
                        pltpu.make_async_remote_copy(
                            src_ref=kv_ref, dst_ref=slot(s, o), send_sem=send_sem.at[0],
                            recv_sem=recv_sem.at[s * NEIGH + o],
                            device_id=(c, i + dy, j + dx), device_id_type=mesh_id).wait_recv()
                attend_chunk(q3, kvbuf, window_limits(s), m_sc, l_sc, acc_sc, s * NEIGH * tok, tok)
            s = order[-1]
            limits = window_limits(s)
            attend_chunk(q3, kvbuf, limits[:1], m_sc, l_sc, acc_sc, s * NEIGH * tok, tok)
            for o in range(1, NEIGH):
                dy, dx = OFFSETS[o]
                done = inside(o)
                if lifted and s == cc and o in (3, 4):
                    done = done & jnp.logical_not(is_a if o == 4 else is_b)
                @pl.when(done)
                def _():
                    pltpu.make_async_remote_copy(
                        src_ref=kv_ref, dst_ref=slot(s, o), send_sem=send_sem.at[0],
                        recv_sem=recv_sem.at[s * NEIGH + o],
                        device_id=(c, i + dy, j + dx), device_id_type=mesh_id).wait_recv()
                @pl.when(inside(o))
                def _():
                    attend_chunk(q3, kvbuf, limits[o:o + 1], m_sc, l_sc, acc_sc, (s * NEIGH + o) * tok, tok)

    for cc in range(spans):
        @pl.when(c == cc)
        def _():
            for s in range(cc + 1):
                for d in range(1, NEIGH):
                    send_side(s, d, kv_ref, wait=True, own=(s == cc))
            if lifted:
                for o, end in ((4, is_a), (3, is_b)):
                    @pl.when(end)
                    def _():
                        for s in range(cc + 1, spans):
                            lift_copy(s, o).wait_send()

    attend_finish(counts_ref[c, i, j], l_sc, acc_sc, o_ref, groups, tok)
    store = pltpu.make_async_copy(o_ref, o_hbm, local_sem.at[1])
    store.start()
    store.wait()


def window_attend(q, kv, pattern, counts, span_mask):
    tok, qw = q.shape
    kw = kv.shape[1]
    spans, rows, cols = counts.shape
    keys = spans * NEIGH * tok
    flops = 2 * 2 * tok * qw * keys
    kernel = lambda *refs: window_kernel(spans, rows, cols, *refs)
    return pl.pallas_call(
        kernel,
        out_shape=jax.ShapeDtypeStruct((tok, qw), q.dtype),
        in_specs=[pl.BlockSpec(memory_space=pl.ANY)] * 2 + [pl.BlockSpec(memory_space=pltpu.SMEM)] * 3,
        out_specs=pl.BlockSpec(memory_space=pl.ANY),
        scratch_shapes=[
            pltpu.VMEM((tok, qw), q.dtype),
            pltpu.VMEM((tok, qw), q.dtype),
            pltpu.VMEM((keys, kw), kv.dtype),
            pltpu.VMEM((kw // (2 * HEAD_SIZE), qw // (kw // 2) * tok, HEAD_SIZE), q.dtype),
            pltpu.VMEM((kw // (2 * HEAD_SIZE), qw // (kw // 2) * tok, 1), jnp.float32),
            pltpu.VMEM((kw // (2 * HEAD_SIZE), qw // (kw // 2) * tok, 1), jnp.float32),
            pltpu.VMEM((kw // (2 * HEAD_SIZE), qw // (kw // 2) * tok, HEAD_SIZE), jnp.float32),
            pltpu.SemaphoreType.DMA((spans + spans * (NEIGH - 1),)),
            pltpu.SemaphoreType.DMA((spans * NEIGH,)),
            pltpu.SemaphoreType.DMA((spans,)),
            pltpu.SemaphoreType.DMA((2,)),
        ],
        compiler_params=pltpu.CompilerParams(
            vmem_limit_bytes=67043328, collective_id=0, has_side_effects=True),
        cost_estimate=pl.CostEstimate(
            flops=flops, transcendentals=tok * qw // HEAD_SIZE * keys,
            bytes_accessed=2 * (2 * tok * qw + keys * kw)),
    )(q, kv, counts, pattern, span_mask)


def shards(queries, key_value, pattern, counts, span_mask):
    tok_rows = queries.shape[3]
    out = window_attend(
        queries.reshape(tok_rows, -1), key_value.reshape(tok_rows, -1), pattern, counts, span_mask)
    return out.reshape(1, 1, 1, tok_rows, -1)


def solution(mesh):
    return jax.shard_map(
        shards,
        mesh=mesh,
        in_specs=(
            P("span", "ty", "tx", None, None),
            P("span", "ty", "tx", None, None),
            P("span", "ty", "tx", None),
            P(),
            P(),
        ),
        out_specs=P("span", "ty", "tx", None, None),
        check_vma=False,
    )
```

```python
import jax
import jax.numpy as jnp
from jax import lax
from jax.experimental import pallas as pl
from jax.experimental.pallas import tpu as pltpu
from jax.sharding import PartitionSpec as P

HEAD_SIZE = 128
NEIGH = 5
OFFSETS = ((0, 0), (-1, 0), (1, 0), (0, -1), (0, 1))
INVERSE = (0, 2, 1, 4, 3)


def cross_tiles(extended):
    return jnp.stack(
        [
            extended[:, 1, 1],
            extended[:, 0, 1],
            extended[:, 2, 1],
            extended[:, 1, 0],
            extended[:, 1, 2],
        ],
        axis=1,
    )


def load_queries(q_ref, q3, kv_heads, groups):
    for h in range(kv_heads):
        q3[h] = jnp.concatenate(
            [q_ref[:, (h * groups + g) * HEAD_SIZE:(h * groups + g + 1) * HEAD_SIZE] for g in range(groups)],
            axis=0,
        )


def attend_chunk(q3, kvbuf, limits, m_sc, l_sc, acc_sc, lo, tok):
    kv_heads = q3.shape[0]
    width = kv_heads * HEAD_SIZE
    scale = HEAD_SIZE ** (-0.5)
    n = len(limits) * tok
    lane = lax.broadcasted_iota(jnp.int32, (1, n), 1)
    block = lane // tok
    limit = jnp.full((1, n), limits[-1], jnp.int32)
    for o in range(len(limits) - 2, -1, -1):
        limit = jnp.where(block == o, limits[o], limit)
    live = (lane % tok) < limit
    for h in range(kv_heads):
        kh = kvbuf[lo:lo + n, h * HEAD_SIZE:(h + 1) * HEAD_SIZE]
        sc = lax.dot_general(q3[h], kh, (((1,), (1,)), ((), ())), preferred_element_type=jnp.float32)
        sc = jnp.where(live, sc * scale, -1e30)
        m_old = m_sc[h]
        m_new = jnp.maximum(m_old, jnp.max(sc, axis=1, keepdims=True))
        p = jnp.where(live, jnp.exp(sc - m_new), 0.0)
        fade = jnp.exp(m_old - m_new)
        l_sc[h] = l_sc[h] * fade + jnp.sum(p, axis=1, keepdims=True)
        vh = kvbuf[lo:lo + n, width + h * HEAD_SIZE:width + (h + 1) * HEAD_SIZE]
        acc_sc[h] = acc_sc[h] * fade + jnp.dot(p.astype(jnp.bfloat16), vh, preferred_element_type=jnp.float32)
        m_sc[h] = m_new


def attend_finish(own_count, l_sc, acc_sc, o_ref, groups, tok):
    kv_heads = acc_sc.shape[0]
    rowok = (lax.broadcasted_iota(jnp.int32, (groups * tok, 1), 0) % tok) < own_count
    for h in range(kv_heads):
        res = jnp.where(rowok, acc_sc[h] / l_sc[h], 0.0).astype(o_ref.dtype)
        for g in range(groups):
            col = (h * groups + g) * HEAD_SIZE
            o_ref[:, col:col + HEAD_SIZE] = res[g * tok:(g + 1) * tok]


def window_kernel(spans, rows, cols, q_hbm, kv_ref, counts_ref, pattern_ref, mask_ref, o_hbm,
                  q_ref, o_ref, kvbuf, q3, m_sc, l_sc, acc_sc,
                  send_sem, recv_sem, lift_sem, local_sem):
    tok = kv_ref.shape[0]
    c = lax.axis_index("span")
    i = lax.axis_index("ty")
    j = lax.axis_index("tx")
    mesh_id = pl.DeviceIdType.MESH
    lifted = cols >= 4
    half = cols // 2
    is_a = j == half - 1
    is_b = j == half

    def inside(d):
        dy, dx = OFFSETS[d]
        y, x = i + dy, j + dx
        return (y >= 0) & (y < rows) & (x >= 0) & (x < cols)

    def slot(s, o):
        return kvbuf.at[pl.ds((s * NEIGH + o) * tok, tok), :]

    def crossing(d):
        if not lifted or d not in (3, 4):
            return None
        return is_a if d == 4 else is_b

    n_nb = sum(inside(d).astype(jnp.int32) for d in range(1, NEIGH))

    def window_limits(s):
        reads = mask_ref[c, s] > 0
        limits = []
        for o in range(NEIGH):
            dy, dx = OFFSETS[o]
            y = jnp.minimum(jnp.maximum(i + dy, 0), rows - 1)
            x = jnp.minimum(jnp.maximum(j + dx, 0), cols - 1)
            ok = inside(o) & reads & (pattern_ref[0, 0, 0, o] > 0)
            limits.append(jnp.where(ok, counts_ref[s, y, x], 0))
        return limits

    barrier = pltpu.get_barrier_semaphore()
    def greet(target):
        pl.semaphore_signal(barrier, 1, device_id=target, device_id_type=mesh_id)
    for s in range(spans):
        @pl.when(s != c)
        def _():
            greet((s, i, j))
    for d in range(1, NEIGH):
        dy, dx = OFFSETS[d]
        @pl.when(inside(d))
        def _():
            greet((c, i + dy, j + dx))
    pl.semaphore_wait(barrier, spans - 1 + n_nb)

    def up_copy(s):
        return pltpu.make_async_remote_copy(
            src_ref=kv_ref, dst_ref=slot(c, 0), send_sem=send_sem.at[s], recv_sem=recv_sem.at[c * NEIGH],
            device_id=(s, i, j), device_id_type=mesh_id)

    def side_copy(s, d, src):
        dy, dx = OFFSETS[d]
        return pltpu.make_async_remote_copy(
            src_ref=src, dst_ref=slot(s, INVERSE[d]),
            send_sem=send_sem.at[spans + s * (NEIGH - 1) + d - 1],
            recv_sem=recv_sem.at[s * NEIGH + INVERSE[d]],
            device_id=(c, i + dy, j + dx), device_id_type=mesh_id)

    def lift_copy(s, o):
        return pltpu.make_async_remote_copy(
            src_ref=slot(c, o), dst_ref=slot(c, o), send_sem=lift_sem.at[s],
            recv_sem=recv_sem.at[c * NEIGH + o],
            device_id=(s, i, j), device_id_type=mesh_id)

    def send_side(s, d, src, wait=False, own=False):
        cross = crossing(d)
        go = inside(d) if (cross is None or own) else inside(d) & jnp.logical_not(cross)
        @pl.when(go)
        def _():
            cp = side_copy(s, d, src)
            cp.wait_send() if wait else cp.start()

    q_load = pltpu.make_async_copy(q_hbm, q_ref, local_sem.at[1])
    q_load.start()

    for s in range(spans):
        @pl.when(s > c)
        def _():
            up_copy(s).start()

    for s in range(spans):
        @pl.when(s == c)
        def _():
            for d in range(1, NEIGH):
                send_side(s, d, kv_ref, own=True)

    own = pltpu.make_async_copy(kv_ref, slot(0, 0), local_sem.at[0])
    for s in range(spans):
        @pl.when(s == c)
        def _():
            pltpu.make_async_copy(kv_ref, slot(s, 0), local_sem.at[0]).start()

    if lifted:
        for o, end in ((4, is_a), (3, is_b)):
            dy, dx = OFFSETS[o]
            @pl.when(end)
            def _():
                for s in range(spans):
                    @pl.when(s == c)
                    def _():
                        pltpu.make_async_remote_copy(
                            src_ref=kv_ref, dst_ref=slot(s, o), send_sem=send_sem.at[0],
                            recv_sem=recv_sem.at[s * NEIGH + o],
                            device_id=(c, i + dy, j + dx), device_id_type=mesh_id).wait_recv()
                for s in range(spans):
                    @pl.when(s > c)
                    def _():
                        lift_copy(s, o).start()

    zeros = jnp.zeros((tok, kv_ref.shape[1]), kv_ref.dtype)
    for s in range(spans):
        @pl.when(s <= c)
        def _():
            for d in range(1, NEIGH):
                @pl.when(jnp.logical_not(inside(INVERSE[d])))
                def _():
                    slot(s, INVERSE[d])[...] = zeros

    def ring_gap(a, b):
        return min((a - b) % spans, (b - a) % spans)

    for cc in range(spans):
        @pl.when(c == cc)
        def _():
            for s in sorted(range(cc), key=lambda s: (ring_gap(s, cc), -s)):
                pltpu.make_async_remote_copy(
                    src_ref=kv_ref, dst_ref=slot(s, 0), send_sem=send_sem.at[s], recv_sem=recv_sem.at[s * NEIGH],
                    device_id=(s, i, j), device_id_type=mesh_id).wait_recv()
                for d in range(1, NEIGH):
                    send_side(s, d, slot(s, 0))

    for s in range(spans):
        @pl.when(s > c)
        def _():
            up_copy(s).wait_send()
    own.wait()
    q_load.wait()

    kv_heads = q3.shape[0]
    groups = q_ref.shape[1] // (kv_heads * HEAD_SIZE)
    load_queries(q_ref, q3, kv_heads, groups)
    m_sc[...] = jnp.full(m_sc.shape, -1e30, jnp.float32)
    l_sc[...] = jnp.zeros(l_sc.shape, jnp.float32)
    acc_sc[...] = jnp.zeros(acc_sc.shape, jnp.float32)

    for cc in range(spans):
        @pl.when(c == cc)
        def _():
            order = [cc] + sorted(range(cc), key=lambda s: (ring_gap(s, cc), -s))
            split = cc == spans - 1 and cc > 0
            for s in order[:-1] if split else order:
                for o in range(1, NEIGH):
                    dy, dx = OFFSETS[o]
                    done = inside(o)
                    if lifted and s == cc and o in (3, 4):
                        done = done & jnp.logical_not(is_a if o == 4 else is_b)
                    @pl.when(done)
                    def _():
                        pltpu.make_async_remote_copy(
                            src_ref=kv_ref, dst_ref=slot(s, o), send_sem=send_sem.at[0],
                            recv_sem=recv_sem.at[s * NEIGH + o],
                            device_id=(c, i + dy, j + dx), device_id_type=mesh_id).wait_recv()
                attend_chunk(q3, kvbuf, window_limits(s), m_sc, l_sc, acc_sc, s * NEIGH * tok, tok)
            if split:
                s = order[-1]
                limits = window_limits(s)
                attend_chunk(q3, kvbuf, limits[:1], m_sc, l_sc, acc_sc, s * NEIGH * tok, tok)
                for o in range(1, NEIGH):
                    dy, dx = OFFSETS[o]
                    @pl.when(inside(o))
                    def _():
                        pltpu.make_async_remote_copy(
                            src_ref=kv_ref, dst_ref=slot(s, o), send_sem=send_sem.at[0],
                            recv_sem=recv_sem.at[s * NEIGH + o],
                            device_id=(c, i + dy, j + dx), device_id_type=mesh_id).wait_recv()
                        attend_chunk(q3, kvbuf, limits[o:o + 1], m_sc, l_sc, acc_sc, (s * NEIGH + o) * tok, tok)

    for cc in range(spans):
        @pl.when(c == cc)
        def _():
            for s in range(cc + 1):
                for d in range(1, NEIGH):
                    send_side(s, d, kv_ref, wait=True, own=(s == cc))
            if lifted:
                for o, end in ((4, is_a), (3, is_b)):
                    @pl.when(end)
                    def _():
                        for s in range(cc + 1, spans):
                            lift_copy(s, o).wait_send()

    attend_finish(counts_ref[c, i, j], l_sc, acc_sc, o_ref, groups, tok)
    store = pltpu.make_async_copy(o_ref, o_hbm, local_sem.at[1])
    store.start()
    store.wait()


def window_attend(q, kv, pattern, counts, span_mask):
    tok, qw = q.shape
    kw = kv.shape[1]
    spans, rows, cols = counts.shape
    keys = spans * NEIGH * tok
    flops = 2 * 2 * tok * qw * keys
    kernel = lambda *refs: window_kernel(spans, rows, cols, *refs)
    return pl.pallas_call(
        kernel,
        out_shape=jax.ShapeDtypeStruct((tok, qw), q.dtype),
        in_specs=[pl.BlockSpec(memory_space=pl.ANY)] * 2 + [pl.BlockSpec(memory_space=pltpu.SMEM)] * 3,
        out_specs=pl.BlockSpec(memory_space=pl.ANY),
        scratch_shapes=[
            pltpu.VMEM((tok, qw), q.dtype),
            pltpu.VMEM((tok, qw), q.dtype),
            pltpu.VMEM((keys, kw), kv.dtype),
            pltpu.VMEM((kw // (2 * HEAD_SIZE), qw // (kw // 2) * tok, HEAD_SIZE), q.dtype),
            pltpu.VMEM((kw // (2 * HEAD_SIZE), qw // (kw // 2) * tok, 1), jnp.float32),
            pltpu.VMEM((kw // (2 * HEAD_SIZE), qw // (kw // 2) * tok, 1), jnp.float32),
            pltpu.VMEM((kw // (2 * HEAD_SIZE), qw // (kw // 2) * tok, HEAD_SIZE), jnp.float32),
            pltpu.SemaphoreType.DMA((spans + spans * (NEIGH - 1),)),
            pltpu.SemaphoreType.DMA((spans * NEIGH,)),
            pltpu.SemaphoreType.DMA((spans,)),
            pltpu.SemaphoreType.DMA((2,)),
        ],
        compiler_params=pltpu.CompilerParams(
            vmem_limit_bytes=67043328, collective_id=0, has_side_effects=True),
        cost_estimate=pl.CostEstimate(
            flops=flops, transcendentals=tok * qw // HEAD_SIZE * keys,
            bytes_accessed=2 * (2 * tok * qw + keys * kw)),
    )(q, kv, counts, pattern, span_mask)


def shards(queries, key_value, pattern, counts, span_mask):
    tok_rows = queries.shape[3]
    out = window_attend(
        queries.reshape(tok_rows, -1), key_value.reshape(tok_rows, -1), pattern, counts, span_mask)
    return out.reshape(1, 1, 1, tok_rows, -1)


def solution(mesh):
    return jax.shard_map(
        shards,
        mesh=mesh,
        in_specs=(
            P("span", "ty", "tx", None, None),
            P("span", "ty", "tx", None, None),
            P("span", "ty", "tx", None),
            P(),
            P(),
        ),
        out_specs=P("span", "ty", "tx", None, None),
        check_vma=False,
    )
```

```python
import jax
import jax.numpy as jnp
from jax import lax
from jax.experimental import pallas as pl
from jax.experimental.pallas import tpu as pltpu
from jax.sharding import PartitionSpec as P

HEAD_SIZE = 128
NEIGH = 5
OFFSETS = ((0, 0), (-1, 0), (1, 0), (0, -1), (0, 1))
INVERSE = (0, 2, 1, 4, 3)


def cross_tiles(extended):
    return jnp.stack(
        [
            extended[:, 1, 1],
            extended[:, 0, 1],
            extended[:, 2, 1],
            extended[:, 1, 0],
            extended[:, 1, 2],
        ],
        axis=1,
    )


def load_queries(q_ref, q3, kv_heads, groups):
    for h in range(kv_heads):
        q3[h] = jnp.concatenate(
            [q_ref[:, (h * groups + g) * HEAD_SIZE:(h * groups + g + 1) * HEAD_SIZE] for g in range(groups)],
            axis=0,
        )


def attend_chunk(q3, kvbuf, limits, m_sc, l_sc, acc_sc, s, tok):
    kv_heads = q3.shape[0]
    width = kv_heads * HEAD_SIZE
    scale = HEAD_SIZE ** (-0.5)
    lo, n = s * NEIGH * tok, NEIGH * tok
    lane = lax.broadcasted_iota(jnp.int32, (1, n), 1)
    block = lane // tok
    limit = jnp.full((1, n), limits[NEIGH - 1], jnp.int32)
    for o in range(NEIGH - 2, -1, -1):
        limit = jnp.where(block == o, limits[o], limit)
    live = (lane % tok) < limit
    for h in range(kv_heads):
        kh = kvbuf[lo:lo + n, h * HEAD_SIZE:(h + 1) * HEAD_SIZE]
        sc = lax.dot_general(q3[h], kh, (((1,), (1,)), ((), ())), preferred_element_type=jnp.float32)
        sc = jnp.where(live, sc * scale, -1e30)
        m_old = m_sc[h]
        m_new = jnp.maximum(m_old, jnp.max(sc, axis=1, keepdims=True))
        p = jnp.where(live, jnp.exp(sc - m_new), 0.0)
        fade = jnp.exp(m_old - m_new)
        l_sc[h] = l_sc[h] * fade + jnp.sum(p, axis=1, keepdims=True)
        vh = kvbuf[lo:lo + n, width + h * HEAD_SIZE:width + (h + 1) * HEAD_SIZE]
        acc_sc[h] = acc_sc[h] * fade + jnp.dot(p.astype(jnp.bfloat16), vh, preferred_element_type=jnp.float32)
        m_sc[h] = m_new


def attend_finish(own_count, l_sc, acc_sc, o_ref, groups, tok):
    kv_heads = acc_sc.shape[0]
    rowok = (lax.broadcasted_iota(jnp.int32, (groups * tok, 1), 0) % tok) < own_count
    for h in range(kv_heads):
        res = jnp.where(rowok, acc_sc[h] / l_sc[h], 0.0).astype(o_ref.dtype)
        for g in range(groups):
            col = (h * groups + g) * HEAD_SIZE
            o_ref[:, col:col + HEAD_SIZE] = res[g * tok:(g + 1) * tok]


def window_kernel(spans, rows, cols, q_hbm, kv_ref, counts_ref, pattern_ref, mask_ref, o_hbm,
                  q_ref, o_ref, kvbuf, q3, m_sc, l_sc, acc_sc,
                  send_sem, recv_sem, lift_sem, local_sem):
    tok = kv_ref.shape[0]
    c = lax.axis_index("span")
    i = lax.axis_index("ty")
    j = lax.axis_index("tx")
    mesh_id = pl.DeviceIdType.MESH
    lifted = cols >= 4
    half = cols // 2
    is_a = j == half - 1
    is_b = j == half

    def inside(d):
        dy, dx = OFFSETS[d]
        y, x = i + dy, j + dx
        return (y >= 0) & (y < rows) & (x >= 0) & (x < cols)

    def slot(s, o):
        return kvbuf.at[pl.ds((s * NEIGH + o) * tok, tok), :]

    def crossing(d):
        if not lifted or d not in (3, 4):
            return None
        return is_a if d == 4 else is_b

    n_nb = sum(inside(d).astype(jnp.int32) for d in range(1, NEIGH))

    def window_limits(s):
        reads = mask_ref[c, s] > 0
        limits = []
        for o in range(NEIGH):
            dy, dx = OFFSETS[o]
            y = jnp.minimum(jnp.maximum(i + dy, 0), rows - 1)
            x = jnp.minimum(jnp.maximum(j + dx, 0), cols - 1)
            ok = inside(o) & reads & (pattern_ref[0, 0, 0, o] > 0)
            limits.append(jnp.where(ok, counts_ref[s, y, x], 0))
        return limits

    barrier = pltpu.get_barrier_semaphore()
    def greet(target):
        pl.semaphore_signal(barrier, 1, device_id=target, device_id_type=mesh_id)
    for s in range(spans):
        @pl.when(s != c)
        def _():
            greet((s, i, j))
    for d in range(1, NEIGH):
        dy, dx = OFFSETS[d]
        @pl.when(inside(d))
        def _():
            greet((c, i + dy, j + dx))
    pl.semaphore_wait(barrier, spans - 1 + n_nb)

    def up_copy(s):
        return pltpu.make_async_remote_copy(
            src_ref=kv_ref, dst_ref=slot(c, 0), send_sem=send_sem.at[s], recv_sem=recv_sem.at[c * NEIGH],
            device_id=(s, i, j), device_id_type=mesh_id)

    def side_copy(s, d, src):
        dy, dx = OFFSETS[d]
        return pltpu.make_async_remote_copy(
            src_ref=src, dst_ref=slot(s, INVERSE[d]),
            send_sem=send_sem.at[spans + s * (NEIGH - 1) + d - 1],
            recv_sem=recv_sem.at[s * NEIGH + INVERSE[d]],
            device_id=(c, i + dy, j + dx), device_id_type=mesh_id)

    def lift_copy(s, o):
        return pltpu.make_async_remote_copy(
            src_ref=slot(c, o), dst_ref=slot(c, o), send_sem=lift_sem.at[s],
            recv_sem=recv_sem.at[c * NEIGH + o],
            device_id=(s, i, j), device_id_type=mesh_id)

    def send_side(s, d, src, wait=False, own=False):
        cross = crossing(d)
        go = inside(d) if (cross is None or own) else inside(d) & jnp.logical_not(cross)
        @pl.when(go)
        def _():
            cp = side_copy(s, d, src)
            cp.wait_send() if wait else cp.start()

    q_load = pltpu.make_async_copy(q_hbm, q_ref, local_sem.at[1])
    q_load.start()

    for s in range(spans):
        @pl.when(s > c)
        def _():
            up_copy(s).start()

    for s in range(spans):
        @pl.when(s == c)
        def _():
            for d in range(1, NEIGH):
                send_side(s, d, kv_ref, own=True)

    own = pltpu.make_async_copy(kv_ref, slot(0, 0), local_sem.at[0])
    for s in range(spans):
        @pl.when(s == c)
        def _():
            pltpu.make_async_copy(kv_ref, slot(s, 0), local_sem.at[0]).start()

    if lifted:
        for o, end in ((4, is_a), (3, is_b)):
            dy, dx = OFFSETS[o]
            @pl.when(end)
            def _():
                for s in range(spans):
                    @pl.when(s == c)
                    def _():
                        pltpu.make_async_remote_copy(
                            src_ref=kv_ref, dst_ref=slot(s, o), send_sem=send_sem.at[0],
                            recv_sem=recv_sem.at[s * NEIGH + o],
                            device_id=(c, i + dy, j + dx), device_id_type=mesh_id).wait_recv()
                for s in range(spans):
                    @pl.when(s > c)
                    def _():
                        lift_copy(s, o).start()

    zeros = jnp.zeros((tok, kv_ref.shape[1]), kv_ref.dtype)
    for s in range(spans):
        @pl.when(s <= c)
        def _():
            for d in range(1, NEIGH):
                @pl.when(jnp.logical_not(inside(INVERSE[d])))
                def _():
                    slot(s, INVERSE[d])[...] = zeros

    def ring_gap(a, b):
        return min((a - b) % spans, (b - a) % spans)

    own.wait()
    q_load.wait()
    kv_heads = q3.shape[0]
    groups = q_ref.shape[1] // (kv_heads * HEAD_SIZE)
    load_queries(q_ref, q3, kv_heads, groups)
    m_sc[...] = jnp.full(m_sc.shape, -1e30, jnp.float32)
    l_sc[...] = jnp.zeros(l_sc.shape, jnp.float32)
    acc_sc[...] = jnp.zeros(acc_sc.shape, jnp.float32)

    def own_group(cc):
        s = cc
        for o in range(1, NEIGH):
            dy, dx = OFFSETS[o]
            done = inside(o)
            if lifted and o in (3, 4):
                done = done & jnp.logical_not(is_a if o == 4 else is_b)
            @pl.when(done)
            def _():
                pltpu.make_async_remote_copy(
                    src_ref=kv_ref, dst_ref=slot(s, o), send_sem=send_sem.at[0],
                    recv_sem=recv_sem.at[s * NEIGH + o],
                    device_id=(c, i + dy, j + dx), device_id_type=mesh_id).wait_recv()
        attend_chunk(q3, kvbuf, window_limits(s), m_sc, l_sc, acc_sc, s, tok)

    for cc in range(spans):
        @pl.when(c == cc)
        def _():
            for n, s in enumerate(sorted(range(cc), key=lambda s: (ring_gap(s, cc), -s))):
                if cc >= 2 and n == cc - 1:
                    own_group(cc)
                pltpu.make_async_remote_copy(
                    src_ref=kv_ref, dst_ref=slot(s, 0), send_sem=send_sem.at[s], recv_sem=recv_sem.at[s * NEIGH],
                    device_id=(s, i, j), device_id_type=mesh_id).wait_recv()
                for d in range(1, NEIGH):
                    send_side(s, d, slot(s, 0))

    for s in range(spans):
        @pl.when(s > c)
        def _():
            up_copy(s).wait_send()

    for cc in range(spans):
        @pl.when(c == cc)
        def _():
            order = [cc] + sorted(range(cc), key=lambda s: (ring_gap(s, cc), -s))
            for s in order[1:] if cc >= 2 else order:
                for o in range(1, NEIGH):
                    dy, dx = OFFSETS[o]
                    done = inside(o)
                    if lifted and s == cc and o in (3, 4):
                        done = done & jnp.logical_not(is_a if o == 4 else is_b)
                    @pl.when(done)
                    def _():
                        pltpu.make_async_remote_copy(
                            src_ref=kv_ref, dst_ref=slot(s, o), send_sem=send_sem.at[0],
                            recv_sem=recv_sem.at[s * NEIGH + o],
                            device_id=(c, i + dy, j + dx), device_id_type=mesh_id).wait_recv()
                attend_chunk(q3, kvbuf, window_limits(s), m_sc, l_sc, acc_sc, s, tok)

    for cc in range(spans):
        @pl.when(c == cc)
        def _():
            for s in range(cc + 1):
                for d in range(1, NEIGH):
                    send_side(s, d, kv_ref, wait=True, own=(s == cc))
            if lifted:
                for o, end in ((4, is_a), (3, is_b)):
                    @pl.when(end)
                    def _():
                        for s in range(cc + 1, spans):
                            lift_copy(s, o).wait_send()

    attend_finish(counts_ref[c, i, j], l_sc, acc_sc, o_ref, groups, tok)
    store = pltpu.make_async_copy(o_ref, o_hbm, local_sem.at[1])
    store.start()
    store.wait()


def window_attend(q, kv, pattern, counts, span_mask):
    tok, qw = q.shape
    kw = kv.shape[1]
    spans, rows, cols = counts.shape
    keys = spans * NEIGH * tok
    flops = 2 * 2 * tok * qw * keys
    kernel = lambda *refs: window_kernel(spans, rows, cols, *refs)
    return pl.pallas_call(
        kernel,
        out_shape=jax.ShapeDtypeStruct((tok, qw), q.dtype),
        in_specs=[pl.BlockSpec(memory_space=pl.ANY)] * 2 + [pl.BlockSpec(memory_space=pltpu.SMEM)] * 3,
        out_specs=pl.BlockSpec(memory_space=pl.ANY),
        scratch_shapes=[
            pltpu.VMEM((tok, qw), q.dtype),
            pltpu.VMEM((tok, qw), q.dtype),
            pltpu.VMEM((keys, kw), kv.dtype),
            pltpu.VMEM((kw // (2 * HEAD_SIZE), qw // (kw // 2) * tok, HEAD_SIZE), q.dtype),
            pltpu.VMEM((kw // (2 * HEAD_SIZE), qw // (kw // 2) * tok, 1), jnp.float32),
            pltpu.VMEM((kw // (2 * HEAD_SIZE), qw // (kw // 2) * tok, 1), jnp.float32),
            pltpu.VMEM((kw // (2 * HEAD_SIZE), qw // (kw // 2) * tok, HEAD_SIZE), jnp.float32),
            pltpu.SemaphoreType.DMA((spans + spans * (NEIGH - 1),)),
            pltpu.SemaphoreType.DMA((spans * NEIGH,)),
            pltpu.SemaphoreType.DMA((spans,)),
            pltpu.SemaphoreType.DMA((2,)),
        ],
        compiler_params=pltpu.CompilerParams(
            vmem_limit_bytes=67043328, collective_id=0, has_side_effects=True),
        cost_estimate=pl.CostEstimate(
            flops=flops, transcendentals=tok * qw // HEAD_SIZE * keys,
            bytes_accessed=2 * (2 * tok * qw + keys * kw)),
    )(q, kv, counts, pattern, span_mask)


def shards(queries, key_value, pattern, counts, span_mask):
    tok_rows = queries.shape[3]
    out = window_attend(
        queries.reshape(tok_rows, -1), key_value.reshape(tok_rows, -1), pattern, counts, span_mask)
    return out.reshape(1, 1, 1, tok_rows, -1)


def solution(mesh):
    return jax.shard_map(
        shards,
        mesh=mesh,
        in_specs=(
            P("span", "ty", "tx", None, None),
            P("span", "ty", "tx", None, None),
            P("span", "ty", "tx", None),
            P(),
            P(),
        ),
        out_specs=P("span", "ty", "tx", None, None),
        check_vma=False,
    )
```

```python
import jax
import jax.numpy as jnp
from jax import lax
from jax.experimental import pallas as pl
from jax.experimental.pallas import tpu as pltpu
from jax.sharding import PartitionSpec as P

HEAD_SIZE = 128
NEIGH = 5
OFFSETS = ((0, 0), (-1, 0), (1, 0), (0, -1), (0, 1))
INVERSE = (0, 2, 1, 4, 3)


def cross_tiles(extended):
    return jnp.stack(
        [
            extended[:, 1, 1],
            extended[:, 0, 1],
            extended[:, 2, 1],
            extended[:, 1, 0],
            extended[:, 1, 2],
        ],
        axis=1,
    )


def load_queries(q_ref, q3, kv_heads, groups):
    for h in range(kv_heads):
        q3[h] = jnp.concatenate(
            [q_ref[:, (h * groups + g) * HEAD_SIZE:(h * groups + g + 1) * HEAD_SIZE] for g in range(groups)],
            axis=0,
        )


def attend_chunk(q3, kvbuf, limits, m_sc, l_sc, acc_sc, s, tok):
    kv_heads = q3.shape[0]
    width = kv_heads * HEAD_SIZE
    scale = HEAD_SIZE ** (-0.5)
    lo, n = s * NEIGH * tok, NEIGH * tok
    lane = lax.broadcasted_iota(jnp.int32, (1, n), 1)
    block = lane // tok
    limit = jnp.full((1, n), limits[NEIGH - 1], jnp.int32)
    for o in range(NEIGH - 2, -1, -1):
        limit = jnp.where(block == o, limits[o], limit)
    live = (lane % tok) < limit
    for h in range(kv_heads):
        kh = kvbuf[lo:lo + n, h * HEAD_SIZE:(h + 1) * HEAD_SIZE]
        sc = lax.dot_general(q3[h], kh, (((1,), (1,)), ((), ())), preferred_element_type=jnp.float32)
        sc = jnp.where(live, sc * scale, -1e30)
        m_old = m_sc[h]
        m_new = jnp.maximum(m_old, jnp.max(sc, axis=1, keepdims=True))
        p = jnp.where(live, jnp.exp(sc - m_new), 0.0)
        fade = jnp.exp(m_old - m_new)
        l_sc[h] = l_sc[h] * fade + jnp.sum(p, axis=1, keepdims=True)
        vh = kvbuf[lo:lo + n, width + h * HEAD_SIZE:width + (h + 1) * HEAD_SIZE]
        acc_sc[h] = acc_sc[h] * fade + jnp.dot(p.astype(jnp.bfloat16), vh, preferred_element_type=jnp.float32)
        m_sc[h] = m_new


def attend_finish(own_count, l_sc, acc_sc, o_ref, groups, tok):
    kv_heads = acc_sc.shape[0]
    rowok = (lax.broadcasted_iota(jnp.int32, (groups * tok, 1), 0) % tok) < own_count
    for h in range(kv_heads):
        res = jnp.where(rowok, acc_sc[h] / l_sc[h], 0.0).astype(o_ref.dtype)
        for g in range(groups):
            col = (h * groups + g) * HEAD_SIZE
            o_ref[:, col:col + HEAD_SIZE] = res[g * tok:(g + 1) * tok]


def window_kernel(spans, rows, cols, q_hbm, kv_ref, counts_ref, pattern_ref, mask_ref, o_hbm,
                  q_ref, o_ref, kvbuf, q3, m_sc, l_sc, acc_sc,
                  send_sem, recv_sem, lift_sem, local_sem):
    tok = kv_ref.shape[0]
    c = lax.axis_index("span")
    i = lax.axis_index("ty")
    j = lax.axis_index("tx")
    mesh_id = pl.DeviceIdType.MESH
    lifted = cols >= 4
    half = cols // 2
    is_a = j == half - 1
    is_b = j == half

    def inside(d):
        dy, dx = OFFSETS[d]
        y, x = i + dy, j + dx
        return (y >= 0) & (y < rows) & (x >= 0) & (x < cols)

    def slot(s, o):
        return kvbuf.at[pl.ds((s * NEIGH + o) * tok, tok), :]

    def crossing(d):
        if not lifted or d not in (3, 4):
            return None
        return is_a if d == 4 else is_b

    n_nb = sum(inside(d).astype(jnp.int32) for d in range(1, NEIGH))

    def window_limits(s):
        reads = mask_ref[c, s] > 0
        limits = []
        for o in range(NEIGH):
            dy, dx = OFFSETS[o]
            y = jnp.minimum(jnp.maximum(i + dy, 0), rows - 1)
            x = jnp.minimum(jnp.maximum(j + dx, 0), cols - 1)
            ok = inside(o) & reads & (pattern_ref[0, 0, 0, o] > 0)
            limits.append(jnp.where(ok, counts_ref[s, y, x], 0))
        return limits

    barrier = pltpu.get_barrier_semaphore()
    def greet(target):
        pl.semaphore_signal(barrier, 1, device_id=target, device_id_type=mesh_id)
    for s in range(spans):
        @pl.when(s != c)
        def _():
            greet((s, i, j))
    for d in range(1, NEIGH):
        dy, dx = OFFSETS[d]
        @pl.when(inside(d))
        def _():
            greet((c, i + dy, j + dx))
    pl.semaphore_wait(barrier, spans - 1 + n_nb)

    def up_copy(s):
        return pltpu.make_async_remote_copy(
            src_ref=kv_ref, dst_ref=slot(c, 0), send_sem=send_sem.at[s], recv_sem=recv_sem.at[c * NEIGH],
            device_id=(s, i, j), device_id_type=mesh_id)

    def side_copy(s, d, src):
        dy, dx = OFFSETS[d]
        return pltpu.make_async_remote_copy(
            src_ref=src, dst_ref=slot(s, INVERSE[d]),
            send_sem=send_sem.at[spans + s * (NEIGH - 1) + d - 1],
            recv_sem=recv_sem.at[s * NEIGH + INVERSE[d]],
            device_id=(c, i + dy, j + dx), device_id_type=mesh_id)

    def lift_copy(s, o):
        return pltpu.make_async_remote_copy(
            src_ref=slot(c, o), dst_ref=slot(c, o), send_sem=lift_sem.at[s],
            recv_sem=recv_sem.at[c * NEIGH + o],
            device_id=(s, i, j), device_id_type=mesh_id)

    def send_side(s, d, src, wait=False, own=False):
        cross = crossing(d)
        go = inside(d) if (cross is None or own) else inside(d) & jnp.logical_not(cross)
        @pl.when(go)
        def _():
            cp = side_copy(s, d, src)
            cp.wait_send() if wait else cp.start()

    q_load = pltpu.make_async_copy(q_hbm, q_ref, local_sem.at[1])
    q_load.start()

    for s in reversed(range(spans)):
        @pl.when(s > c)
        def _():
            up_copy(s).start()

    for s in range(spans):
        @pl.when(s == c)
        def _():
            for d in range(1, NEIGH):
                send_side(s, d, kv_ref, own=True)

    own = pltpu.make_async_copy(kv_ref, slot(0, 0), local_sem.at[0])
    for s in range(spans):
        @pl.when(s == c)
        def _():
            pltpu.make_async_copy(kv_ref, slot(s, 0), local_sem.at[0]).start()

    if lifted:
        for o, end in ((4, is_a), (3, is_b)):
            dy, dx = OFFSETS[o]
            @pl.when(end)
            def _():
                for s in range(spans):
                    @pl.when(s == c)
                    def _():
                        pltpu.make_async_remote_copy(
                            src_ref=kv_ref, dst_ref=slot(s, o), send_sem=send_sem.at[0],
                            recv_sem=recv_sem.at[s * NEIGH + o],
                            device_id=(c, i + dy, j + dx), device_id_type=mesh_id).wait_recv()
                for s in range(spans):
                    @pl.when(s > c)
                    def _():
                        lift_copy(s, o).start()

    zeros = jnp.zeros((tok, kv_ref.shape[1]), kv_ref.dtype)
    for s in range(spans):
        @pl.when(s <= c)
        def _():
            for d in range(1, NEIGH):
                @pl.when(jnp.logical_not(inside(INVERSE[d])))
                def _():
                    slot(s, INVERSE[d])[...] = zeros

    def ring_gap(a, b):
        return min((a - b) % spans, (b - a) % spans)

    own.wait()
    q_load.wait()
    kv_heads = q3.shape[0]
    groups = q_ref.shape[1] // (kv_heads * HEAD_SIZE)
    load_queries(q_ref, q3, kv_heads, groups)
    m_sc[...] = jnp.full(m_sc.shape, -1e30, jnp.float32)
    l_sc[...] = jnp.zeros(l_sc.shape, jnp.float32)
    acc_sc[...] = jnp.zeros(acc_sc.shape, jnp.float32)

    def own_group(cc):
        s = cc
        for o in range(1, NEIGH):
            dy, dx = OFFSETS[o]
            done = inside(o)
            if lifted and o in (3, 4):
                done = done & jnp.logical_not(is_a if o == 4 else is_b)
            @pl.when(done)
            def _():
                pltpu.make_async_remote_copy(
                    src_ref=kv_ref, dst_ref=slot(s, o), send_sem=send_sem.at[0],
                    recv_sem=recv_sem.at[s * NEIGH + o],
                    device_id=(c, i + dy, j + dx), device_id_type=mesh_id).wait_recv()
        attend_chunk(q3, kvbuf, window_limits(s), m_sc, l_sc, acc_sc, s, tok)

    for cc in range(spans):
        @pl.when(c == cc)
        def _():
            for n, s in enumerate(sorted(range(cc), key=lambda s: (ring_gap(s, cc), -s))):
                if cc >= 2 and n == cc - 1:
                    own_group(cc)
                pltpu.make_async_remote_copy(
                    src_ref=kv_ref, dst_ref=slot(s, 0), send_sem=send_sem.at[s], recv_sem=recv_sem.at[s * NEIGH],
                    device_id=(s, i, j), device_id_type=mesh_id).wait_recv()
                for d in range(1, NEIGH):
                    send_side(s, d, slot(s, 0))

    for s in range(spans):
        @pl.when(s > c)
        def _():
            up_copy(s).wait_send()

    for cc in range(spans):
        @pl.when(c == cc)
        def _():
            order = [cc] + sorted(range(cc), key=lambda s: (ring_gap(s, cc), -s))
            for s in order[1:] if cc >= 2 else order:
                for o in range(1, NEIGH):
                    dy, dx = OFFSETS[o]
                    done = inside(o)
                    if lifted and s == cc and o in (3, 4):
                        done = done & jnp.logical_not(is_a if o == 4 else is_b)
                    @pl.when(done)
                    def _():
                        pltpu.make_async_remote_copy(
                            src_ref=kv_ref, dst_ref=slot(s, o), send_sem=send_sem.at[0],
                            recv_sem=recv_sem.at[s * NEIGH + o],
                            device_id=(c, i + dy, j + dx), device_id_type=mesh_id).wait_recv()
                attend_chunk(q3, kvbuf, window_limits(s), m_sc, l_sc, acc_sc, s, tok)

    for cc in range(spans):
        @pl.when(c == cc)
        def _():
            for s in range(cc + 1):
                for d in range(1, NEIGH):
                    send_side(s, d, kv_ref, wait=True, own=(s == cc))
            if lifted:
                for o, end in ((4, is_a), (3, is_b)):
                    @pl.when(end)
                    def _():
                        for s in range(cc + 1, spans):
                            lift_copy(s, o).wait_send()

    attend_finish(counts_ref[c, i, j], l_sc, acc_sc, o_ref, groups, tok)
    store = pltpu.make_async_copy(o_ref, o_hbm, local_sem.at[1])
    store.start()
    store.wait()


def window_attend(q, kv, pattern, counts, span_mask):
    tok, qw = q.shape
    kw = kv.shape[1]
    spans, rows, cols = counts.shape
    keys = spans * NEIGH * tok
    flops = 2 * 2 * tok * qw * keys
    kernel = lambda *refs: window_kernel(spans, rows, cols, *refs)
    return pl.pallas_call(
        kernel,
        out_shape=jax.ShapeDtypeStruct((tok, qw), q.dtype),
        in_specs=[pl.BlockSpec(memory_space=pl.ANY)] * 2 + [pl.BlockSpec(memory_space=pltpu.SMEM)] * 3,
        out_specs=pl.BlockSpec(memory_space=pl.ANY),
        scratch_shapes=[
            pltpu.VMEM((tok, qw), q.dtype),
            pltpu.VMEM((tok, qw), q.dtype),
            pltpu.VMEM((keys, kw), kv.dtype),
            pltpu.VMEM((kw // (2 * HEAD_SIZE), qw // (kw // 2) * tok, HEAD_SIZE), q.dtype),
            pltpu.VMEM((kw // (2 * HEAD_SIZE), qw // (kw // 2) * tok, 1), jnp.float32),
            pltpu.VMEM((kw // (2 * HEAD_SIZE), qw // (kw // 2) * tok, 1), jnp.float32),
            pltpu.VMEM((kw // (2 * HEAD_SIZE), qw // (kw // 2) * tok, HEAD_SIZE), jnp.float32),
            pltpu.SemaphoreType.DMA((spans + spans * (NEIGH - 1),)),
            pltpu.SemaphoreType.DMA((spans * NEIGH,)),
            pltpu.SemaphoreType.DMA((spans,)),
            pltpu.SemaphoreType.DMA((2,)),
        ],
        compiler_params=pltpu.CompilerParams(
            vmem_limit_bytes=67043328, collective_id=0, has_side_effects=True),
        cost_estimate=pl.CostEstimate(
            flops=flops, transcendentals=tok * qw // HEAD_SIZE * keys,
            bytes_accessed=2 * (2 * tok * qw + keys * kw)),
    )(q, kv, counts, pattern, span_mask)


def shards(queries, key_value, pattern, counts, span_mask):
    tok_rows = queries.shape[3]
    out = window_attend(
        queries.reshape(tok_rows, -1), key_value.reshape(tok_rows, -1), pattern, counts, span_mask)
    return out.reshape(1, 1, 1, tok_rows, -1)


def solution(mesh):
    return jax.shard_map(
        shards,
        mesh=mesh,
        in_specs=(
            P("span", "ty", "tx", None, None),
            P("span", "ty", "tx", None, None),
            P("span", "ty", "tx", None),
            P(),
            P(),
        ),
        out_specs=P("span", "ty", "tx", None, None),
        check_vma=False,
    )
```

```python
import jax
import jax.numpy as jnp
from jax import lax
from jax.experimental import pallas as pl
from jax.experimental.pallas import tpu as pltpu
from jax.sharding import PartitionSpec as P

HEAD_SIZE = 128
NEIGH = 5
OFFSETS = ((0, 0), (-1, 0), (1, 0), (0, -1), (0, 1))
INVERSE = (0, 2, 1, 4, 3)


def cross_tiles(extended):
    return jnp.stack(
        [
            extended[:, 1, 1],
            extended[:, 0, 1],
            extended[:, 2, 1],
            extended[:, 1, 0],
            extended[:, 1, 2],
        ],
        axis=1,
    )


def load_queries(q_ref, q3, kv_heads, groups):
    for h in range(kv_heads):
        q3[h] = jnp.concatenate(
            [q_ref[:, (h * groups + g) * HEAD_SIZE:(h * groups + g + 1) * HEAD_SIZE] for g in range(groups)],
            axis=0,
        )


def attend_chunk(q3, kvbuf, limits, m_sc, l_sc, acc_sc, s, tok):
    kv_heads = q3.shape[0]
    width = kv_heads * HEAD_SIZE
    scale = HEAD_SIZE ** (-0.5)
    lo, n = s * NEIGH * tok, NEIGH * tok
    lane = lax.broadcasted_iota(jnp.int32, (1, n), 1)
    block = lane // tok
    limit = jnp.full((1, n), limits[NEIGH - 1], jnp.int32)
    for o in range(NEIGH - 2, -1, -1):
        limit = jnp.where(block == o, limits[o], limit)
    live = (lane % tok) < limit
    for h in range(kv_heads):
        kh = kvbuf[lo:lo + n, h * HEAD_SIZE:(h + 1) * HEAD_SIZE]
        sc = lax.dot_general(q3[h], kh, (((1,), (1,)), ((), ())), preferred_element_type=jnp.float32)
        sc = jnp.where(live, sc * scale, -1e30)
        m_old = m_sc[h]
        m_new = jnp.maximum(m_old, jnp.max(sc, axis=1, keepdims=True))
        p = jnp.where(live, jnp.exp(sc - m_new), 0.0)
        fade = jnp.exp(m_old - m_new)
        l_sc[h] = l_sc[h] * fade + jnp.sum(p, axis=1, keepdims=True)
        vh = kvbuf[lo:lo + n, width + h * HEAD_SIZE:width + (h + 1) * HEAD_SIZE]
        acc_sc[h] = acc_sc[h] * fade + jnp.dot(p.astype(jnp.bfloat16), vh, preferred_element_type=jnp.float32)
        m_sc[h] = m_new


def attend_finish(own_count, l_sc, acc_sc, o_ref, groups, tok):
    kv_heads = acc_sc.shape[0]
    rowok = (lax.broadcasted_iota(jnp.int32, (groups * tok, 1), 0) % tok) < own_count
    for h in range(kv_heads):
        res = jnp.where(rowok, acc_sc[h] / l_sc[h], 0.0).astype(o_ref.dtype)
        for g in range(groups):
            col = (h * groups + g) * HEAD_SIZE
            o_ref[:, col:col + HEAD_SIZE] = res[g * tok:(g + 1) * tok]


def window_kernel(spans, rows, cols, q_hbm, kv_ref, counts_ref, pattern_ref, mask_ref, o_hbm,
                  q_ref, o_ref, kvbuf, q3, m_sc, l_sc, acc_sc,
                  send_sem, recv_sem, lift_sem, local_sem):
    tok = kv_ref.shape[0]
    c = lax.axis_index("span")
    i = lax.axis_index("ty")
    j = lax.axis_index("tx")
    mesh_id = pl.DeviceIdType.MESH
    lifted = cols >= 4
    half = cols // 2
    is_a = j == half - 1
    is_b = j == half

    def inside(d):
        dy, dx = OFFSETS[d]
        y, x = i + dy, j + dx
        return (y >= 0) & (y < rows) & (x >= 0) & (x < cols)

    def slot(s, o):
        return kvbuf.at[pl.ds((s * NEIGH + o) * tok, tok), :]

    def crossing(d):
        if not lifted or d not in (3, 4):
            return None
        return is_a if d == 4 else is_b

    n_nb = sum(inside(d).astype(jnp.int32) for d in range(1, NEIGH))

    def window_limits(s):
        reads = mask_ref[c, s] > 0
        limits = []
        for o in range(NEIGH):
            dy, dx = OFFSETS[o]
            y = jnp.minimum(jnp.maximum(i + dy, 0), rows - 1)
            x = jnp.minimum(jnp.maximum(j + dx, 0), cols - 1)
            ok = inside(o) & reads & (pattern_ref[0, 0, 0, o] > 0)
            limits.append(jnp.where(ok, counts_ref[s, y, x], 0))
        return limits

    barrier = pltpu.get_barrier_semaphore()
    def greet(target):
        pl.semaphore_signal(barrier, 1, device_id=target, device_id_type=mesh_id)
    for s in range(spans):
        @pl.when(s != c)
        def _():
            greet((s, i, j))
    for d in range(1, NEIGH):
        dy, dx = OFFSETS[d]
        @pl.when(inside(d))
        def _():
            greet((c, i + dy, j + dx))
    pl.semaphore_wait(barrier, spans - 1 + n_nb)

    def up_copy(s):
        return pltpu.make_async_remote_copy(
            src_ref=kv_ref, dst_ref=slot(c, 0), send_sem=send_sem.at[s], recv_sem=recv_sem.at[c * NEIGH],
            device_id=(s, i, j), device_id_type=mesh_id)

    def side_copy(s, d, src):
        dy, dx = OFFSETS[d]
        return pltpu.make_async_remote_copy(
            src_ref=src, dst_ref=slot(s, INVERSE[d]),
            send_sem=send_sem.at[spans + s * (NEIGH - 1) + d - 1],
            recv_sem=recv_sem.at[s * NEIGH + INVERSE[d]],
            device_id=(c, i + dy, j + dx), device_id_type=mesh_id)

    def lift_copy(s, o):
        return pltpu.make_async_remote_copy(
            src_ref=slot(c, o), dst_ref=slot(c, o), send_sem=lift_sem.at[s],
            recv_sem=recv_sem.at[c * NEIGH + o],
            device_id=(s, i, j), device_id_type=mesh_id)

    def send_side(s, d, src, wait=False, own=False):
        cross = crossing(d)
        go = inside(d) if (cross is None or own) else inside(d) & jnp.logical_not(cross)
        @pl.when(go)
        def _():
            cp = side_copy(s, d, src)
            cp.wait_send() if wait else cp.start()

    q_load = pltpu.make_async_copy(q_hbm, q_ref, local_sem.at[1])
    q_load.start()

    for s in reversed(range(spans)):
        @pl.when(s > c)
        def _():
            up_copy(s).start()

    for s in range(spans):
        @pl.when(s == c)
        def _():
            for d in range(1, NEIGH):
                send_side(s, d, kv_ref, own=True)

    own = pltpu.make_async_copy(kv_ref, slot(0, 0), local_sem.at[0])
    for s in range(spans):
        @pl.when(s == c)
        def _():
            pltpu.make_async_copy(kv_ref, slot(s, 0), local_sem.at[0]).start()

    if lifted:
        for o, end in ((4, is_a), (3, is_b)):
            dy, dx = OFFSETS[o]
            @pl.when(end)
            def _():
                for s in range(spans):
                    @pl.when(s == c)
                    def _():
                        pltpu.make_async_remote_copy(
                            src_ref=kv_ref, dst_ref=slot(s, o), send_sem=send_sem.at[0],
                            recv_sem=recv_sem.at[s * NEIGH + o],
                            device_id=(c, i + dy, j + dx), device_id_type=mesh_id).wait_recv()
                for s in reversed(range(spans)):
                    @pl.when(s > c)
                    def _():
                        lift_copy(s, o).start()

    zeros = jnp.zeros((tok, kv_ref.shape[1]), kv_ref.dtype)
    for s in range(spans):
        @pl.when(s <= c)
        def _():
            for d in range(1, NEIGH):
                @pl.when(jnp.logical_not(inside(INVERSE[d])))
                def _():
                    slot(s, INVERSE[d])[...] = zeros

    def ring_gap(a, b):
        return min((a - b) % spans, (b - a) % spans)

    own.wait()
    q_load.wait()
    kv_heads = q3.shape[0]
    groups = q_ref.shape[1] // (kv_heads * HEAD_SIZE)
    load_queries(q_ref, q3, kv_heads, groups)
    m_sc[...] = jnp.full(m_sc.shape, -1e30, jnp.float32)
    l_sc[...] = jnp.zeros(l_sc.shape, jnp.float32)
    acc_sc[...] = jnp.zeros(acc_sc.shape, jnp.float32)

    def own_group(cc):
        s = cc
        for o in range(1, NEIGH):
            dy, dx = OFFSETS[o]
            done = inside(o)
            if lifted and o in (3, 4):
                done = done & jnp.logical_not(is_a if o == 4 else is_b)
            @pl.when(done)
            def _():
                pltpu.make_async_remote_copy(
                    src_ref=kv_ref, dst_ref=slot(s, o), send_sem=send_sem.at[0],
                    recv_sem=recv_sem.at[s * NEIGH + o],
                    device_id=(c, i + dy, j + dx), device_id_type=mesh_id).wait_recv()
        attend_chunk(q3, kvbuf, window_limits(s), m_sc, l_sc, acc_sc, s, tok)

    for cc in range(spans):
        @pl.when(c == cc)
        def _():
            for n, s in enumerate(sorted(range(cc), key=lambda s: (ring_gap(s, cc), -s))):
                if cc >= 2 and n == cc - 1:
                    own_group(cc)
                pltpu.make_async_remote_copy(
                    src_ref=kv_ref, dst_ref=slot(s, 0), send_sem=send_sem.at[s], recv_sem=recv_sem.at[s * NEIGH],
                    device_id=(s, i, j), device_id_type=mesh_id).wait_recv()
                for d in range(1, NEIGH):
                    send_side(s, d, slot(s, 0))

    for s in range(spans):
        @pl.when(s > c)
        def _():
            up_copy(s).wait_send()

    for cc in range(spans):
        @pl.when(c == cc)
        def _():
            order = [cc] + sorted(range(cc), key=lambda s: (ring_gap(s, cc), -s))
            for s in order[1:] if cc >= 2 else order:
                for o in range(1, NEIGH):
                    dy, dx = OFFSETS[o]
                    done = inside(o)
                    if lifted and s == cc and o in (3, 4):
                        done = done & jnp.logical_not(is_a if o == 4 else is_b)
                    @pl.when(done)
                    def _():
                        pltpu.make_async_remote_copy(
                            src_ref=kv_ref, dst_ref=slot(s, o), send_sem=send_sem.at[0],
                            recv_sem=recv_sem.at[s * NEIGH + o],
                            device_id=(c, i + dy, j + dx), device_id_type=mesh_id).wait_recv()
                attend_chunk(q3, kvbuf, window_limits(s), m_sc, l_sc, acc_sc, s, tok)

    for cc in range(spans):
        @pl.when(c == cc)
        def _():
            for s in range(cc + 1):
                for d in range(1, NEIGH):
                    send_side(s, d, kv_ref, wait=True, own=(s == cc))
            if lifted:
                for o, end in ((4, is_a), (3, is_b)):
                    @pl.when(end)
                    def _():
                        for s in range(cc + 1, spans):
                            lift_copy(s, o).wait_send()

    attend_finish(counts_ref[c, i, j], l_sc, acc_sc, o_ref, groups, tok)
    store = pltpu.make_async_copy(o_ref, o_hbm, local_sem.at[1])
    store.start()
    store.wait()


def window_attend(q, kv, pattern, counts, span_mask):
    tok, qw = q.shape
    kw = kv.shape[1]
    spans, rows, cols = counts.shape
    keys = spans * NEIGH * tok
    flops = 2 * 2 * tok * qw * keys
    kernel = lambda *refs: window_kernel(spans, rows, cols, *refs)
    return pl.pallas_call(
        kernel,
        out_shape=jax.ShapeDtypeStruct((tok, qw), q.dtype),
        in_specs=[pl.BlockSpec(memory_space=pl.ANY)] * 2 + [pl.BlockSpec(memory_space=pltpu.SMEM)] * 3,
        out_specs=pl.BlockSpec(memory_space=pl.ANY),
        scratch_shapes=[
            pltpu.VMEM((tok, qw), q.dtype),
            pltpu.VMEM((tok, qw), q.dtype),
            pltpu.VMEM((keys, kw), kv.dtype),
            pltpu.VMEM((kw // (2 * HEAD_SIZE), qw // (kw // 2) * tok, HEAD_SIZE), q.dtype),
            pltpu.VMEM((kw // (2 * HEAD_SIZE), qw // (kw // 2) * tok, 1), jnp.float32),
            pltpu.VMEM((kw // (2 * HEAD_SIZE), qw // (kw // 2) * tok, 1), jnp.float32),
            pltpu.VMEM((kw // (2 * HEAD_SIZE), qw // (kw // 2) * tok, HEAD_SIZE), jnp.float32),
            pltpu.SemaphoreType.DMA((spans + spans * (NEIGH - 1),)),
            pltpu.SemaphoreType.DMA((spans * NEIGH,)),
            pltpu.SemaphoreType.DMA((spans,)),
            pltpu.SemaphoreType.DMA((2,)),
        ],
        compiler_params=pltpu.CompilerParams(
            vmem_limit_bytes=67043328, collective_id=0, has_side_effects=True),
        cost_estimate=pl.CostEstimate(
            flops=flops, transcendentals=tok * qw // HEAD_SIZE * keys,
            bytes_accessed=2 * (2 * tok * qw + keys * kw)),
    )(q, kv, counts, pattern, span_mask)


def shards(queries, key_value, pattern, counts, span_mask):
    tok_rows = queries.shape[3]
    out = window_attend(
        queries.reshape(tok_rows, -1), key_value.reshape(tok_rows, -1), pattern, counts, span_mask)
    return out.reshape(1, 1, 1, tok_rows, -1)


def solution(mesh):
    return jax.shard_map(
        shards,
        mesh=mesh,
        in_specs=(
            P("span", "ty", "tx", None, None),
            P("span", "ty", "tx", None, None),
            P("span", "ty", "tx", None),
            P(),
            P(),
        ),
        out_specs=P("span", "ty", "tx", None, None),
        check_vma=False,
    )
```

```python
import jax
import jax.numpy as jnp
from jax import lax
from jax.experimental import pallas as pl
from jax.experimental.pallas import tpu as pltpu
from jax.sharding import PartitionSpec as P

HEAD_SIZE = 128
NEIGH = 5
OFFSETS = ((0, 0), (-1, 0), (1, 0), (0, -1), (0, 1))
INVERSE = (0, 2, 1, 4, 3)


def cross_tiles(extended):
    return jnp.stack(
        [
            extended[:, 1, 1],
            extended[:, 0, 1],
            extended[:, 2, 1],
            extended[:, 1, 0],
            extended[:, 1, 2],
        ],
        axis=1,
    )


def load_queries(q_ref, q3, kv_heads, groups):
    for h in range(kv_heads):
        q3[h] = jnp.concatenate(
            [q_ref[:, (h * groups + g) * HEAD_SIZE:(h * groups + g + 1) * HEAD_SIZE] for g in range(groups)],
            axis=0,
        )


def attend_chunk(q3, kvbuf, limits, m_sc, l_sc, acc_sc, s, tok):
    kv_heads = q3.shape[0]
    width = kv_heads * HEAD_SIZE
    scale = HEAD_SIZE ** (-0.5)
    lo, n = s * NEIGH * tok, NEIGH * tok
    lane = lax.broadcasted_iota(jnp.int32, (1, n), 1)
    block = lane // tok
    limit = jnp.full((1, n), limits[NEIGH - 1], jnp.int32)
    for o in range(NEIGH - 2, -1, -1):
        limit = jnp.where(block == o, limits[o], limit)
    live = (lane % tok) < limit
    for h in range(kv_heads):
        kh = kvbuf[lo:lo + n, h * HEAD_SIZE:(h + 1) * HEAD_SIZE]
        sc = lax.dot_general(q3[h], kh, (((1,), (1,)), ((), ())), preferred_element_type=jnp.float32)
        sc = jnp.where(live, sc * scale, -1e30)
        m_old = m_sc[h]
        m_new = jnp.maximum(m_old, jnp.max(sc, axis=1, keepdims=True))
        p = jnp.where(live, jnp.exp(sc - m_new), 0.0)
        fade = jnp.exp(m_old - m_new)
        l_sc[h] = l_sc[h] * fade + jnp.sum(p, axis=1, keepdims=True)
        vh = kvbuf[lo:lo + n, width + h * HEAD_SIZE:width + (h + 1) * HEAD_SIZE]
        acc_sc[h] = acc_sc[h] * fade + jnp.dot(p.astype(jnp.bfloat16), vh, preferred_element_type=jnp.float32)
        m_sc[h] = m_new


def attend_finish(own_count, l_sc, acc_sc, o_ref, groups, tok):
    kv_heads = acc_sc.shape[0]
    rowok = (lax.broadcasted_iota(jnp.int32, (groups * tok, 1), 0) % tok) < own_count
    for h in range(kv_heads):
        res = jnp.where(rowok, acc_sc[h] / l_sc[h], 0.0).astype(o_ref.dtype)
        for g in range(groups):
            col = (h * groups + g) * HEAD_SIZE
            o_ref[:, col:col + HEAD_SIZE] = res[g * tok:(g + 1) * tok]


def window_kernel(spans, rows, cols, q_hbm, kv_ref, counts_ref, pattern_ref, mask_ref, o_hbm,
                  q_ref, o_ref, kvbuf, q3, m_sc, l_sc, acc_sc,
                  send_sem, recv_sem, lift_sem, local_sem):
    tok = kv_ref.shape[0]
    c = lax.axis_index("span")
    i = lax.axis_index("ty")
    j = lax.axis_index("tx")
    mesh_id = pl.DeviceIdType.MESH
    lifted = cols >= 4
    half = cols // 2
    is_a = j == half - 1
    is_b = j == half

    def inside(d):
        dy, dx = OFFSETS[d]
        y, x = i + dy, j + dx
        return (y >= 0) & (y < rows) & (x >= 0) & (x < cols)

    def slot(s, o):
        return kvbuf.at[pl.ds((s * NEIGH + o) * tok, tok), :]

    def crossing(d):
        if not lifted or d not in (3, 4):
            return None
        return is_a if d == 4 else is_b

    n_nb = sum(inside(d).astype(jnp.int32) for d in range(1, NEIGH))

    def window_limits(s):
        reads = mask_ref[c, s] > 0
        limits = []
        for o in range(NEIGH):
            dy, dx = OFFSETS[o]
            y = jnp.minimum(jnp.maximum(i + dy, 0), rows - 1)
            x = jnp.minimum(jnp.maximum(j + dx, 0), cols - 1)
            ok = inside(o) & reads & (pattern_ref[0, 0, 0, o] > 0)
            limits.append(jnp.where(ok, counts_ref[s, y, x], 0))
        return limits

    barrier = pltpu.get_barrier_semaphore()
    def greet(target):
        pl.semaphore_signal(barrier, 1, device_id=target, device_id_type=mesh_id)
    for s in range(spans):
        @pl.when(s != c)
        def _():
            greet((s, i, j))
    for d in range(1, NEIGH):
        dy, dx = OFFSETS[d]
        @pl.when(inside(d))
        def _():
            greet((c, i + dy, j + dx))
    pl.semaphore_wait(barrier, spans - 1 + n_nb)

    def up_copy(s):
        return pltpu.make_async_remote_copy(
            src_ref=kv_ref, dst_ref=slot(c, 0), send_sem=send_sem.at[s], recv_sem=recv_sem.at[c * NEIGH],
            device_id=(s, i, j), device_id_type=mesh_id)

    def side_copy(s, d, src):
        dy, dx = OFFSETS[d]
        return pltpu.make_async_remote_copy(
            src_ref=src, dst_ref=slot(s, INVERSE[d]),
            send_sem=send_sem.at[spans + s * (NEIGH - 1) + d - 1],
            recv_sem=recv_sem.at[s * NEIGH + INVERSE[d]],
            device_id=(c, i + dy, j + dx), device_id_type=mesh_id)

    def lift_copy(s, o):
        return pltpu.make_async_remote_copy(
            src_ref=slot(c, o), dst_ref=slot(c, o), send_sem=lift_sem.at[s],
            recv_sem=recv_sem.at[c * NEIGH + o],
            device_id=(s, i, j), device_id_type=mesh_id)

    def send_side(s, d, src, wait=False, own=False):
        cross = crossing(d)
        go = inside(d) if (cross is None or own) else inside(d) & jnp.logical_not(cross)
        @pl.when(go)
        def _():
            cp = side_copy(s, d, src)
            cp.wait_send() if wait else cp.start()

    def send_all(s, src, own=False):
        for parity, dirs in ((0, (1, 3, 4, 2)), (1, (2, 3, 4, 1))):
            @pl.when(i % 2 == parity)
            def _():
                for d in dirs:
                    send_side(s, d, src, own=own)

    q_load = pltpu.make_async_copy(q_hbm, q_ref, local_sem.at[1])
    q_load.start()

    for s in reversed(range(spans)):
        @pl.when(s > c)
        def _():
            up_copy(s).start()

    for s in range(spans):
        @pl.when(s == c)
        def _():
            send_all(s, kv_ref, own=True)

    own = pltpu.make_async_copy(kv_ref, slot(0, 0), local_sem.at[0])
    for s in range(spans):
        @pl.when(s == c)
        def _():
            pltpu.make_async_copy(kv_ref, slot(s, 0), local_sem.at[0]).start()

    if lifted:
        for o, end in ((4, is_a), (3, is_b)):
            dy, dx = OFFSETS[o]
            @pl.when(end)
            def _():
                for s in range(spans):
                    @pl.when(s == c)
                    def _():
                        pltpu.make_async_remote_copy(
                            src_ref=kv_ref, dst_ref=slot(s, o), send_sem=send_sem.at[0],
                            recv_sem=recv_sem.at[s * NEIGH + o],
                            device_id=(c, i + dy, j + dx), device_id_type=mesh_id).wait_recv()
                for s in range(spans):
                    @pl.when(s > c)
                    def _():
                        lift_copy(s, o).start()

    zeros = jnp.zeros((tok, kv_ref.shape[1]), kv_ref.dtype)
    for s in range(spans):
        @pl.when(s <= c)
        def _():
            for d in range(1, NEIGH):
                @pl.when(jnp.logical_not(inside(INVERSE[d])))
                def _():
                    slot(s, INVERSE[d])[...] = zeros

    def ring_gap(a, b):
        return min((a - b) % spans, (b - a) % spans)

    own.wait()
    q_load.wait()
    kv_heads = q3.shape[0]
    groups = q_ref.shape[1] // (kv_heads * HEAD_SIZE)
    load_queries(q_ref, q3, kv_heads, groups)
    m_sc[...] = jnp.full(m_sc.shape, -1e30, jnp.float32)
    l_sc[...] = jnp.zeros(l_sc.shape, jnp.float32)
    acc_sc[...] = jnp.zeros(acc_sc.shape, jnp.float32)

    def own_group(cc):
        s = cc
        for o in range(1, NEIGH):
            dy, dx = OFFSETS[o]
            done = inside(o)
            if lifted and o in (3, 4):
                done = done & jnp.logical_not(is_a if o == 4 else is_b)
            @pl.when(done)
            def _():
                pltpu.make_async_remote_copy(
                    src_ref=kv_ref, dst_ref=slot(s, o), send_sem=send_sem.at[0],
                    recv_sem=recv_sem.at[s * NEIGH + o],
                    device_id=(c, i + dy, j + dx), device_id_type=mesh_id).wait_recv()
        attend_chunk(q3, kvbuf, window_limits(s), m_sc, l_sc, acc_sc, s, tok)

    for cc in range(spans):
        @pl.when(c == cc)
        def _():
            for n, s in enumerate(sorted(range(cc), key=lambda s: (ring_gap(s, cc), -s))):
                if cc >= 2 and n == cc - 1:
                    own_group(cc)
                pltpu.make_async_remote_copy(
                    src_ref=kv_ref, dst_ref=slot(s, 0), send_sem=send_sem.at[s], recv_sem=recv_sem.at[s * NEIGH],
                    device_id=(s, i, j), device_id_type=mesh_id).wait_recv()
                send_all(s, slot(s, 0))

    for s in range(spans):
        @pl.when(s > c)
        def _():
            up_copy(s).wait_send()

    for cc in range(spans):
        @pl.when(c == cc)
        def _():
            order = [cc] + sorted(range(cc), key=lambda s: (ring_gap(s, cc), -s))
            for s in order[1:] if cc >= 2 else order:
                for o in range(1, NEIGH):
                    dy, dx = OFFSETS[o]
                    done = inside(o)
                    if lifted and s == cc and o in (3, 4):
                        done = done & jnp.logical_not(is_a if o == 4 else is_b)
                    @pl.when(done)
                    def _():
                        pltpu.make_async_remote_copy(
                            src_ref=kv_ref, dst_ref=slot(s, o), send_sem=send_sem.at[0],
                            recv_sem=recv_sem.at[s * NEIGH + o],
                            device_id=(c, i + dy, j + dx), device_id_type=mesh_id).wait_recv()
                attend_chunk(q3, kvbuf, window_limits(s), m_sc, l_sc, acc_sc, s, tok)

    for cc in range(spans):
        @pl.when(c == cc)
        def _():
            for s in range(cc + 1):
                for d in range(1, NEIGH):
                    send_side(s, d, kv_ref, wait=True, own=(s == cc))
            if lifted:
                for o, end in ((4, is_a), (3, is_b)):
                    @pl.when(end)
                    def _():
                        for s in range(cc + 1, spans):
                            lift_copy(s, o).wait_send()

    attend_finish(counts_ref[c, i, j], l_sc, acc_sc, o_ref, groups, tok)
    store = pltpu.make_async_copy(o_ref, o_hbm, local_sem.at[1])
    store.start()
    store.wait()


def window_attend(q, kv, pattern, counts, span_mask):
    tok, qw = q.shape
    kw = kv.shape[1]
    spans, rows, cols = counts.shape
    keys = spans * NEIGH * tok
    flops = 2 * 2 * tok * qw * keys
    kernel = lambda *refs: window_kernel(spans, rows, cols, *refs)
    return pl.pallas_call(
        kernel,
        out_shape=jax.ShapeDtypeStruct((tok, qw), q.dtype),
        in_specs=[pl.BlockSpec(memory_space=pl.ANY)] * 2 + [pl.BlockSpec(memory_space=pltpu.SMEM)] * 3,
        out_specs=pl.BlockSpec(memory_space=pl.ANY),
        scratch_shapes=[
            pltpu.VMEM((tok, qw), q.dtype),
            pltpu.VMEM((tok, qw), q.dtype),
            pltpu.VMEM((keys, kw), kv.dtype),
            pltpu.VMEM((kw // (2 * HEAD_SIZE), qw // (kw // 2) * tok, HEAD_SIZE), q.dtype),
            pltpu.VMEM((kw // (2 * HEAD_SIZE), qw // (kw // 2) * tok, 1), jnp.float32),
            pltpu.VMEM((kw // (2 * HEAD_SIZE), qw // (kw // 2) * tok, 1), jnp.float32),
            pltpu.VMEM((kw // (2 * HEAD_SIZE), qw // (kw // 2) * tok, HEAD_SIZE), jnp.float32),
            pltpu.SemaphoreType.DMA((spans + spans * (NEIGH - 1),)),
            pltpu.SemaphoreType.DMA((spans * NEIGH,)),
            pltpu.SemaphoreType.DMA((spans,)),
            pltpu.SemaphoreType.DMA((2,)),
        ],
        compiler_params=pltpu.CompilerParams(
            vmem_limit_bytes=67043328, collective_id=0, has_side_effects=True),
        cost_estimate=pl.CostEstimate(
            flops=flops, transcendentals=tok * qw // HEAD_SIZE * keys,
            bytes_accessed=2 * (2 * tok * qw + keys * kw)),
    )(q, kv, counts, pattern, span_mask)


def shards(queries, key_value, pattern, counts, span_mask):
    tok_rows = queries.shape[3]
    out = window_attend(
        queries.reshape(tok_rows, -1), key_value.reshape(tok_rows, -1), pattern, counts, span_mask)
    return out.reshape(1, 1, 1, tok_rows, -1)


def solution(mesh):
    return jax.shard_map(
        shards,
        mesh=mesh,
        in_specs=(
            P("span", "ty", "tx", None, None),
            P("span", "ty", "tx", None, None),
            P("span", "ty", "tx", None),
            P(),
            P(),
        ),
        out_specs=P("span", "ty", "tx", None, None),
        check_vma=False,
    )
```
